32 devices in a mesh: dp: 8 (over y, x, core), mp: 4 (over z).
Axes of the slice: x: 2, y: 2, z: 4, core: 2. Of those that a mesh axis runs over, the one named last changes fastest.
Arguments:
- x_in: bfloat16 [8192, 768], P(('dp', 'mp')), may hold values from -6 to 6
- enc_in: bfloat16 [4096, 768], P(('dp', 'mp')), may hold values from -6 to 6
- cotangent: bfloat16 [8192, 768], P(('dp', 'mp')), may hold values from -6 to 6
- dec_len: int32 [8], P('dp'), may hold values from 128 to 1024, as said below
- enc_len: int32 [8], P('dp'), may hold values from 64 to 512, as said below
- self_qkv: bfloat16 [768, 3, 768], P(None, None, 'mp'), may hold values from -0.109375 to 0.109375
- self_out: bfloat16 [768, 768], P('mp'), may hold values from -1.75 to 1.75
- cross_q: bfloat16 [768, 768], P(None, 'mp'), may hold values from -0.0546875 to 0.0546875
- cross_kv: bfloat16 [768, 2, 768], P(None, None, 'mp'), may hold values from -0.21875 to 0.21875
- cross_out: bfloat16 [768, 768], P('mp'), may hold values from -1.25 to 1.25
- ff_in: bfloat16 [768, 2, 2048], P(None, None, 'mp'), may hold values from -0.21875 to 0.21875
- ff_out: bfloat16 [2048, 768], P('mp'), may hold values from -0.1875 to 0.1875
- gains: bfloat16 [3, 768], replicated, may hold values from 0.5 to 1.5
- table: bfloat16 [32, 12], P(None, 'mp'), may hold values from -6 to 6
Outputs:
- layer_out: bfloat16 [8192, 768], P(('dp', 'mp'))
- input_grad: float32 [8192, 768], P(('dp', 'mp'))
- enc_grad: float32 [4096, 768], P(('dp', 'mp'))
- self_qkv_grad: float32 [768, 3, 768], P(None, None, 'mp')
- self_out_grad: float32 [768, 768], P('mp')
- cross_q_grad: float32 [768, 768], P(None, 'mp')
- cross_kv_grad: float32 [768, 2, 768], P(None, None, 'mp')
- cross_out_grad: float32 [768, 768], P('mp')
- ff_in_grad: float32 [768, 2, 2048], P(None, None, 'mp')
- ff_out_grad: float32 [2048, 768], P('mp')
- gains_grad: float32 [3, 768], replicated
- table_grad: float32 [32, 12], P(None, 'mp')
The draws below stay inside these ranges and needn't reach their ends.
Inputs may be any that keep to these rules, and one draw needn't show every extreme that they name: dec_len[s] is the number of live decoder positions of sequence s; the sequences on one index of dp are of similar length; some sequence has exactly 1024. enc_len[s] is the number of live encoder positions of sequence s; some sequence has exactly 512.
All inputs are finite; a program needn't handle non-finite values.
Results may differ from the reference program's by a relative error of at most 0.035.
Values may be sent and summed in bfloat16 or wider, within the bound.
A program may use at most 192 MiB of HBM per device.

```python
import math
import jax
import jax.numpy as jnp
from jax import lax

D = 768
H = 12
DH = 64
FF = 2048
NB = 32
MAXD = 128
LDEC = 1024
LENC = 512
SEQUENCES_SHARD = 1
SEQS = 8
TOKENS = 8192
ENC_TOKENS = 4096


def draw_lengths(key, longest):
    seq_total = SEQS
    shortest = max(longest // 8, 1)
    level_key, jitter_key, pick_key = jax.random.split(key, 3)
    groups = seq_total // SEQUENCES_SHARD
    levels = jax.random.randint(level_key, (groups,), shortest, longest + 1)
    spread_levels = jnp.repeat(levels, SEQUENCES_SHARD)
    jitter = jax.random.randint(jitter_key, (seq_total,), 0, longest // 8 + 1)
    lengths_out = jnp.maximum(spread_levels - jitter, shortest)
    chosen = jax.random.randint(pick_key, (), 0, seq_total)
    return jnp.where(jnp.arange(seq_total) == chosen, longest, lengths_out).astype(jnp.int32)


def draw_dec_len(key, part):
    return draw_lengths(jax.random.fold_in(key, 11), LDEC)


def draw_enc_len(key, part):
    return draw_lengths(jax.random.fold_in(key, 23), LENC)


def steps_of(key, dims, cuts, low, high):
    level, own = 1.0, jax.random.fold_in(key, 6)
    for axis_at, parts in cuts:
        draws = jnp.exp(jax.random.uniform(jax.random.fold_in(own, axis_at), (parts,), jnp.float32, low / len(cuts), high / len(cuts)))
        level = level * jnp.repeat(draws, dims[axis_at] // parts).reshape([-1 if axis == axis_at else 1 for axis in range(len(dims))])
    return level


def centred(key, dims, width, limit, cuts=(), held_as=jnp.bfloat16):
    loudness = steps_of(key, dims, cuts, -0.22, 0.18) if cuts else 1.0
    values = jax.random.normal(key, dims, jnp.float32) * width * loudness
    return jnp.minimum(jnp.maximum(values, -limit), limit).astype(held_as)


def setup_inputs(seed: int = 0) -> dict:
    key_of = jax.random.split(jax.random.key(seed), 15)
    return {
        "x_in": centred(key_of[0], (TOKENS, D), 1.0, 6.0, ((0, 32),)),
        "enc_in": centred(key_of[1], (ENC_TOKENS, D), 1.0, 6.0, ((0, 32),)),
        "cotangent": centred(key_of[2], (TOKENS, D), 1.0, 6.0, ((0, 32),)),
        "dec_len": draw_dec_len(jax.random.fold_in(key_of[14], 71), 0),
        "enc_len": draw_enc_len(jax.random.fold_in(key_of[14], 71), 0),
        "self_qkv": centred(key_of[5], (D, 3, D), (4 * D) ** -0.5, 0.109375, ((2, 4),)),
        "self_out": centred(key_of[6], (D, D), (D // 64) ** -0.5, 1.75, ((0, 4),)),
        "cross_q": centred(key_of[7], (D, D), (16 * D) ** -0.5, 0.0546875, ((1, 4),)),
        "cross_kv": centred(key_of[8], (D, 2, D), D ** -0.5, 0.21875, ((2, 4),)),
        "cross_out": centred(key_of[9], (D, D), (D // 32) ** -0.5, 1.25, ((0, 4),)),
        "ff_in": centred(key_of[10], (D, 2, FF), D ** -0.5, 0.21875, ((2, 4),)),
        "ff_out": centred(key_of[11], (FF, D), (FF // 2) ** -0.5, 0.1875, ((0, 4),)),
        "gains": jnp.clip(1.0 + 0.1 * jax.random.normal(key_of[12], (3, D), jnp.float32), 0.5, 1.5).astype(jnp.bfloat16),
        "table": centred(key_of[13], (NB, H), 1.0, 6.0, ((1, 4),)),
    }


NORM_EPS = 1e-06
MASK_FILL = -1000000000.0
PRECISE = lax.Precision.HIGHEST

@jax.custom_vjp
def low(v):
    return lax.optimization_barrier(v.astype(jnp.bfloat16)).astype(jnp.float32)

@jax.custom_vjp
def low_back(v):
    return v

def low_keep(v):
    return (low(v), None)

def low_pass(kept, grad):
    return (grad,)

def back_keep(v):
    return (v, None)

def back_low(kept, grad):
    return (low(grad),)
low.defvjp(low_keep, low_pass)
low_back.defvjp(back_keep, back_low)

def bucket_index(distance):
    half_count = NB // 2
    clipped = jnp.maximum(distance, 0)
    bucket_ids = jnp.minimum(clipped, half_count)
    for level_pos in range(1, half_count):
        threshold = math.ceil(half_count * (MAXD / half_count) ** (level_pos / half_count))
        bucket_ids = bucket_ids + (clipped >= threshold).astype(jnp.int32)
    return bucket_ids

def rms_norm(values, gain_row):
    inv_rms = lax.rsqrt(lax.optimization_barrier(jnp.mean(values * values, axis=-1, keepdims=True)) + NORM_EPS)
    return values * inv_rms * gain_row

def matmul(left, right):
    return jnp.dot(left, right, precision=PRECISE, preferred_element_type=jnp.float32)

def softmax_attend(queries, key_rows, value_rows, rel_bias, allowed):
    scores = jnp.einsum('qhd,khd->hqk', queries, key_rows, precision=PRECISE) + rel_bias
    scores = low_back(scores)
    scores = jnp.where(allowed[None], scores, MASK_FILL)
    weights_low = low(jax.nn.softmax(scores, axis=-1))
    return jnp.einsum('hqk,khd->qhd', weights_low, value_rows, precision=PRECISE)

def layer(x_rows, enc_rows, lengths_dec, lengths_enc, self_qkv, self_out, cross_q, cross_kv, cross_out, ff_in, ff_out, gains, table):
    group_size = lengths_dec.shape[0]
    normed_one = low(rms_norm(x_rows, gains[0]))
    qkv_proj = low_back(low(matmul(normed_one, self_qkv.reshape(D, 3 * D)))).reshape(group_size, LDEC, 3, H, DH)
    positions = jnp.arange(LDEC, dtype=jnp.int32)
    query_pos = positions[:, None]
    key_pos = positions[None, :]
    rel_bias = jnp.transpose(jnp.take(table, bucket_index(query_pos - key_pos), axis=0), (2, 0, 1))

    def self_block(packed):
        queries, key_rows, value_rows, length_one = packed
        allowed = (key_pos <= query_pos) & (key_pos < length_one)
        return softmax_attend(queries, key_rows, value_rows, rel_bias, allowed)
    attended_one = lax.map(jax.checkpoint(self_block), (qkv_proj[:, :, 0], qkv_proj[:, :, 1], qkv_proj[:, :, 2], lengths_dec))
    attended_one = low_back(low(attended_one.reshape(group_size * LDEC, D)))
    resid_one = x_rows + low_back(matmul(attended_one, self_out))
    normed_two = low(rms_norm(resid_one, gains[1]))
    query_two = low_back(low(matmul(normed_two, cross_q))).reshape(group_size, LDEC, H, DH)
    kv_two = low_back(low(matmul(enc_rows, cross_kv.reshape(D, 2 * D)))).reshape(group_size, LENC, 2, H, DH)
    enc_pos = jnp.arange(LENC, dtype=jnp.int32)

    def cross_block(packed):
        queries, key_rows, value_rows, length_one = packed
        allowed = jnp.broadcast_to(enc_pos[None, :] < length_one, (LDEC, LENC))
        return softmax_attend(queries, key_rows, value_rows, 0.0, allowed)
    attended_two = lax.map(jax.checkpoint(cross_block), (query_two, kv_two[:, :, 0], kv_two[:, :, 1], lengths_enc))
    attended_two = low_back(low(attended_two.reshape(group_size * LDEC, D)))
    resid_two = resid_one + low_back(matmul(attended_two, cross_out))
    normed_three = low(rms_norm(resid_two, gains[2]))
    gate_up = low_back(matmul(normed_three, ff_in.reshape(D, 2 * FF)))
    activated = low(jax.nn.gelu(gate_up[:, :FF], approximate=True) * gate_up[:, FF:])
    return resid_two + low_back(matmul(activated, ff_out))

def reference(x_in, enc_in, cotangent, dec_len, enc_len, self_qkv, self_out, cross_q, cross_kv, cross_out, ff_in, ff_out, gains, table):
    per_group = 4 if SEQS % 4 == 0 else 1
    group_count = SEQS // per_group
    weight_list = tuple((weight_val.astype(jnp.float32) for weight_val in (self_qkv, self_out, cross_q, cross_kv, cross_out, ff_in, ff_out, gains, table)))
    x_groups = x_in.astype(jnp.float32).reshape(group_count, per_group * LDEC, D)
    enc_groups = enc_in.astype(jnp.float32).reshape(group_count, per_group * LENC, D)
    cot_groups = cotangent.astype(jnp.float32).reshape(group_count, per_group * LDEC, D)
    dec_groups = dec_len.reshape(group_count, per_group)
    encl_groups = enc_len.reshape(group_count, per_group)

    def one_group(running, packed):
        x_rows, enc_rows, cot_rows, lengths_dec, lengths_enc = packed

        def forward(x_val, enc_val, *weight_vals):
            return layer(x_val, enc_val, lengths_dec, lengths_enc, *weight_vals)
        result, pullback = jax.vjp(forward, x_rows, enc_rows, *weight_list)
        gradients = pullback(cot_rows)
        running = tuple((acc_sum + new_part for acc_sum, new_part in zip(running, gradients[2:])))
        return (running, (result.astype(jnp.bfloat16), gradients[0], gradients[1]))
    initial = tuple((jnp.zeros(weight_val.shape, jnp.float32) for weight_val in weight_list))
    sums, stacked = lax.scan(one_group, initial, (x_groups, enc_groups, cot_groups, dec_groups, encl_groups))
    layer_out = stacked[0].reshape(TOKENS, D)
    input_grad = stacked[1].reshape(TOKENS, D)
    enc_grad = stacked[2].reshape(ENC_TOKENS, D)
    self_qkv_grad, self_out_grad, cross_q_grad, cross_kv_grad, cross_out_grad, ff_in_grad, ff_out_grad, gains_grad, table_grad = sums
    return (layer_out, input_grad, enc_grad, self_qkv_grad, self_out_grad, cross_q_grad, cross_kv_grad, cross_out_grad, ff_in_grad, ff_out_grad, gains_grad, table_grad)
```

```python
import math

import jax
import jax.numpy as jnp
from jax import lax
from jax.experimental import pallas as pl
from jax.experimental.pallas import tpu as pltpu
from jax.sharding import PartitionSpec as P

NB = 32
MAXD = 128
NORM_EPS = 1e-06
MASK_FILL = -1000000000.0
MESH = pl.DeviceIdType.MESH
BF = jnp.bfloat16
F32 = jnp.float32
PARTS = 2
PADH = 16
GELU_C = math.sqrt(2.0 / math.pi)
SEMS = 224


def bucket_index(distance):
    half_count = NB // 2
    clipped = jnp.maximum(distance, 0)
    bucket_ids = jnp.minimum(clipped, half_count)
    for level_pos in range(1, half_count):
        threshold = math.ceil(half_count * (MAXD / half_count) ** (level_pos / half_count))
        bucket_ids = bucket_ids + (clipped >= threshold).astype(jnp.int32)
    return bucket_ids


def dot_nn(a, b):
    return lax.dot_general(a, b, (((1,), (0,)), ((), ())), preferred_element_type=F32)


def dot_nt(a, b):
    return lax.dot_general(a, b, (((1,), (1,)), ((), ())), preferred_element_type=F32)


def dot_tn(a, b):
    return lax.dot_general(a, b, (((0,), (0,)), ((), ())), preferred_element_type=F32)


def norm_fwd(v, g):
    inv = lax.rsqrt(jnp.mean(v * v, axis=-1, keepdims=True) + NORM_EPS)
    return (v * inv * g).astype(BF)


def norm_bwd(v, g, u):
    inv = lax.rsqrt(jnp.mean(v * v, axis=-1, keepdims=True) + NORM_EPS)
    gu = u * g
    mean = jnp.mean(gu * v, axis=-1, keepdims=True)
    grad = inv * gu - v * (inv * inv * inv * mean)
    gain = jnp.sum(u * v * inv, axis=0, keepdims=True)
    return grad, gain


class Dims:
    pass


def make_dims(mesh, x_in, enc_in, self_qkv, ff_in, table):
    d = Dims()
    d.ndp, d.nmp = mesh.shape["dp"], mesh.shape["mp"]
    d.nd = min(4, d.ndp // 2)
    d.R, d.D = x_in.shape
    d.E = enc_in.shape[0]
    d.nh = table.shape[1]
    d.hc = self_qkv.shape[2]
    d.hd = d.hc // d.nh
    d.F = ff_in.shape[2]
    d.ha = d.hd + PADH
    d.ne = 4 * d.E // d.R
    d.axr = -(-(2 + 2 * d.nh) // 8) * 8
    hc, F = d.hc, d.F
    names = (("qkv", 3 * hc), ("so", hc), ("cq", hc), ("ckv", 2 * hc), ("co", hc), ("gu", 2 * F), ("fo", F))
    d.w, at = {}, 0
    for name, rows in names:
        d.w[name] = (at, rows)
        at += rows
    d.rows = at
    s, c = 4 * hc, 4 * hc
    d.groups = {}
    land = 0
    for name, base, rows, loc in (("S", 0, s, 0), ("C", s, c, s), ("F", s + c, 3 * F, 0)):
        d.groups[name] = (base, rows, loc, land)
        land += rows // d.nd
    d.land = land
    d.locrows = max(s + c, 3 * F)
    d.small = -(-(3 + 4 * d.nh) // 8) * 8
    return d


def scratch_list(d):
    R, D, hc, nh, hd, ha, F, E = d.R, d.D, d.hc, d.nh, d.hd, d.ha, d.F, d.E
    full = ((4, R, D), BF)
    return [
        ("xb", (R, D), BF), ("cotb", (R, D), BF), ("aux", (d.axr, 4 * R), F32), ("wv", (d.rows, D), BF),
        ("h1f",) + full, ("h2f",) + full, ("h3f",) + full, ("d3f",) + full, ("d2f",) + full, ("d1f",) + full,
        ("encf", (4, E, D), BF),
        ("qa", (4, nh, ha, R), BF), ("ka", (4, nh, ha, R), BF), ("vT", (4, hc, R), BF), ("o1", (4, hc, R), BF),
        ("q2a", (4, nh, ha, R), BF), ("k2a", (d.ne, nh, ha, R), BF), ("v2T", (d.ne, hc, R), BF), ("o2", (4, hc, R), BF),
        ("lse1", (4, 8, R), F32), ("lse2", (4, 8, R), F32),
        ("bias", (nh, 3, R, R), F32), ("dsacc", (nh, 3, R, R), F32),
        ("x1", (R, D), F32), ("x2", (R, D), F32), ("gb", (R, D), F32),
        ("pb", (R, D), F32), ("sb", (3, R, D), BF), ("rb", (3, R, D), BF),
        ("opb", (R, D), F32), ("osb", (3, R, D), BF), ("orb", (3, R, D), BF), ("lov", (R, D), BF), ("igv", (R, D), BF),
        ("epb", (E, D), F32), ("esb", (3, E, D), BF), ("erb", (3, E, D), BF), ("egv", (E, D), BF),
        ("actT", (4, F, R), BF), ("dguT", (4, 2 * F, R), BF),
        ("da", (hc, R), BF), ("dqkvT", (4, 3 * hc, R), BF), ("dq2T", (4, hc, R), BF), ("dkv2T", (4, 2 * hc, E), BF),
        ("dka", (4, nh, ha, R), F32), ("dva", (4, hc, R), F32),
        ("gf", (d.locrows, D), F32), ("gsend", (d.rows, D), BF), ("grecv", (max(d.nd - 1, 1), d.land, D), BF),
        ("gz", (d.land, D), BF), ("gk", (d.land, D), F32), ("gfo", (d.land, D), BF),
        ("smc", (d.small, D), F32), ("sms", (6, d.small, D), F32), ("smr", (5, d.small, D), F32),
    ]


def build_kernel(d):
    R, D, hc, nh, hd, ha, F, E = d.R, d.D, d.hc, d.nh, d.hd, d.ha, d.F, d.E
    names = [item[0] for item in scratch_list(d)]
    wnames = list(d.w)
    HR = R // PARTS

    def kernel(*refs):
        x_ref, e_ref, cot_ref, aux_ref, gains_ref = refs[:5]
        w_refs = dict(zip(wnames, refs[5 : 5 + len(wnames)]))
        lo_ref, ig_ref, eg_ref, gout_ref, sm_ref = refs[5 + len(wnames) : 10 + len(wnames)]
        tail = refs[10 + len(wnames) :]
        v = Dims()
        for name, ref in zip(names, tail):
            setattr(v, name, ref)
        ss, rs, ls = tail[len(names) :]

        dp, z = lax.axis_index("dp"), lax.axis_index("mp")
        c, chip = dp % 2, dp // 2
        a, u = z % 2, z // 2
        t = a + 2 * c
        sw = c + u - 2 * c * u
        dl = chip % d.nd
        base_dp = (chip - dl) * 2
        sib = (dp + 1 - 2 * c, z)
        zp = (dp, z + 1 - 2 * a)
        z2 = (dp, z + 2 - 4 * u)
        mate = (2 * chip + u, a + 2 * c)
        d0, d1 = dl % 2, dl // 2
        flips = [dl, dl + 1 - 2 * d0, dl + 2 - 4 * d1, 3 - dl][: d.nd]
        peers = [(base_dp + 2 * f + c, z) for f in flips]
        is_sw, not_sw = sw == 1, sw == 0

        count = [0]

        def new_id():
            count[0] += 1
            assert count[0] <= SEMS
            return count[0] - 1

        class Xfer:
            def __init__(self, src, dst, dev):
                self.i, self.src, self.dst, self.dev = new_id(), src, dst, dev

            def desc(self):
                return pltpu.make_async_remote_copy(
                    src_ref=self.src, dst_ref=self.dst, send_sem=ss.at[self.i], recv_sem=rs.at[self.i],
                    device_id={"dp": self.dev[0], "mp": self.dev[1]}, device_id_type=MESH,
                )

            def start(self):
                self.desc().start()

            def recv(self):
                self.desc().wait_recv()

            def sent(self):
                self.desc().wait_send()

        class Local:
            def __init__(self, src, dst):
                self.i, self.src, self.dst = new_id(), src, dst

            def desc(self):
                return pltpu.make_async_copy(self.src, self.dst, ls.at[self.i])

            def start(self):
                self.desc().start()

            def wait(self):
                self.desc().wait()

        class Swap:
            def __init__(self, src, dst):
                self.far, self.near = Xfer(src, dst, mate), Local(src, dst)

            def start(self):
                pl.when(is_sw)(self.far.start)
                pl.when(not_sw)(self.near.start)

            def wait(self):
                pl.when(is_sw)(self.far.recv)
                pl.when(not_sw)(self.near.wait)

            def sent(self):
                pl.when(is_sw)(self.far.sent)

        class Weight:
            def __init__(self, name):
                first, rows = d.w[name]
                sl = rows // d.nd
                mine = pl.ds(pl.multiple_of(dl * sl, 16), sl)
                here = v.wv.at[pl.ds(pl.multiple_of(first + dl * sl, 16), sl)]
                self.near = Local(w_refs[name], v.wv.at[pl.ds(first, rows)])
                self.far = Xfer(w_refs[name].at[mine], here, mate)
                self.on = [Xfer(here, here, peer) for peer in peers[1:]]

            def start(self):
                pl.when(is_sw)(self.far.start)
                pl.when(not_sw)(self.near.start)

            def forward(self):
                @pl.when(is_sw)
                def _():
                    self.far.recv()
                    for x in self.on:
                        x.start()

            def wait(self):
                pl.when(not_sw)(self.near.wait)

                @pl.when(is_sw)
                def _():
                    for x in self.on:
                        x.recv()

            def sent(self):
                @pl.when(is_sw)
                def _():
                    self.far.sent()
                    for x in self.on:
                        x.sent()

        def blk_ag(k):
            k1, k2 = k % 2, k // 2
            return (a + k2 - 2 * a * k2) + 2 * (c + k1 - 2 * c * k1)

        def blk_rs(k):
            return blk_ag(3 - k)

        class Gather:
            def __init__(self, full, rows, parts):
                self.parts = parts
                n = rows // parts
                at = lambda b, h: full.at[b, pl.ds(h * n, n)]
                b_zp = (1 - a) + 2 * c
                self.z = [Xfer(at(t, h), at(t, h), zp) for h in range(parts)]
                self.c = [Xfer(at(t, h), at(t, h), sib) for h in range(parts)]
                self.f = [Xfer(at(b_zp, h), at(b_zp, h), sib) for h in range(parts)]

            def send(self, h):
                self.z[h].start()
                self.c[h].start()

            def near(self):
                for x in self.c:
                    x.recv()

            def far(self):
                for x, y in zip(self.z, self.f):
                    x.recv()
                    y.start()

            def last(self):
                for x in self.f:
                    x.recv()

            def arrive(self, k):
                pl.when(k == 1)(self.near)
                pl.when(k == 2)(self.far)
                pl.when(k == 3)(self.last)

            def sent(self):
                for x in self.z + self.c + self.f:
                    x.sent()

        class Scatter:
            def __init__(self, pb, sb, rb, rows, parts):
                self.pb, self.sb, self.rb, self.parts, self.n = pb, sb, rb, parts, rows // parts
                at = lambda r, i, h: r.at[i, pl.ds(h * self.n, self.n)]
                self.c0 = Xfer(sb.at[0], rb.at[0], sib)
                self.z = [Xfer(at(sb, 1, h), at(rb, 1, h), zp) for h in range(parts)]
                self.c2 = Xfer(sb.at[2], rb.at[2], sib)

            def emit(self, k):
                @pl.when(k == 0)
                def _():
                    self.sb[0] = self.pb[...].astype(BF)
                    self.c0.start()

                @pl.when(k == 1)
                def _():
                    self.c0.recv()
                    for h in range(self.parts):
                        rows = pl.ds(h * self.n, self.n)
                        self.sb[1, rows] = (self.pb[rows] + self.rb[0, rows].astype(F32)).astype(BF)
                        self.z[h].start()

                @pl.when(k == 2)
                def _():
                    self.sb[2] = self.pb[...].astype(BF)
                    self.c2.start()

            def loop(self, partial):
                def step(k, carry):
                    partial(blk_rs(k))
                    self.emit(k)
                    return carry

                lax.fori_loop(0, 4, step, 0)

            def finish(self, fin):
                self.c2.recv()
                for h in range(self.parts):
                    rows = pl.ds(h * self.n, self.n)
                    self.z[h].recv()
                    fin(h, rows, self.pb[rows] + self.rb[2, rows].astype(F32) + self.rb[1, rows].astype(F32))

            def sent(self):
                for x in [self.c0, self.c2] + self.z:
                    x.sent()

        def ag_loop(gather, body):
            def step(k, carry):
                gather.arrive(k)
                body(blk_ag(k))
                return carry

            lax.fori_loop(0, 4, step, 0)

        def W(name, lo=0, rows=None):
            first, total = d.w[name]
            return v.wv[pl.ds(first + lo, total if rows is None else rows)]

        def gain(i):
            return gains_ref[pl.ds(i, 1)]

        sx = [Swap(x_ref.at[pl.ds(h * HR, HR)], v.xb.at[pl.ds(h * HR, HR)]) for h in range(PARTS)]
        saux, scot = Swap(aux_ref, v.aux), Swap(cot_ref, v.cotb)
        senc = Swap(e_ref, v.encf.at[z])
        weights = {name: Weight(name) for name in wnames}
        ag1, ag2, ag3 = (Gather(f, R, PARTS) for f in (v.h1f, v.h2f, v.h3f))
        agd3, agd2, agd1 = (Gather(f, R, PARTS) for f in (v.d3f, v.d2f, v.d1f))
        agenc = Gather(v.encf, E, 1)
        rs1, rs2, rs3, rs4, rs5 = (Scatter(v.pb, v.sb, v.rb, R, PARTS) for _ in range(5))
        rso = Scatter(v.opb, v.osb, v.orb, R, 1)
        rse = Scatter(v.epb, v.esb, v.erb, E, 1)
        out_lo, out_eg = Swap(v.lov, lo_ref), Swap(v.egv, eg_ref)
        out_ig = [Swap(v.igv.at[pl.ds(h * HR, HR)], ig_ref.at[pl.ds(h * HR, HR)]) for h in range(PARTS)]

        class Reduce:
            def __init__(self, name):
                self.base, self.rows, self.loc, self.land = d.groups[name]
                self.sl = sl = self.rows // d.nd
                self.tile = 96 if sl % 96 == 0 else sl
                at = lambda f: pl.ds(pl.multiple_of(self.base + f * sl, 16), sl)
                here = pl.ds(self.land, sl)
                self.own = at(dl)
                self.to = [
                    Xfer(v.gsend.at[at(f)], v.grecv.at[k, here], peer)
                    for k, (f, peer) in enumerate(zip(flips[1:], peers[1:]))
                ]
                self.zx = Xfer(v.gsend.at[self.own], v.gz.at[here], z2)
                self.keep = Local(v.gfo.at[here], gout_ref.at[self.own])
                self.spread = [Xfer(v.gfo.at[here], gout_ref.at[self.own], peer) for peer in peers[1:]]
                self.core = [Xfer(v.gfo.at[here], gout_ref.at[self.own], sib)] + [
                    Xfer(gout_ref.at[at(f)], gout_ref.at[at(f)], sib) for f in flips[1:]
                ]

            def tiles(self, rows, body):
                def step(i, carry):
                    body(pl.multiple_of(i * self.tile, 16))
                    return carry

                lax.fori_loop(0, rows // self.tile, step, 0)

            def send(self):
                def cast(r):
                    v.gsend[pl.ds(self.base + r, self.tile)] = v.gf[pl.ds(self.loc + r, self.tile)].astype(BF)

                self.tiles(self.rows, cast)
                for x in self.to:
                    x.start()

            def combine(self):
                for x in self.to:
                    x.recv()

                def add(r):
                    total = v.gf[pl.ds(self.loc + pl.multiple_of(dl * self.sl, 16) + r, self.tile)]
                    for k in range(d.nd - 1):
                        total = total + v.grecv[k, pl.ds(self.land + r, self.tile)].astype(F32)
                    v.gk[pl.ds(self.land + r, self.tile)] = total
                    v.gsend[pl.ds(pl.multiple_of(self.base + dl * self.sl, 16) + r, self.tile)] = total.astype(BF)

                self.tiles(self.sl, add)
                pl.when(is_sw)(self.zx.start)

            def finish(self):
                @pl.when(not_sw)
                def _():
                    self.zx.recv()

                    def add(r):
                        rows = pl.ds(self.land + r, self.tile)
                        v.gfo[rows] = (v.gk[rows] + v.gz[rows].astype(F32)).astype(BF)

                    self.tiles(self.sl, add)
                    self.keep.start()
                    for x in self.spread:
                        x.start()
                    self.core[0].start()

            def relay(self):
                @pl.when(not_sw)
                def _():
                    for x, y in zip(self.spread, self.core[1:]):
                        x.recv()
                        y.start()

            def done(self):
                for x in self.to:
                    x.sent()

                @pl.when(is_sw)
                def _():
                    self.zx.sent()
                    for x in self.core:
                        x.recv()

                @pl.when(not_sw)
                def _():
                    self.keep.wait()
                    for x in self.spread + self.core:
                        x.sent()

        redS, redC, redF = Reduce("S"), Reduce("C"), Reduce("F")

        bar = pltpu.get_barrier_semaphore()
        for dev in [sib, zp, z2] + peers[1:]:
            pl.semaphore_signal(bar, inc=1, device_id={"dp": dev[0], "mp": dev[1]}, device_id_type=MESH)

        @pl.when(is_sw)
        def _():
            pl.semaphore_signal(bar, inc=1, device_id={"dp": mate[0], "mp": mate[1]}, device_id_type=MESH)

        pl.semaphore_wait(bar, 2 + d.nd + sw)

        for x in sx:
            x.start()
        saux.start()
        weights["qkv"].start()

        for h in range(PARTS):
            sx[h].wait()
            rows = pl.ds(h * HR, HR)
            v.h1f[t, rows] = norm_fwd(v.xb[rows].astype(F32), gain(0))
            ag1.send(h)
        weights["so"].start()
        senc.start()
        weights["qkv"].forward()
        saux.wait()

        row16 = lax.broadcasted_iota(jnp.int32, (PADH, R), 0)
        ones_row = jnp.where(row16 == 0, 1.0, 0.0).astype(BF)

        def mask_rows(row, b):
            line = v.aux[pl.ds(row, 1), pl.ds(b * R, R)]
            return jnp.where(row16 == 0, jnp.broadcast_to(line, (PADH, R)), 0.0).astype(BF)

        for b in range(4):
            for h in range(nh):
                v.qa[b, h, pl.ds(hd, PADH)] = ones_row
                v.q2a[b, h, pl.ds(hd, PADH)] = ones_row
                v.ka[b, h, pl.ds(hd, PADH)] = mask_rows(0, b)
        for b in range(d.ne):
            for h in range(nh):
                v.k2a[b, h, pl.ds(hd, PADH)] = mask_rows(1, b)
        for h in range(nh):
            for i in range(2):
                line = v.aux[pl.ds(2 + h, 1), pl.ds(i * 2 * R, 2 * R)]
                v.bias[h, i] = pltpu.roll(jnp.broadcast_to(line, (R, 2 * R)), 0, 1, stride=1, stride_axis=0)[:, :R]
            v.bias[h, 2] = jnp.broadcast_to(v.aux[pl.ds(2 + nh + h, 1), pl.ds(0, R)], (R, R))
        weights["qkv"].wait()

        def project_self(b):
            rows = v.h1f[b]
            q = dot_nt(W("qkv", 0, hc), rows).astype(BF)
            k = dot_nt(W("qkv", hc, hc), rows).astype(BF)
            for h in range(nh):
                v.qa[b, h, pl.ds(0, hd)] = q[h * hd : (h + 1) * hd]
                v.ka[b, h, pl.ds(0, hd)] = k[h * hd : (h + 1) * hd]
            v.vT[b] = dot_nt(W("qkv", 2 * hc, hc), rows).astype(BF)

        ag_loop(ag1, project_self)
        ag1.sent()
        senc.wait()
        agenc.send(0)
        for name in ("cq", "ckv", "co"):
            weights[name].start()
        scot.start()
        weights["so"].forward()

        def attend(b, blocks, qa, ka, vT, out, lse, biased):
            def head(h, carry):
                feat = pl.ds(pl.multiple_of(h * hd, hd), hd)
                q = qa[b, h]

                def block(j, state):
                    m, total, acc = state
                    s = dot_tn(ka[j, h], q)
                    if biased:
                        s = s + v.bias[h, jnp.minimum(b - j, 2)]
                    new = jnp.maximum(m, jnp.max(s, axis=0, keepdims=True))
                    p = jnp.exp(s - new)
                    scale = jnp.exp(m - new)
                    total = total * scale + jnp.sum(p, axis=0, keepdims=True)
                    acc = acc * scale + dot_nn(vT[j, feat], p.astype(BF))
                    return new, total, acc

                first = (jnp.full((1, R), -1e30, F32), jnp.zeros((1, R), F32), jnp.zeros((hd, R), F32))
                m, total, acc = lax.fori_loop(0, blocks, block, first)
                out[b, feat] = (acc / total).astype(BF)
                lse[b, pl.ds(h, 1)] = m + jnp.log(total)
                return carry

            lax.fori_loop(0, nh, head, 0)

        def attend_back(b, blocks, qa, ka, vT, out, lse, dqT, biased):
            def head(h, carry):
                feat = pl.ds(pl.multiple_of(h * hd, hd), hd)
                q, da = qa[b, h], v.da[feat]
                inner = jnp.sum(da.astype(F32) * out[b, feat].astype(F32), axis=0, keepdims=True)
                logsum = lse[b, pl.ds(h, 1)]

                def block(j, dq):
                    k = ka[j, h]
                    s = dot_tn(k, q)
                    if biased:
                        kind = jnp.minimum(b - j, 2)
                        s = s + v.bias[h, kind]
                    p = jnp.exp(s - logsum)
                    ds = p * (dot_tn(vT[j, feat], da) - inner)
                    low = ds.astype(BF)
                    v.dka[j, h] += dot_nt(q, low)
                    v.dva[j, feat] += dot_nt(da, p.astype(BF))
                    if biased:
                        v.dsacc[h, kind] += ds
                    return dq + dot_nn(k, low)

                dq = lax.fori_loop(0, blocks, block, jnp.zeros((ha, R), F32))
                dqT[b, feat] = dq[:hd].astype(BF)
                return carry

            lax.fori_loop(0, nh, head, 0)

        weights["so"].wait()

        def self_out_part(b):
            attend(b, b + 1, v.qa, v.ka, v.vT, v.o1, v.lse1, True)
            v.pb[...] = dot_tn(v.o1[b], W("so"))

        rs1.loop(self_out_part)
        agenc.near()
        agenc.far()
        for name in ("cq", "ckv", "co"):
            weights[name].forward()
        agenc.last()
        agenc.sent()
        weights["ckv"].wait()
        per = R // E
        for b in range(4):
            rows = v.encf[b]
            lanes = pl.ds((b % per) * E, E)
            k = dot_nt(W("ckv", 0, hc), rows).astype(BF)
            for h in range(nh):
                v.k2a[b // per, h, pl.ds(0, hd), lanes] = k[h * hd : (h + 1) * hd]
            v.v2T[b // per, :, lanes] = dot_nt(W("ckv", hc, hc), rows).astype(BF)

        def fin1(h, rows, total):
            x1 = v.xb[rows].astype(F32) + total
            v.x1[rows] = x1
            v.h2f[t, rows] = norm_fwd(x1, gain(1))
            ag2.send(h)

        rs1.finish(fin1)
        rs1.sent()
        for name in ("gu", "fo"):
            weights[name].start()

        weights["cq"].wait()

        def cross_block(b):
            q = dot_nt(W("cq"), v.h2f[b]).astype(BF)
            for h in range(nh):
                v.q2a[b, h, pl.ds(0, hd)] = q[h * hd : (h + 1) * hd]
            attend(b, d.ne, v.q2a, v.k2a, v.v2T, v.o2, v.lse2, False)

        ag_loop(ag2, cross_block)
        ag2.sent()
        scot.wait()
        v.d3f[t] = v.cotb[...]
        for h in range(PARTS):
            agd3.send(h)
        weights["co"].wait()

        def cross_out_part(b):
            v.pb[...] = dot_tn(v.o2[b], W("co"))

        rs2.loop(cross_out_part)
        for name in ("gu", "fo"):
            weights[name].forward()
        agd3.near()
        agd3.far()

        def fin2(h, rows, total):
            x2 = v.x1[rows] + total
            v.x2[rows] = x2
            v.h3f[t, rows] = norm_fwd(x2, gain(2))
            ag3.send(h)

        rs2.finish(fin2)
        rs2.sent()
        agd3.last()
        agd3.sent()
        for name in ("gu", "fo"):
            weights[name].wait()

        fc = 128

        def hidden_block(b):
            def chunk(i, carry):
                r = pl.multiple_of(i * fc, fc)
                rows, back = v.h3f[b], v.d3f[b]
                gu, fo = d.w["gu"][0], d.w["fo"][0]
                gate = dot_nt(v.wv[pl.ds(gu + r, fc)], rows)
                up = dot_nt(v.wv[pl.ds(gu + F + r, fc)], rows)
                sq = gate * gate
                th = jnp.tanh(gate * (GELU_C + (GELU_C * 0.044715) * sq))
                half = 0.5 + 0.5 * th
                gelu = gate * half
                slope = half + gate * (0.5 - 0.5 * th * th) * (GELU_C + (3.0 * GELU_C * 0.044715) * sq)
                v.actT[b, pl.ds(r, fc)] = (gelu * up).astype(BF)
                dact = dot_nt(v.wv[pl.ds(fo + r, fc)], back)
                v.dguT[b, pl.ds(r, fc)] = (dact * up * slope).astype(BF)
                v.dguT[b, pl.ds(F + r, fc)] = (dact * gelu).astype(BF)
                return carry

            lax.fori_loop(0, F // fc, chunk, 0)

        ag_loop(ag3, hidden_block)
        ag3.sent()

        def hidden_back_part(b):
            v.pb[...] = dot_tn(v.dguT[b], W("gu"))

        rs3.loop(hidden_back_part)

        def grads(at, lhs, rows, rhs, tile):
            def step(i, carry):
                r = pl.multiple_of(i * tile, 64)
                total = dot_nn(lhs[0, pl.ds(r, tile)], rhs[0])
                for b in range(1, 4):
                    total = total + dot_nn(lhs[b, pl.ds(r, tile)], rhs[b])
                v.gf[pl.ds(at + r, tile)] = total
                return carry

            lax.fori_loop(0, rows // tile, step, 0)

        def loc(name, group):
            base, _, at, _ = d.groups[group]
            return d.w[name][0] - base + at

        grads(loc("gu", "F"), v.dguT, 2 * F, v.h3f, 256)

        def add_gain(i, h, part):
            if h == 0:
                v.smc[pl.ds(i, 1)] = part
            else:
                v.smc[pl.ds(i, 1)] += part

        v.smc[...] = jnp.zeros(v.smc.shape, F32)

        def fin3(h, rows, total):
            grad, part = norm_bwd(v.x2[rows], gain(2), total)
            add_gain(2, h, part)
            g2 = v.cotb[rows].astype(F32) + grad
            v.gb[rows] = g2
            v.d2f[t, rows] = g2.astype(BF)
            agd2.send(h)

        rs3.finish(fin3)
        rs3.sent()
        grads(loc("fo", "F"), v.actT, F, v.d3f, 256)
        redF.send()

        v.dka[...] = jnp.zeros(v.dka.shape, F32)
        v.dva[...] = jnp.zeros(v.dva.shape, F32)

        def cross_back_block(b):
            v.da[...] = dot_nt(W("co"), v.d2f[b]).astype(BF)
            attend_back(b, d.ne, v.q2a, v.k2a, v.v2T, v.o2, v.lse2, v.dq2T, False)

        ag_loop(agd2, cross_back_block)
        agd2.sent()

        def cross_q_part(b):
            v.pb[...] = dot_tn(v.dq2T[b], W("cq"))

        rs4.loop(cross_q_part)
        for b in range(4):
            lanes = pl.ds((b % per) * E, E)
            for h in range(nh):
                v.dkv2T[b, pl.ds(h * hd, hd)] = v.dka[b // per, h, pl.ds(0, hd), lanes].astype(BF)
            v.dkv2T[b, pl.ds(hc, hc)] = v.dva[b // per, :, lanes].astype(BF)
        redF.combine()
        grads(loc("cq", "C"), v.dq2T, hc, v.h2f, hc)
        grads(loc("co", "C"), v.o2, hc, v.d2f, hc)
        grads(loc("ckv", "C"), v.dkv2T, 2 * hc, v.encf, hc)

        def fin4(h, rows, total):
            grad, part = norm_bwd(v.x1[rows], gain(1), total)
            add_gain(1, h, part)
            g1 = v.gb[rows] + grad
            v.gb[rows] = g1
            v.d1f[t, rows] = g1.astype(BF)
            agd1.send(h)

        rs4.finish(fin4)
        rs4.sent()
        redC.send()

        v.dka[...] = jnp.zeros(v.dka.shape, F32)
        v.dva[...] = jnp.zeros(v.dva.shape, F32)
        v.dsacc[...] = jnp.zeros(v.dsacc.shape, F32)

        def self_back_block(b):
            v.da[...] = dot_nt(W("so"), v.d1f[b]).astype(BF)
            attend_back(b, b + 1, v.qa, v.ka, v.vT, v.o1, v.lse1, v.dqkvT, True)

        ag_loop(agd1, self_back_block)
        agd1.sent()
        redF.finish()
        redC.combine()

        def enc_part(b):
            v.epb[...] = dot_tn(v.dkv2T[b], W("ckv"))

        rse.loop(enc_part)

        for b in range(4):
            for h in range(nh):
                v.dqkvT[b, pl.ds(hc + h * hd, hd)] = v.dka[b, h, pl.ds(0, hd)].astype(BF)
            v.dqkvT[b, pl.ds(2 * hc, hc)] = v.dva[b].astype(BF)
        grads(loc("qkv", "S"), v.dqkvT, 3 * hc, v.h1f, hc)
        grads(loc("so", "S"), v.o1, hc, v.d1f, hc)
        redS.send()

        def self_qkv_part(b):
            v.pb[...] = dot_tn(v.dqkvT[b], W("qkv"))

        rs5.loop(self_qkv_part)

        def hidden_out_part(b):
            v.opb[...] = dot_tn(v.actT[b], W("fo"))

        rso.loop(hidden_out_part)
        redC.finish()
        redF.relay()

        iota0 = lax.broadcasted_iota(jnp.int32, (R, R), 0)
        iota1 = lax.broadcasted_iota(jnp.int32, (R, R), 1)
        flip = (iota0 + iota1 == R - 1).astype(F32)

        def diagonals(h, i):
            turned = lax.dot_general(
                flip, v.dsacc[h, i], (((1,), (0,)), ((), ())), precision=lax.Precision.HIGHEST, preferred_element_type=F32
            )
            wide = jnp.concatenate([turned, jnp.zeros((R, R), F32)], axis=1)
            return jnp.sum(pltpu.roll(wide, 0, 1, stride=1, stride_axis=0), axis=0, keepdims=True)

        lane = lax.broadcasted_iota(jnp.int32, (1, 2 * R), 1)
        for h in range(nh):
            near, off = diagonals(h, 0), diagonals(h, 1)
            far = jnp.sum(jnp.sum(v.dsacc[h, 2], axis=0, keepdims=True), axis=1, keepdims=True)
            off = off + jnp.where(lane == 2 * R - 1, far, 0.0)
            line = jnp.concatenate([pltpu.roll(near, R + 1, 1)[:, :R], off], axis=1)
            for q in range(4):
                v.smc[pl.ds(3 + q * nh + h, 1), pl.ds(0, 3 * R)] = jnp.where(t == q, line, 0.0)

        def fin5(h, rows, total):
            grad, part = norm_bwd(v.xb[rows].astype(F32), gain(0), total)
            add_gain(0, h, part)
            v.igv[rows] = (v.gb[rows] + grad).astype(BF)
            out_ig[h].start()

        rs5.finish(fin5)
        rs5.sent()
        redS.combine()

        def fin_out(h, rows, total):
            v.lov[rows] = (v.x2[rows] + total).astype(BF)

        rso.finish(fin_out)
        rso.sent()
        out_lo.start()

        def fin_enc(h, rows, total):
            v.egv[rows] = total.astype(BF)

        rse.finish(fin_enc)
        rse.sent()
        out_eg.start()

        steps = [sib, zp, z2] + peers[1:3]
        v.sms[0] = v.smc[...]
        small = [Xfer(v.sms.at[i], v.smr.at[i], dev) for i, dev in enumerate(steps)]
        for i, x in enumerate(small):
            x.start()
            if i == 1:
                redC.relay()
            if i == 2:
                redS.finish()
            x.recv()
            v.sms[i + 1] = v.sms[i] + v.smr[i]
        sm_ref[...] = v.sms[len(steps)]
        redS.relay()

        for x in small:
            x.sent()
        for x in [saux, scot, senc] + sx:
            x.sent()
        for name in wnames:
            weights[name].sent()
        for x in [out_lo, out_eg] + out_ig:
            x.wait()
            x.sent()
        for r in (redF, redC, redS):
            r.done()

    return kernel


def local_fn(mesh):
    def local(x_in, enc_in, cotangent, dec_len, enc_len, self_qkv, self_out, cross_q, cross_kv, cross_out, ff_in, ff_out, gains, table):
        d = make_dims(mesh, x_in, enc_in, self_qkv, ff_in, table)
        R, D, hc, nh, F = d.R, d.D, d.hc, d.nh, d.F
        hbm = pl.BlockSpec(memory_space=pl.ANY)
        vmem = pl.BlockSpec(memory_space=pltpu.VMEM)
        ws = {
            "qkv": jnp.transpose(self_qkv, (1, 2, 0)).reshape(3 * hc, D),
            "so": self_out,
            "cq": jnp.transpose(cross_q),
            "ckv": jnp.transpose(cross_kv, (1, 2, 0)).reshape(2 * hc, D),
            "co": cross_out,
            "gu": jnp.transpose(ff_in, (1, 2, 0)).reshape(2 * F, D),
            "fo": ff_out,
        }
        lane = jnp.arange(4 * R, dtype=jnp.int32)
        dist = jnp.where(lane < 2 * R, lane, jnp.where(lane < 3 * R, lane - R, lane - 3 * R))
        onehot = (bucket_index(dist)[:, None] == jnp.arange(NB)[None, :]).astype(BF)
        lines = jnp.einsum("vh,lv->hl", table, onehot, preferred_element_type=F32)
        lines = jnp.where((lane >= R) & (lane < 2 * R), MASK_FILL, lines)
        pos = lane[None, :]
        aux = jnp.concatenate(
            [
                jnp.where(pos < dec_len[0], 0.0, MASK_FILL),
                jnp.where(pos < enc_len[0], 0.0, MASK_FILL),
                lines,
                jnp.broadcast_to(table[NB - 1].astype(F32)[:, None], (nh, 4 * R)),
                jnp.zeros((d.axr - 2 - 2 * nh, 4 * R), F32),
            ],
            axis=0,
        )
        gains_f = gains.astype(F32)
        outs = pl.pallas_call(
            build_kernel(d),
            out_shape=(
                jax.ShapeDtypeStruct((R, D), BF),
                jax.ShapeDtypeStruct((R, D), BF),
                jax.ShapeDtypeStruct((d.E, D), BF),
                jax.ShapeDtypeStruct((d.rows, D), BF),
                jax.ShapeDtypeStruct((d.small, D), F32),
            ),
            in_specs=[hbm, hbm, hbm, hbm, vmem] + [hbm] * len(d.w),
            out_specs=(hbm, hbm, hbm, hbm, vmem),
            scratch_shapes=[pltpu.VMEM(shape, dtype) for _, shape, dtype in scratch_list(d)]
            + [pltpu.SemaphoreType.DMA((SEMS,))] * 3,
            compiler_params=pltpu.CompilerParams(collective_id=0, has_side_effects=True, vmem_limit_bytes=63 << 20),
        )(x_in, enc_in, cotangent, aux, gains_f, *[ws[name] for name in d.w])
        lo, ig, eg, gw, sm = outs
        others = d.ndp // (2 * d.nd)
        if others > 1:
            gw, sm = lax.psum((gw.astype(F32), sm), "dp")
            gw, sm = gw * (1.0 / (2 * d.nd)), sm * (1.0 / (2 * d.nd))
        g = {name: gw[first : first + rows].astype(F32) for name, (first, rows) in d.w.items()}
        mine = lax.dynamic_slice_in_dim(sm, 3 + lax.axis_index("mp") * nh, nh, axis=0)
        col = jnp.arange(D)
        dist = jnp.where(col < R, col, jnp.where(col < 3 * R - 1, col - R + 1, 4 * R))
        pick = (bucket_index(dist)[:, None] == jnp.arange(NB)[None, :]).astype(F32)
        table_grad = jnp.einsum("hl,lv->vh", mine, pick, precision=lax.Precision.HIGHEST, preferred_element_type=F32)
        return (
            lo,
            ig.astype(F32),
            eg.astype(F32),
            jnp.transpose(g["qkv"].reshape(3, hc, D), (2, 0, 1)),
            g["so"],
            jnp.transpose(g["cq"]),
            jnp.transpose(g["ckv"].reshape(2, hc, D), (2, 0, 1)),
            g["co"],
            jnp.transpose(g["gu"].reshape(2, F, D), (2, 0, 1)),
            g["fo"],
            sm[:3],
            table_grad,
        )

    return local


def solution(mesh):
    rows = P(("dp", "mp"), None)
    in_specs = (
        rows, rows, rows, P("dp"), P("dp"), P(None, None, "mp"), P("mp", None), P(None, "mp"), P(None, None, "mp"),
        P("mp", None), P(None, None, "mp"), P("mp", None), P(), P(None, "mp"),
    )
    out_specs = (
        rows, rows, rows, P(None, None, "mp"), P("mp", None), P(None, "mp"), P(None, None, "mp"), P("mp", None),
        P(None, None, "mp"), P("mp", None), P(), P(None, "mp"),
    )
    return jax.shard_map(local_fn(mesh), mesh=mesh, in_specs=in_specs, out_specs=out_specs, check_vma=False)
```

```python
import math

import jax
import jax.numpy as jnp
from jax import lax
from jax.experimental import pallas as pl
from jax.experimental.pallas import tpu as pltpu
from jax.sharding import PartitionSpec as P

NB = 32
MAXD = 128
NORM_EPS = 1e-06
MASK_FILL = -1000000000.0
MESH = pl.DeviceIdType.MESH
BF = jnp.bfloat16
F32 = jnp.float32
PARTS = 2
PADH = 16
GELU_C = math.sqrt(2.0 / math.pi)
SEMS = 224


def bucket_index(distance):
    half_count = NB // 2
    clipped = jnp.maximum(distance, 0)
    bucket_ids = jnp.minimum(clipped, half_count)
    for level_pos in range(1, half_count):
        threshold = math.ceil(half_count * (MAXD / half_count) ** (level_pos / half_count))
        bucket_ids = bucket_ids + (clipped >= threshold).astype(jnp.int32)
    return bucket_ids


def dot_nn(a, b):
    return lax.dot_general(a, b, (((1,), (0,)), ((), ())), preferred_element_type=F32)


def dot_nt(a, b):
    return lax.dot_general(a, b, (((1,), (1,)), ((), ())), preferred_element_type=F32)


def dot_tn(a, b):
    return lax.dot_general(a, b, (((0,), (0,)), ((), ())), preferred_element_type=F32)


def norm_fwd(v, g):
    inv = lax.rsqrt(jnp.mean(v * v, axis=-1, keepdims=True) + NORM_EPS)
    return (v * inv * g).astype(BF)


def norm_bwd(v, g, u):
    inv = lax.rsqrt(jnp.mean(v * v, axis=-1, keepdims=True) + NORM_EPS)
    gu = u * g
    mean = jnp.mean(gu * v, axis=-1, keepdims=True)
    grad = inv * gu - v * (inv * inv * inv * mean)
    gain = jnp.sum(u * v * inv, axis=0, keepdims=True)
    return grad, gain


class Dims:
    pass


def make_dims(mesh, x_in, enc_in, self_qkv, ff_in, table):
    d = Dims()
    d.ndp, d.nmp = mesh.shape["dp"], mesh.shape["mp"]
    d.nd = min(4, d.ndp // 2)
    d.R, d.D = x_in.shape
    d.E = enc_in.shape[0]
    d.nh = table.shape[1]
    d.hc = self_qkv.shape[2]
    d.hd = d.hc // d.nh
    d.F = ff_in.shape[2]
    d.ha = d.hd + PADH
    d.ne = 4 * d.E // d.R
    d.axr = -(-(2 + 2 * d.nh) // 8) * 8
    hc, F = d.hc, d.F
    names = (("qkv", 3 * hc), ("so", hc), ("cq", hc), ("ckv", 2 * hc), ("co", hc), ("gu", 2 * F), ("fo", F))
    d.w, at = {}, 0
    for name, rows in names:
        d.w[name] = (at, rows)
        at += rows
    d.rows = at
    s, c = 4 * hc, 4 * hc
    d.groups = {}
    land = 0
    for name, base, rows in (("S", 0, s), ("C", s, c), ("G", s + c, 2 * F), ("H", s + c + 2 * F, F)):
        d.groups[name] = (base, rows, 0, land)
        land += rows // d.nd
    d.land = land
    d.locrows = max(s, c, 2 * F)
    d.small = -(-(3 + 4 * d.nh) // 8) * 8
    return d


def scratch_list(d):
    R, D, hc, nh, hd, ha, F, E = d.R, d.D, d.hc, d.nh, d.hd, d.ha, d.F, d.E
    full = ((4, R, D), BF)
    pair = ((2, 2, R, D), BF)
    HR = R // 2
    return [
        ("xb", (R, D), BF), ("cotb", (R, D), BF), ("aux", (d.axr, 4 * R), F32), ("wv", (d.rows, D), BF),
        ("h1f",) + full, ("h2f",) + pair, ("h3f",) + pair, ("d3f",) + pair, ("d2f",) + pair, ("d1f",) + full,
        ("encf", (4, E, D), BF),
        ("qa", (4, nh, ha, R), BF), ("ka", (4, nh, ha, R), BF), ("vT", (4, hc, R), BF), ("o1", (4, hc, R), BF),
        ("q2a", (2, 2, nh, ha, R), BF), ("k2a", (d.ne, nh, ha, R), BF), ("v2T", (d.ne, hc, R), BF), ("o2", (2, 2, hc, R), BF),
        ("lse1", (4, 8, R), F32), ("lse2", (2, 2, 8, R), F32),
        ("bias", (nh, 3, R, R), F32), ("dsacc", (nh, 3, R, R), F32),
        ("x1", (R, D), F32), ("x2", (R, D), F32), ("gb", (R, D), F32),
        ("pb", (R, D), F32), ("pf", (R, D), F32), ("sb", (2, 3, HR, D), BF), ("rb", (2, 3, HR, D), BF),
        ("opb", (R, D), F32), ("osb", (2, 3, HR, D), BF), ("orb", (2, 3, HR, D), BF), ("lov", (R, D), BF), ("igv", (R, D), BF),
        ("epb", (E, D), F32), ("esb", (1, 3, E, D), BF), ("erb", (1, 3, E, D), BF), ("egv", (E, D), BF),
        ("actT", (2, 2, F, R), BF), ("dguT", (2, 2, 2 * F, R), BF), ("gus", (3 * F, R), F32),
        ("da", (hc, R), BF), ("dqkvT", (4, 3 * hc, R), BF), ("dq2T", (2, 2, hc, R), BF), ("dkv2T", (4, 2 * hc, E), BF),
        ("dka", (4, nh, ha, R), F32), ("dva", (4, hc, R), F32),
        ("gf", (d.locrows, D), F32), ("gsend", (d.rows, D), BF), ("grecv", (max(d.nd - 1, 1), d.land, D), BF),
        ("gz", (d.land, D), BF), ("gk", (d.land, D), F32), ("gfo", (d.land, D), BF),
        ("smc", (d.small, D), F32), ("sms", (3, d.small, D), F32), ("smr", (7, d.small, D), F32),
    ]


def build_kernel(d):
    R, D, hc, nh, hd, ha, F, E = d.R, d.D, d.hc, d.nh, d.hd, d.ha, d.F, d.E
    names = [item[0] for item in scratch_list(d)]
    wnames = list(d.w)
    HR = R // PARTS

    def kernel(*refs):
        x_ref, e_ref, cot_ref, aux_ref, gains_ref = refs[:5]
        w_refs = dict(zip(wnames, refs[5 : 5 + len(wnames)]))
        lo_ref, ig_ref, eg_ref, gout_ref, sm_ref = refs[5 + len(wnames) : 10 + len(wnames)]
        tail = refs[10 + len(wnames) :]
        v = Dims()
        for name, ref in zip(names, tail):
            setattr(v, name, ref)
        ss, rs, ls = tail[len(names) :]

        dp, z = lax.axis_index("dp"), lax.axis_index("mp")
        c, chip = dp % 2, dp // 2
        a, u = z % 2, z // 2
        t = a + 2 * c
        sw = c + u - 2 * c * u
        dl = chip % d.nd
        base_dp = (chip - dl) * 2
        sib = (dp + 1 - 2 * c, z)
        zp = (dp, z + 1 - 2 * a)
        z2 = (dp, z + 2 - 4 * u)
        z3 = (dp, 3 - z)
        mate = (2 * chip + u, a + 2 * c)
        d0, d1 = dl % 2, dl // 2
        flips = [dl, dl + 1 - 2 * d0, dl + 2 - 4 * d1, 3 - dl][: d.nd]
        peers = [(base_dp + 2 * f + c, z) for f in flips]
        is_sw, not_sw = sw == 1, sw == 0

        count = [0]

        def new_id():
            count[0] += 1
            assert count[0] <= SEMS
            return count[0] - 1

        class Xfer:
            def __init__(self, src, dst, dev, i=None):
                self.i, self.src, self.dst, self.dev = new_id() if i is None else i, src, dst, dev

            def desc(self):
                return pltpu.make_async_remote_copy(
                    src_ref=self.src, dst_ref=self.dst, send_sem=ss.at[self.i], recv_sem=rs.at[self.i],
                    device_id={"dp": self.dev[0], "mp": self.dev[1]}, device_id_type=MESH,
                )

            def start(self):
                self.desc().start()

            def recv(self):
                self.desc().wait_recv()

            def sent(self):
                self.desc().wait_send()

        class Local:
            def __init__(self, src, dst):
                self.i, self.src, self.dst = new_id(), src, dst

            def desc(self):
                return pltpu.make_async_copy(self.src, self.dst, ls.at[self.i])

            def start(self):
                self.desc().start()

            def wait(self):
                self.desc().wait()

        class Swap:
            def __init__(self, src, dst):
                self.far, self.near = Xfer(src, dst, mate), Local(src, dst)

            def start(self):
                pl.when(is_sw)(self.far.start)
                pl.when(not_sw)(self.near.start)

            def wait(self):
                pl.when(is_sw)(self.far.recv)
                pl.when(not_sw)(self.near.wait)

            def sent(self):
                pl.when(is_sw)(self.far.sent)

        class Weight:
            def __init__(self, name, piece=0, pieces=1):
                first, rows = d.w[name]
                rows = rows // pieces
                at = piece * rows
                first += at
                sl = rows // d.nd
                mine = pl.ds(pl.multiple_of(at + dl * sl, 16), sl)
                here = v.wv.at[pl.ds(pl.multiple_of(first + dl * sl, 16), sl)]
                self.near = Local(w_refs[name].at[pl.ds(at, rows)], v.wv.at[pl.ds(first, rows)])
                self.far = Xfer(w_refs[name].at[mine], here, mate)
                self.on = [Xfer(here, here, peer) for peer in peers[1:]]

            def start(self):
                pl.when(is_sw)(self.far.start)
                pl.when(not_sw)(self.near.start)

            def forward(self):
                @pl.when(is_sw)
                def _():
                    self.far.recv()
                    for x in self.on:
                        x.start()

            def wait(self):
                pl.when(not_sw)(self.near.wait)

                @pl.when(is_sw)
                def _():
                    for x in self.on:
                        x.recv()

            def sent(self):
                @pl.when(is_sw)
                def _():
                    self.far.sent()
                    for x in self.on:
                        x.sent()

        def blk_ag(k):
            k1, k2 = k % 2, k // 2
            return (a + k2 - 2 * a * k2) + 2 * (c + k1 - 2 * c * k1)

        def blk_rs(k):
            return blk_ag(3 - k)

        class Gather:
            def __init__(self, full, rows, parts):
                self.parts = parts
                n = rows // parts
                at = lambda b, h: full.at[b, pl.ds(h * n, n)]
                b_zp = (1 - a) + 2 * c
                self.z = [Xfer(at(t, h), at(t, h), zp) for h in range(parts)]
                self.c = [Xfer(at(t, h), at(t, h), sib) for h in range(parts)]
                self.f = [Xfer(at(b_zp, h), at(b_zp, h), sib) for h in range(parts)]

            def send(self, h):
                self.z[h].start()
                self.c[h].start()

            def near(self):
                for x in self.c:
                    x.recv()

            def far(self):
                for x, y in zip(self.z, self.f):
                    x.recv()
                    y.start()

            def last(self):
                for x in self.f:
                    x.recv()

            def arrive(self, k):
                pl.when(k == 1)(self.near)
                pl.when(k == 2)(self.far)
                pl.when(k == 3)(self.last)

            def sent(self):
                for x in self.z + self.c + self.f:
                    x.sent()

        class PairGather:
            def __init__(self, full):
                self.full, self.ids = full, [new_id() for _ in range(6)][0]

            def own(self, h):
                return self.full.at[h, a, pl.ds(pl.multiple_of(c * HR, HR), HR)]

            def z(self, h):
                return Xfer(self.own(h), self.own(h), zp, self.ids + h)

            def c(self, h):
                return Xfer(self.own(h), self.own(h), sib, self.ids + 2 + h)

            def f(self, h):
                there = self.full.at[h, 1 - a, pl.ds(pl.multiple_of(c * HR, HR), HR)]
                return Xfer(there, there, sib, self.ids + 4 + h)

            def send(self, h):
                self.z(h).start()
                self.c(h).start()

            def near(self, h):
                self.c(h).recv()

            def pass_on(self, h):
                self.z(h).recv()
                self.f(h).start()

            def last(self, h):
                self.f(h).recv()

            def sent(self):
                for h in range(2):
                    for x in (self.z(h), self.c(h), self.f(h)):
                        x.sent()

        class Scatter:
            def __init__(self, pb, sb, rb):
                self.pb, self.sb, self.rb = pb, sb, rb
                self.parts, self.n = sb.shape[0], sb.shape[2]
                self.ids = [new_id() for _ in range(3 * self.parts)][0]

            def rows(self, h):
                return pl.ds(h * self.n if isinstance(h, int) else pl.multiple_of(h * self.n, self.n), self.n)

            def x(self, slot, h, dev):
                return Xfer(self.sb.at[h, slot], self.rb.at[h, slot], dev, self.ids + slot * self.parts + h)

            def c0(self, h):
                return self.x(0, h, sib)

            def z(self, h):
                return self.x(1, h, zp)

            def c2(self, h):
                return self.x(2, h, sib)

            def emit(self, k):
                @pl.when(k == 0)
                def _():
                    for h in range(self.parts):
                        self.sb[h, 0] = self.pb[self.rows(h)].astype(BF)
                        self.c0(h).start()

                @pl.when(k == 1)
                def _():
                    for h in range(self.parts):
                        self.c0(h).recv()
                        self.sb[h, 1] = (self.pb[self.rows(h)] + self.rb[h, 0].astype(F32)).astype(BF)
                        self.z(h).start()

                @pl.when(k == 2)
                def _():
                    for h in range(self.parts):
                        self.sb[h, 2] = self.pb[self.rows(h)].astype(BF)
                        self.c2(h).start()

            def loop(self, partial):
                def step(k, carry):
                    partial(blk_rs(k))
                    self.emit(k)
                    return carry

                lax.fori_loop(0, 4, step, 0)

            def emit_pair(self, h, partial, kick=True):
                mine = pl.ds(pl.multiple_of(c * HR, HR), HR)
                other = pl.ds(pl.multiple_of((1 - c) * HR, HR), HR)
                v.pf[...] = partial(h, 1 - a)
                self.sb[h, 0] = v.pf[other].astype(BF)
                self.c0(h).start()
                self.sb[h, 1] = v.pf[mine].astype(BF)
                v.pf[...] = partial(h, a)
                self.sb[h, 2] = v.pf[other].astype(BF)
                self.c2(h).start()
                self.pb[self.rows(h)] = v.pf[mine]
                self.c0(h).recv()
                self.sb[h, 1] = (self.sb[h, 1].astype(F32) + self.rb[h, 0].astype(F32)).astype(BF)
                if kick:
                    self.z(h).start()

            def kick(self):
                for h in range(self.parts):
                    self.z(h).start()

            def finish(self, h, fin):
                self.c2(h).recv()
                self.z(h).recv()
                rows = self.rows(h)
                fin(h, rows, self.pb[rows] + self.rb[h, 2].astype(F32) + self.rb[h, 1].astype(F32))

            def sent(self):
                for h in range(self.parts):
                    for x in (self.c0(h), self.z(h), self.c2(h)):
                        x.sent()

        def ag_loop(gather, body):
            def step(k, carry):
                gather.arrive(k)
                body(blk_ag(k))
                return carry

            lax.fori_loop(0, 4, step, 0)

        def halves(gather, body, scatter, partial, after=None):
            def half(h, carry):
                def step(k, inner):
                    pl.when(k == 0)(lambda: gather.near(h))

                    @pl.when(k == 1)
                    def _():
                        gather.pass_on(h)
                        gather.last(h)

                    body(h, a + k - 2 * a * k)
                    return inner

                lax.fori_loop(0, 2, step, 0)
                scatter.emit_pair(h, partial)
                if after is not None:
                    after(h)
                return carry

            lax.fori_loop(0, 2, half, 0)

        def W(name, lo=0, rows=None):
            first, total = d.w[name]
            return v.wv[pl.ds(first + lo, total if rows is None else rows)]

        def gain(i):
            return gains_ref[pl.ds(i, 1)]

        sx = [Swap(x_ref.at[pl.ds(h * HR, HR)], v.xb.at[pl.ds(h * HR, HR)]) for h in range(PARTS)]
        saux, scot = Swap(aux_ref, v.aux), Swap(cot_ref, v.cotb)
        senc = Swap(e_ref, v.encf.at[z])
        weights = {name: Weight(name) for name in wnames if name != "qkv"}
        qkv3 = [Weight("qkv", i, 3) for i in range(3)]
        ag1, agd1 = (Gather(f, R, PARTS) for f in (v.h1f, v.d1f))
        ag2, ag3, agd3, agd2 = (PairGather(f) for f in (v.h2f, v.h3f, v.d3f, v.d2f))
        agenc = Gather(v.encf, E, 1)
        rs1, rs2, rs3, rs4, rs5 = (Scatter(v.pb, v.sb, v.rb) for _ in range(5))
        rso = Scatter(v.opb, v.osb, v.orb)
        rse = Scatter(v.epb, v.esb, v.erb)
        out_lo, out_eg = Swap(v.lov, lo_ref), Swap(v.egv, eg_ref)
        out_ig = [Swap(v.igv.at[pl.ds(h * HR, HR)], ig_ref.at[pl.ds(h * HR, HR)]) for h in range(PARTS)]

        class Reduce:
            def __init__(self, name):
                self.base, self.rows, self.loc, self.land = d.groups[name]
                self.sl = sl = self.rows // d.nd
                self.tile = 96 if sl % 96 == 0 else sl
                at = lambda f: pl.ds(pl.multiple_of(self.base + f * sl, 16), sl)
                here = pl.ds(self.land, sl)
                self.own = at(dl)
                self.to = [
                    Xfer(v.gsend.at[at(f)], v.grecv.at[k, here], peer)
                    for k, (f, peer) in enumerate(zip(flips[1:], peers[1:]))
                ]
                self.zx = Xfer(v.gsend.at[self.own], v.gz.at[here], z2)
                self.keep = Local(v.gfo.at[here], gout_ref.at[self.own])
                self.spread = [Xfer(v.gfo.at[here], gout_ref.at[self.own], peer) for peer in peers[1:]]
                self.core = [Xfer(v.gfo.at[here], gout_ref.at[self.own], sib)] + [
                    Xfer(gout_ref.at[at(f)], gout_ref.at[at(f)], sib) for f in flips[1:]
                ]

            def tiles(self, rows, body):
                def step(i, carry):
                    body(pl.multiple_of(i * self.tile, 16))
                    return carry

                lax.fori_loop(0, rows // self.tile, step, 0)

            def send(self):
                def cast(r):
                    v.gsend[pl.ds(self.base + r, self.tile)] = v.gf[pl.ds(self.loc + r, self.tile)].astype(BF)

                self.tiles(self.rows, cast)
                for x in self.to:
                    x.start()

                def keep(r):
                    v.gk[pl.ds(self.land + r, self.tile)] = v.gf[
                        pl.ds(self.loc + pl.multiple_of(dl * self.sl, 16) + r, self.tile)
                    ]

                self.tiles(self.sl, keep)

            def combine(self):
                for x in self.to:
                    x.recv()

                def add(r):
                    total = v.gk[pl.ds(self.land + r, self.tile)]
                    for k in range(d.nd - 1):
                        total = total + v.grecv[k, pl.ds(self.land + r, self.tile)].astype(F32)
                    v.gk[pl.ds(self.land + r, self.tile)] = total
                    v.gsend[pl.ds(pl.multiple_of(self.base + dl * self.sl, 16) + r, self.tile)] = total.astype(BF)

                self.tiles(self.sl, add)
                pl.when(is_sw)(self.zx.start)

            def finish(self):
                @pl.when(not_sw)
                def _():
                    self.zx.recv()

                    def add(r):
                        rows = pl.ds(self.land + r, self.tile)
                        v.gfo[rows] = (v.gk[rows] + v.gz[rows].astype(F32)).astype(BF)

                    self.tiles(self.sl, add)
                    self.keep.start()
                    for x in self.spread:
                        x.start()
                    self.core[0].start()

            def relay(self):
                @pl.when(not_sw)
                def _():
                    for x, y in zip(self.spread, self.core[1:]):
                        x.recv()
                        y.start()

            def done(self):
                for x in self.to:
                    x.sent()

                @pl.when(is_sw)
                def _():
                    self.zx.sent()
                    for x in self.core:
                        x.recv()

                @pl.when(not_sw)
                def _():
                    self.keep.wait()
                    for x in self.spread + self.core:
                        x.sent()

        redS, redC, redG, redH = (Reduce(name) for name in "SCGH")

        bar = pltpu.get_barrier_semaphore()
        for dev in [sib, zp, z2, z3] + peers[1:]:
            pl.semaphore_signal(bar, inc=1, device_id={"dp": dev[0], "mp": dev[1]}, device_id_type=MESH)

        @pl.when(is_sw)
        def _():
            pl.semaphore_signal(bar, inc=1, device_id={"dp": mate[0], "mp": mate[1]}, device_id_type=MESH)

        pl.semaphore_wait(bar, 3 + d.nd + sw)

        for x in sx:
            x.start()
        saux.start()
        for x in qkv3:
            x.start()

        for h in range(PARTS):
            sx[h].wait()
            rows = pl.ds(h * HR, HR)
            v.h1f[t, rows] = norm_fwd(v.xb[rows].astype(F32), gain(0))
            ag1.send(h)
        weights["so"].start()
        senc.start()
        for name in ("ckv", "cq", "co"):
            weights[name].start()
        for x in qkv3:
            x.forward()
        saux.wait()

        row16 = lax.broadcasted_iota(jnp.int32, (PADH, R), 0)
        ones_row = jnp.where(row16 == 0, 1.0, 0.0).astype(BF)

        def mask_rows(row, b):
            line = v.aux[pl.ds(row, 1), pl.ds(b * R, R)]
            return jnp.where(row16 == 0, jnp.broadcast_to(line, (PADH, R)), 0.0).astype(BF)

        for b in range(4):
            for h in range(nh):
                v.qa[b, h, pl.ds(hd, PADH)] = ones_row
                v.q2a[b // 2, b % 2, h, pl.ds(hd, PADH)] = ones_row
                v.ka[b, h, pl.ds(hd, PADH)] = mask_rows(0, b)
        for b in range(d.ne):
            for h in range(nh):
                v.k2a[b, h, pl.ds(hd, PADH)] = mask_rows(1, b)
        for h in range(nh):
            for i in range(2):
                line = v.aux[pl.ds(2 + h, 1), pl.ds(i * 2 * R, 2 * R)]
                v.bias[h, i] = pltpu.roll(jnp.broadcast_to(line, (R, 2 * R)), 0, 1, stride=1, stride_axis=0)[:, :R]
            v.bias[h, 2] = jnp.broadcast_to(v.aux[pl.ds(2 + nh + h, 1), pl.ds(0, R)], (R, R))

        @pl.when(is_sw)
        def _():
            ag1.near()
            ag1.far()

        for x in qkv3:
            x.wait()

        def project_self(b):
            qkv = dot_nt(W("qkv"), v.h1f[b]).astype(BF)
            for h in range(nh):
                v.qa[b, h, pl.ds(0, hd)] = qkv[h * hd : (h + 1) * hd]
                v.ka[b, h, pl.ds(0, hd)] = qkv[hc + h * hd : hc + (h + 1) * hd]
            v.vT[b] = qkv[2 * hc :]

        def project_step(k, carry):
            pl.when((k == 1) & not_sw)(ag1.near)
            pl.when((k == 2) & not_sw)(ag1.far)
            pl.when(k == 3)(ag1.last)
            pl.when(k == 2)(weights["so"].forward)
            project_self(blk_ag(k))
            return carry

        lax.fori_loop(0, 4, project_step, 0)
        senc.wait()
        agenc.send(0)

        def feat(h):
            return pl.ds(h * hd, hd)

        def attend_self(b):
            qs = [v.qa[b, h] for h in range(nh)]

            def block(j, state):
                out = []
                for h in range(nh):
                    m, total, acc = state[h]
                    s = dot_tn(v.ka[j, h], qs[h]) + v.bias[h, jnp.minimum(b - j, 2)]
                    new = jnp.maximum(m, jnp.max(s, axis=0, keepdims=True))
                    p = jnp.exp(s - new)
                    scale = jnp.exp(m - new)
                    total = total * scale + jnp.sum(p, axis=0, keepdims=True)
                    out.append((new, total, acc * scale + dot_nn(v.vT[j, feat(h)], p.astype(BF))))
                return tuple(out)

            first = (jnp.full((1, R), -1e30, F32), jnp.zeros((1, R), F32), jnp.zeros((hd, R), F32))
            state = lax.fori_loop(0, b + 1, block, (first,) * nh)
            for h in range(nh):
                m, total, acc = state[h]
                v.o1[b, feat(h)] = (acc / total).astype(BF)
                v.lse1[b, pl.ds(h, 1)] = m + jnp.log(total)

        def attend_cross(i, j):
            for h in range(nh):
                q = v.q2a[i, j, h]
                s = [dot_tn(v.k2a[e, h], q) for e in range(d.ne)]
                m = jnp.max(s[0], axis=0, keepdims=True)
                for part in s[1:]:
                    m = jnp.maximum(m, jnp.max(part, axis=0, keepdims=True))
                p = [jnp.exp(part - m) for part in s]
                total = sum(jnp.sum(part, axis=0, keepdims=True) for part in p)
                acc = sum(dot_nn(v.v2T[e, feat(h)], part.astype(BF)) for e, part in enumerate(p))
                v.o2[i, j, feat(h)] = (acc / total).astype(BF)
                v.lse2[i, j, pl.ds(h, 1)] = m + jnp.log(total)

        def tile_back(h, q, k, vals, da, inner, logsum, bias):
            s = dot_tn(k, q)
            if bias is not None:
                s = s + bias
            p = jnp.exp(s - logsum)
            ds = p * (dot_tn(vals, da) - inner)
            return p.astype(BF), ds, ds.astype(BF)

        def head_back(h, q, out, lse):
            da = v.da[feat(h)]
            inner = jnp.sum(da.astype(F32) * out.astype(F32), axis=0, keepdims=True)
            return q, da, inner, lse

        def attend_self_back(b):
            heads = [head_back(h, v.qa[b, h], v.o1[b, feat(h)], v.lse1[b, pl.ds(h, 1)]) for h in range(nh)]

            def block(j, dqs):
                kind = jnp.minimum(b - j, 2)
                out = []
                for h in range(nh):
                    q, da, inner, logsum = heads[h]
                    k = v.ka[j, h]
                    p, ds, low = tile_back(h, q, k, v.vT[j, feat(h)], da, inner, logsum, v.bias[h, kind])
                    v.dka[j, h] += dot_nt(q, low)
                    v.dva[j, feat(h)] += dot_nt(da, p)
                    v.dsacc[h, kind] += ds
                    out.append(dqs[h] + dot_nn(k, low))
                return tuple(out)

            dqs = lax.fori_loop(0, b + 1, block, (jnp.zeros((ha, R), F32),) * nh)
            for h in range(nh):
                v.dqkvT[b, feat(h)] = dqs[h][:hd].astype(BF)

        def attend_cross_back(i, j):
            for h in range(nh):
                q, da, inner, logsum = head_back(h, v.q2a[i, j, h], v.o2[i, j, feat(h)], v.lse2[i, j, pl.ds(h, 1)])
                dq = jnp.zeros((ha, R), F32)
                for e in range(d.ne):
                    k = v.k2a[e, h]
                    p, ds, low = tile_back(h, q, k, v.v2T[e, feat(h)], da, inner, logsum, None)
                    v.dka[e, h] += dot_nt(q, low)
                    v.dva[e, feat(h)] += dot_nt(da, p)
                    dq = dq + dot_nn(k, low)
                v.dq2T[i, j, feat(h)] = dq[:hd].astype(BF)

        def self_forward(k, carry):
            b = blk_rs(k)
            attend_self(b)
            pl.when(k == 0)(weights["so"].wait)
            v.pb[...] = dot_tn(v.o1[b], W("so"))
            rs1.emit(k)
            pl.when(k == 1)(scot.start)
            pl.when(k == 1)(agenc.near)
            pl.when(k == 1)(agenc.far)
            for name in ("ckv", "cq", "co"):
                pl.when(k == 2)(weights[name].forward)
            return carry

        lax.fori_loop(0, 4, self_forward, 0)
        agenc.last()
        weights["ckv"].wait()
        per = R // E
        for b in range(4):
            lanes = pl.ds((b % per) * E, E)
            kv = dot_nt(W("ckv"), v.encf[b]).astype(BF)
            for h in range(nh):
                v.k2a[b // per, h, pl.ds(0, hd), lanes] = kv[h * hd : (h + 1) * hd]
            v.v2T[b // per, :, lanes] = kv[hc:]

        def fin1(h, rows, total):
            x1 = v.xb[rows].astype(F32) + total
            v.x1[rows] = x1
            v.h2f[h, a, pl.ds(pl.multiple_of(c * HR, HR), HR)] = norm_fwd(x1, gain(1))
            ag2.send(h)

        for h in range(2):
            rs1.finish(h, fin1)
        for name in ("gu", "fo"):
            weights[name].start()

        weights["cq"].wait()
        weights["co"].wait()

        def cross_block(i, j):
            q = dot_nt(W("cq"), v.h2f[i, j]).astype(BF)
            for h in range(nh):
                v.q2a[i, j, h, pl.ds(0, hd)] = q[h * hd : (h + 1) * hd]
            attend_cross(i, j)

        def send_cot(h):
            pl.when(h == 0)(scot.wait)
            rows = pl.ds(pl.multiple_of(h * HR, HR), HR)
            v.d3f[h, a, pl.ds(pl.multiple_of(c * HR, HR), HR)] = v.cotb[rows]
            agd3.send(h)

        rs1.sent()
        halves(ag2, cross_block, rs2, lambda i, j: dot_tn(v.o2[i, j], W("co")), send_cot)
        for name in ("gu", "fo"):
            weights[name].forward()

        def fin2(h, rows, total):
            x2 = v.x1[rows] + total
            v.x2[rows] = x2
            v.h3f[h, a, pl.ds(pl.multiple_of(c * HR, HR), HR)] = norm_fwd(x2, gain(2))
            ag3.send(h)

        for h in range(2):
            rs2.finish(h, fin2)
        for h in range(2):
            agd3.near(h)
            agd3.pass_on(h)
        for h in range(2):
            agd3.last(h)
        for name in ("gu", "fo"):
            weights[name].wait()

        fc = 64

        def hidden_block(i, j):
            rows = v.h3f[i, j]
            v.gus[pl.ds(0, F)] = dot_nt(W("gu", 0, F), rows)
            v.gus[pl.ds(F, F)] = dot_nt(W("gu", F, F), rows)
            v.gus[pl.ds(2 * F, F)] = dot_nt(W("fo"), v.d3f[i, j])

            def chunk(n, carry):
                r = pl.multiple_of(n * fc, fc)
                gate, up, dact = (v.gus[pl.ds(m * F + r, fc)] for m in range(3))
                sq = gate * gate
                th = jnp.tanh(gate * (GELU_C + (GELU_C * 0.044715) * sq))
                half = 0.5 + 0.5 * th
                gelu = gate * half
                slope = half + gate * (0.5 - 0.5 * th * th) * (GELU_C + (3.0 * GELU_C * 0.044715) * sq)
                v.actT[i, j, pl.ds(r, fc)] = (gelu * up).astype(BF)
                v.dguT[i, j, pl.ds(r, fc)] = (dact * up * slope).astype(BF)
                v.dguT[i, j, pl.ds(F + r, fc)] = (dact * gelu).astype(BF)
                return carry

            lax.fori_loop(0, F // fc, chunk, 0)

        rs2.sent()
        halves(ag3, hidden_block, rs3, lambda i, j: dot_tn(v.dguT[i, j], W("gu")))

        def grads(at, lhs, rows, rhs, tile):
            spots = [(b,) for b in range(4)] if len(lhs.shape) == 3 else [(b // 2, b % 2) for b in range(4)]

            def step(i, carry):
                r = pl.multiple_of(i * tile, 64)
                total = None
                for spot in spots:
                    part = dot_nn(lhs[spot + (pl.ds(r, tile),)], rhs[spot])
                    total = part if total is None else total + part
                v.gf[pl.ds(at + r, tile)] = total
                return carry

            lax.fori_loop(0, rows // tile, step, 0)

        def loc(name, group):
            base, _, at, _ = d.groups[group]
            return d.w[name][0] - base + at

        def add_gain(i, h, part):
            if h == 0:
                v.smc[pl.ds(i, 1)] = part
            else:
                v.smc[pl.ds(i, 1)] += part

        v.smc[...] = jnp.zeros(v.smc.shape, F32)

        def fin3(h, rows, total):
            grad, part = norm_bwd(v.x2[rows], gain(2), total)
            add_gain(2, h, part)
            g2 = v.cotb[rows].astype(F32) + grad
            v.gb[rows] = g2
            v.d2f[h, a, pl.ds(pl.multiple_of(c * HR, HR), HR)] = g2.astype(BF)
            agd2.send(h)

        rs3.finish(0, fin3)
        grads(loc("gu", "G"), v.dguT, 2 * F, v.h3f, 256)
        redG.send()
        rs3.finish(1, fin3)
        grads(loc("fo", "H"), v.actT, F, v.d3f, 256)
        redH.send()

        v.dka[...] = jnp.zeros(v.dka.shape, F32)
        v.dva[...] = jnp.zeros(v.dva.shape, F32)

        def cross_back_block(i, j):
            v.da[...] = dot_nt(W("co"), v.d2f[i, j]).astype(BF)
            attend_cross_back(i, j)

        rs3.sent()
        halves(agd2, cross_back_block, rs4, lambda i, j: dot_tn(v.dq2T[i, j], W("cq")))

        def fin4(h, rows, total):
            grad, part = norm_bwd(v.x1[rows], gain(1), total)
            add_gain(1, h, part)
            g1 = v.gb[rows] + grad
            v.gb[rows] = g1
            v.d1f[t, rows] = g1.astype(BF)
            agd1.send(h)

        rs4.finish(0, fin4)
        for b in range(4):
            lanes = pl.ds((b % per) * E, E)
            for h in range(nh):
                v.dkv2T[b, pl.ds(h * hd, hd)] = v.dka[b // per, h, pl.ds(0, hd), lanes].astype(BF)
            v.dkv2T[b, pl.ds(hc, hc)] = v.dva[b // per, :, lanes].astype(BF)
        rs4.finish(1, fin4)
        redG.combine()
        grads(loc("cq", "C"), v.dq2T, hc, v.h2f, hc)
        grads(loc("co", "C"), v.o2, hc, v.d2f, hc)
        grads(loc("ckv", "C"), v.dkv2T, 2 * hc, v.encf, hc)
        redC.send()

        def hidden_out(h, carry):
            rso.emit_pair(h, lambda i, j: dot_tn(v.actT[i, j], W("fo")), kick=False)
            return carry

        lax.fori_loop(0, 2, hidden_out, 0)

        v.dka[...] = jnp.zeros(v.dka.shape, F32)
        v.dva[...] = jnp.zeros(v.dva.shape, F32)
        v.dsacc[...] = jnp.zeros(v.dsacc.shape, F32)

        def self_back(k, carry):
            b = blk_ag(k)
            agd1.arrive(k)
            pl.when(k == 1)(rso.kick)
            pl.when(k == 2)(redH.combine)
            pl.when(k == 3)(redG.finish)
            v.da[...] = dot_nt(W("so"), v.d1f[b]).astype(BF)
            attend_self_back(b)
            return carry

        lax.fori_loop(0, 4, self_back, 0)

        for b in range(4):
            for h in range(nh):
                v.dqkvT[b, pl.ds(hc + h * hd, hd)] = v.dka[b, h, pl.ds(0, hd)].astype(BF)
            v.dqkvT[b, pl.ds(2 * hc, hc)] = v.dva[b].astype(BF)
        grads(loc("qkv", "S"), v.dqkvT, 3 * hc, v.h1f, hc)
        grads(loc("so", "S"), v.o1, hc, v.d1f, hc)
        redS.send()

        def self_qkv_part(b):
            v.pb[...] = dot_tn(v.dqkvT[b], W("qkv"))

        redC.combine()
        rs4.sent()
        rs5.loop(self_qkv_part)
        redH.finish()

        def fin_out(h, rows, total):
            v.lov[rows] = (v.x2[rows] + total).astype(BF)

        for h in range(2):
            rso.finish(h, fin_out)
        out_lo.start()

        def enc_part(b):
            v.epb[...] = dot_tn(v.dkv2T[b], W("ckv"))

        rse.loop(enc_part)

        iota0 = lax.broadcasted_iota(jnp.int32, (R, R), 0)
        iota1 = lax.broadcasted_iota(jnp.int32, (R, R), 1)
        flip = (iota0 + iota1 == R - 1).astype(F32)

        def diagonals(h, i):
            turned = lax.dot_general(
                flip, v.dsacc[h, i], (((1,), (0,)), ((), ())), precision=lax.Precision.HIGHEST, preferred_element_type=F32
            )
            wide = jnp.concatenate([turned, jnp.zeros((R, R), F32)], axis=1)
            return jnp.sum(pltpu.roll(wide, 0, 1, stride=1, stride_axis=0), axis=0, keepdims=True)

        lane = lax.broadcasted_iota(jnp.int32, (1, 2 * R), 1)
        for h in range(nh):
            near, off = diagonals(h, 0), diagonals(h, 1)
            far = jnp.sum(jnp.sum(v.dsacc[h, 2], axis=0, keepdims=True), axis=1, keepdims=True)
            off = off + jnp.where(lane == 2 * R - 1, far, 0.0)
            line = jnp.concatenate([pltpu.roll(near, R + 1, 1)[:, :R], off], axis=1)
            for q in range(4):
                v.smc[pl.ds(3 + q * nh + h, 1), pl.ds(0, 3 * R)] = jnp.where(t == q, line, 0.0)

        def fin5(h, rows, total):
            grad, part = norm_bwd(v.xb[rows].astype(F32), gain(0), total)
            add_gain(0, h, part)
            v.igv[rows] = (v.gb[rows] + grad).astype(BF)

        for h in range(2):
            rs5.finish(h, fin5)

        plane = peers[1:]
        lines = [zp, z2, z3]
        v.sms[0] = v.smc[...]
        first = [Xfer(v.sms.at[0], v.smr.at[i], dev) for i, dev in enumerate(lines)]
        second = [Xfer(v.sms.at[1], v.smr.at[3 + i], dev) for i, dev in enumerate(plane)]
        third = [Xfer(v.sms.at[2], v.smr.at[6], sib)]
        for x in first:
            x.start()
        out_ig[0].start()
        redC.finish()
        redS.combine()
        out_ig[1].start()
        for x in first:
            x.recv()
        v.sms[1] = (v.sms[0] + v.smr[0]) + (v.smr[1] + v.smr[2])
        for x in second:
            x.start()

        def fin_enc(h, rows, total):
            v.egv[rows] = total.astype(BF)

        rse.finish(0, fin_enc)
        out_eg.start()
        for x in second:
            x.recv()
        if len(plane) == 3:
            v.sms[2] = (v.sms[1] + v.smr[3]) + (v.smr[4] + v.smr[5])
        elif len(plane) == 1:
            v.sms[2] = v.sms[1] + v.smr[3]
        else:
            v.sms[2] = v.sms[1]
        third[0].start()
        redS.finish()
        third[0].recv()
        sm_ref[...] = v.sms[2] + v.smr[6]
        redG.relay()
        redH.relay()
        redC.relay()
        redS.relay()

        for x in first + second + third:
            x.sent()
        for x in (ag1, ag2, ag3, agd1, agd2, agd3, agenc, rs5, rso, rse):
            x.sent()
        for x in [saux, scot, senc] + sx:
            x.sent()
        for x in list(weights.values()) + qkv3:
            x.sent()
        for x in [out_lo, out_eg] + out_ig:
            x.wait()
            x.sent()
        for r in (redG, redH, redC, redS):
            r.done()

    return kernel


def local_fn(mesh):
    def local(x_in, enc_in, cotangent, dec_len, enc_len, self_qkv, self_out, cross_q, cross_kv, cross_out, ff_in, ff_out, gains, table):
        d = make_dims(mesh, x_in, enc_in, self_qkv, ff_in, table)
        R, D, hc, nh, F = d.R, d.D, d.hc, d.nh, d.F
        hbm = pl.BlockSpec(memory_space=pl.ANY)
        vmem = pl.BlockSpec(memory_space=pltpu.VMEM)
        ws = {
            "qkv": jnp.transpose(self_qkv, (1, 2, 0)).reshape(3 * hc, D),
            "so": self_out,
            "cq": jnp.transpose(cross_q),
            "ckv": jnp.transpose(cross_kv, (1, 2, 0)).reshape(2 * hc, D),
            "co": cross_out,
            "gu": jnp.transpose(ff_in, (1, 2, 0)).reshape(2 * F, D),
            "fo": ff_out,
        }
        lane = jnp.arange(4 * R, dtype=jnp.int32)
        dist = jnp.where(lane < 2 * R, lane, jnp.where(lane < 3 * R, lane - R, lane - 3 * R))
        onehot = (bucket_index(dist)[:, None] == jnp.arange(NB)[None, :]).astype(BF)
        lines = jnp.einsum("vh,lv->hl", table, onehot, preferred_element_type=F32)
        lines = jnp.where((lane >= R) & (lane < 2 * R), MASK_FILL, lines)
        pos = lane[None, :]
        aux = jnp.concatenate(
            [
                jnp.where(pos < dec_len[0], 0.0, MASK_FILL),
                jnp.where(pos < enc_len[0], 0.0, MASK_FILL),
                lines,
                jnp.broadcast_to(table[NB - 1].astype(F32)[:, None], (nh, 4 * R)),
                jnp.zeros((d.axr - 2 - 2 * nh, 4 * R), F32),
            ],
            axis=0,
        )
        gains_f = gains.astype(F32)
        outs = pl.pallas_call(
            build_kernel(d),
            out_shape=(
                jax.ShapeDtypeStruct((R, D), BF),
                jax.ShapeDtypeStruct((R, D), BF),
                jax.ShapeDtypeStruct((d.E, D), BF),
                jax.ShapeDtypeStruct((d.rows, D), BF),
                jax.ShapeDtypeStruct((d.small, D), F32),
            ),
            in_specs=[hbm, hbm, hbm, hbm, vmem] + [hbm] * len(d.w),
            out_specs=(hbm, hbm, hbm, hbm, vmem),
            scratch_shapes=[pltpu.VMEM(shape, dtype) for _, shape, dtype in scratch_list(d)]
            + [pltpu.SemaphoreType.DMA((SEMS,))] * 3,
            compiler_params=pltpu.CompilerParams(collective_id=0, has_side_effects=True, vmem_limit_bytes=63 << 20),
        )(x_in, enc_in, cotangent, aux, gains_f, *[ws[name] for name in d.w])
        lo, ig, eg, gw, sm = outs
        others = d.ndp // (2 * d.nd)
        if others > 1:
            gw, sm = lax.psum((gw.astype(F32), sm), "dp")
            gw, sm = gw * (1.0 / (2 * d.nd)), sm * (1.0 / (2 * d.nd))
        g = {name: gw[first : first + rows].astype(F32) for name, (first, rows) in d.w.items()}
        mine = lax.dynamic_slice_in_dim(sm, 3 + lax.axis_index("mp") * nh, nh, axis=0)
        col = jnp.arange(D)
        dist = jnp.where(col < R, col, jnp.where(col < 3 * R - 1, col - R + 1, 4 * R))
        pick = (bucket_index(dist)[:, None] == jnp.arange(NB)[None, :]).astype(F32)
        table_grad = jnp.einsum("hl,lv->vh", mine, pick, precision=lax.Precision.HIGHEST, preferred_element_type=F32)
        return (
            lo,
            ig.astype(F32),
            eg.astype(F32),
            jnp.transpose(g["qkv"].reshape(3, hc, D), (2, 0, 1)),
            g["so"],
            jnp.transpose(g["cq"]),
            jnp.transpose(g["ckv"].reshape(2, hc, D), (2, 0, 1)),
            g["co"],
            jnp.transpose(g["gu"].reshape(2, F, D), (2, 0, 1)),
            g["fo"],
            sm[:3],
            table_grad,
        )

    return local


def solution(mesh):
    rows = P(("dp", "mp"), None)
    in_specs = (
        rows, rows, rows, P("dp"), P("dp"), P(None, None, "mp"), P("mp", None), P(None, "mp"), P(None, None, "mp"),
        P("mp", None), P(None, None, "mp"), P("mp", None), P(), P(None, "mp"),
    )
    out_specs = (
        rows, rows, rows, P(None, None, "mp"), P("mp", None), P(None, "mp"), P(None, None, "mp"), P("mp", None),
        P(None, None, "mp"), P("mp", None), P(), P(None, "mp"),
    )
    return jax.shard_map(local_fn(mesh), mesh=mesh, in_specs=in_specs, out_specs=out_specs, check_vma=False)
```

```python
import math

import jax
import jax.numpy as jnp
from jax import lax
from jax.experimental import pallas as pl
from jax.experimental.pallas import tpu as pltpu
from jax.sharding import PartitionSpec as P

NB = 32
MAXD = 128
NORM_EPS = 1e-06
MASK_FILL = -1000000000.0
MESH = pl.DeviceIdType.MESH
BF = jnp.bfloat16
F32 = jnp.float32
PARTS = 2
PADH = 16
GELU_C = math.sqrt(2.0 / math.pi)
SEMS = 256


def bucket_index(distance):
    half_count = NB // 2
    clipped = jnp.maximum(distance, 0)
    bucket_ids = jnp.minimum(clipped, half_count)
    for level_pos in range(1, half_count):
        threshold = math.ceil(half_count * (MAXD / half_count) ** (level_pos / half_count))
        bucket_ids = bucket_ids + (clipped >= threshold).astype(jnp.int32)
    return bucket_ids


def dot_nn(a, b):
    return lax.dot_general(a, b, (((1,), (0,)), ((), ())), preferred_element_type=F32)


def dot_nt(a, b):
    return lax.dot_general(a, b, (((1,), (1,)), ((), ())), preferred_element_type=F32)


def dot_tn(a, b):
    return lax.dot_general(a, b, (((0,), (0,)), ((), ())), preferred_element_type=F32)


def norm_fwd(v, g):
    inv = lax.rsqrt(jnp.mean(v * v, axis=-1, keepdims=True) + NORM_EPS)
    return (v * inv * g).astype(BF)


def norm_bwd(v, g, u):
    inv = lax.rsqrt(jnp.mean(v * v, axis=-1, keepdims=True) + NORM_EPS)
    gu = u * g
    mean = jnp.mean(gu * v, axis=-1, keepdims=True)
    grad = inv * gu - v * (inv * inv * inv * mean)
    gain = jnp.sum(u * v * inv, axis=0, keepdims=True)
    return grad, gain


class Dims:
    pass


def make_dims(mesh, x_in, enc_in, self_qkv, ff_in, table):
    d = Dims()
    d.ndp, d.nmp = mesh.shape["dp"], mesh.shape["mp"]
    d.nd = min(4, d.ndp // 2)
    d.R, d.D = x_in.shape
    d.E = enc_in.shape[0]
    d.nh = table.shape[1]
    d.hc = self_qkv.shape[2]
    d.hd = d.hc // d.nh
    d.F = ff_in.shape[2]
    d.ha = d.hd + PADH
    d.ne = 4 * d.E // d.R
    d.axr = -(-(2 + 2 * d.nh) // 8) * 8
    hc, F = d.hc, d.F
    names = (("gu", 2 * F), ("fo", F), ("qkv", 3 * hc), ("so", hc), ("ckv", 2 * hc), ("cq", hc), ("co", hc))
    d.w, at = {}, 0
    for name, rows in names:
        d.w[name] = (at, rows)
        at += rows
    d.rows = at
    s, c = 3 * hc, 4 * hc
    d.groups = {}
    land = 0
    for name, base, rows in (("G", 0, 2 * F), ("H", 2 * F, F), ("S", 3 * F, s), ("O", 3 * F + s, hc), ("C", 3 * F + s + hc, c)):
        d.groups[name] = (base, rows, 0, land)
        land += rows // d.nd
    d.land = land
    d.locrows = max(s, c, 2 * F)
    d.small = -(-(3 + 4 * d.nh) // 8) * 8
    return d


def scratch_list(d):
    R, D, hc, nh, hd, ha, F, E = d.R, d.D, d.hc, d.nh, d.hd, d.ha, d.F, d.E
    full = ((4, R, D), BF)
    pair = ((2, 2, R, D), BF)
    HR = R // 2
    return [
        ("xb", (R, D), BF), ("cotb", (R, D), BF), ("aux", (d.axr, 4 * R), F32), ("aux0", (d.axr, 4 * R), F32), ("ffb", (2, 1024, 128), BF), ("ffs", (1024, 128), F32), ("wv", (d.rows, D), BF),
        ("h1f",) + full, ("h2f",) + pair, ("h3f",) + pair, ("d3f",) + pair, ("d2f",) + pair, ("d1f",) + full,
        ("encf", (4, E, D), BF),
        ("qa", (4, nh, ha, R), BF), ("ka", (4, nh, ha, R), BF), ("vT", (4, hc, R), BF), ("o1", (4, hc, R), BF),
        ("q2a", (2, 2, nh, ha, R), BF), ("k2a", (d.ne, nh, ha, R), BF), ("v2T", (d.ne, hc, R), BF), ("o2", (2, 2, hc, R), BF),
        ("lse1", (4, 8, R), F32), ("lse2", (2, 2, 8, R), F32),
        ("bias", (nh, 3, R, R), F32), ("dsacc", (nh, 3, R, R), F32),
        ("x1", (R, D), F32), ("x2", (R, D), F32), ("gb", (R, D), F32),
        ("pb", (R, D), F32), ("pf", (R, D), F32), ("sb", (2, 3, HR, D), BF), ("rb", (2, 3, HR, D), BF),
        ("opb", (R, D), F32), ("osb", (2, 3, HR, D), BF), ("orb", (2, 3, HR, D), BF), ("lov", (R, D), BF), ("igv", (R, D), BF),
        ("epb", (E, D), F32), ("esb", (1, 3, E, D), BF), ("erb", (1, 3, E, D), BF), ("egv", (E, D), BF),
        ("actT", (2, 2, F, R), BF), ("dguT", (2, 2, 2 * F, R), BF), ("gus", (3 * F, R), F32),
        ("da", (hc, R), BF), ("dqkvT", (4, 3 * hc, R), BF), ("dq2T", (2, 2, hc, R), BF), ("dkv2T", (4, 2 * hc, E), BF),
        ("dka", (4, nh, ha, R), F32), ("dva", (4, hc, R), F32),
        ("gf", (d.locrows, D), F32), ("gsend", (d.rows, D), BF), ("grecv", (max(d.nd - 1, 1), d.land, D), BF),
        ("gz", (d.land, D), BF), ("gk", (d.land, D), F32), ("gfo", (d.land, D), BF),
        ("smc", (d.small, D), F32), ("sms", (4, d.small, D), F32), ("smr", (7, d.small, D), F32),
    ]


def build_kernel(d):
    R, D, hc, nh, hd, ha, F, E = d.R, d.D, d.hc, d.nh, d.hd, d.ha, d.F, d.E
    names = [item[0] for item in scratch_list(d)]
    wnames = list(d.w)
    HR = R // PARTS

    def kernel(*refs):
        x_ref, e_ref, cot_ref, tab_ref, dlen_ref, elen_ref, gains_ref = refs[:7]
        w_refs = dict(zip(wnames, refs[7 : 7 + len(wnames)]))
        lo_ref, ig_ref, eg_ref, gout_ref, sm_ref = refs[7 + len(wnames) : 12 + len(wnames)]
        tail = refs[12 + len(wnames) :]
        v = Dims()
        for name, ref in zip(names, tail):
            setattr(v, name, ref)
        ss, rs, ls = tail[len(names) :]
        ff_ref = w_refs["gu"]
        w_refs["gu"] = v.gsend.at[pl.ds(0, 2 * F)]

        dp, z = lax.axis_index("dp"), lax.axis_index("mp")
        c, chip = dp % 2, dp // 2
        a, u = z % 2, z // 2
        t = a + 2 * c
        sw = c + u - 2 * c * u
        dl = chip % d.nd
        base_dp = (chip - dl) * 2
        sib = (dp + 1 - 2 * c, z)
        zp = (dp, z + 1 - 2 * a)
        z2 = (dp, z + 2 - 4 * u)
        mate = (2 * chip + u, a + 2 * c)
        d0, d1 = dl % 2, dl // 2
        flips = [dl, dl + 1 - 2 * d0, dl + 2 - 4 * d1, 3 - dl][: d.nd]
        peers = [(base_dp + 2 * f + c, z) for f in flips]
        is_sw, not_sw = sw == 1, sw == 0

        count = [0]

        def new_id():
            count[0] += 1
            assert count[0] <= SEMS
            return count[0] - 1

        class Xfer:
            def __init__(self, src, dst, dev, i=None):
                self.i, self.src, self.dst, self.dev = new_id() if i is None else i, src, dst, dev

            def desc(self):
                return pltpu.make_async_remote_copy(
                    src_ref=self.src, dst_ref=self.dst, send_sem=ss.at[self.i], recv_sem=rs.at[self.i],
                    device_id={"dp": self.dev[0], "mp": self.dev[1]}, device_id_type=MESH,
                )

            def start(self):
                self.desc().start()

            def recv(self):
                self.desc().wait_recv()

            def sent(self):
                self.desc().wait_send()

        class Local:
            def __init__(self, src, dst):
                self.i, self.src, self.dst = new_id(), src, dst

            def desc(self):
                return pltpu.make_async_copy(self.src, self.dst, ls.at[self.i])

            def start(self):
                self.desc().start()

            def wait(self):
                self.desc().wait()

        class Swap:
            def __init__(self, src, dst):
                self.far, self.near = Xfer(src, dst, mate), Local(src, dst)

            def start(self):
                pl.when(is_sw)(self.far.start)
                pl.when(not_sw)(self.near.start)

            def wait(self):
                pl.when(is_sw)(self.far.recv)
                pl.when(not_sw)(self.near.wait)

            def sent(self):
                pl.when(is_sw)(self.far.sent)

        class Weight:
            def __init__(self, name, piece=0, pieces=1):
                first, rows = d.w[name]
                rows = rows // pieces
                at = piece * rows
                first += at
                sl = rows // d.nd
                mine = pl.ds(pl.multiple_of(at + dl * sl, 16), sl)
                here = v.wv.at[pl.ds(pl.multiple_of(first + dl * sl, 16), sl)]
                self.near = Local(w_refs[name].at[pl.ds(at, rows)], v.wv.at[pl.ds(first, rows)])
                self.far = Xfer(w_refs[name].at[mine], here, mate)
                self.on = [Xfer(here, here, peer) for peer in peers[1:]]

            def start(self):
                pl.when(is_sw)(self.far.start)
                pl.when(not_sw)(self.near.start)

            def forward(self):
                @pl.when(is_sw)
                def _():
                    self.far.recv()
                    for x in self.on:
                        x.start()

            def wait(self):
                pl.when(not_sw)(self.near.wait)

                @pl.when(is_sw)
                def _():
                    for x in self.on:
                        x.recv()

            def sent(self, first=True):
                @pl.when(is_sw)
                def _():
                    if first:
                        self.far.sent()
                    for x in self.on:
                        x.sent()

        def blk_ag(k):
            k1, k2 = k % 2, k // 2
            return (a + k2 - 2 * a * k2) + 2 * (c + k1 - 2 * c * k1)

        def blk_rs(k):
            return blk_ag(3 - k)

        class Gather:
            def __init__(self, full, rows, parts):
                self.parts = parts
                n = rows // parts
                at = lambda b, h: full.at[b, pl.ds(h * n, n)]
                b_zp = (1 - a) + 2 * c
                self.z = [Xfer(at(t, h), at(t, h), zp) for h in range(parts)]
                self.c = [Xfer(at(t, h), at(t, h), sib) for h in range(parts)]
                self.f = [Xfer(at(b_zp, h), at(b_zp, h), sib) for h in range(parts)]

            def send(self, h):
                self.z[h].start()
                self.c[h].start()

            def near(self):
                for x in self.c:
                    x.recv()

            def far(self):
                for x, y in zip(self.z, self.f):
                    x.recv()
                    y.start()

            def last(self):
                for x in self.f:
                    x.recv()

            def arrive(self, k):
                pl.when(k == 1)(self.near)
                pl.when(k == 2)(self.far)
                pl.when(k == 3)(self.last)

            def sent(self):
                for x in self.z + self.c + self.f:
                    x.sent()

        class PairGather:
            def __init__(self, full):
                self.full, self.ids = full, [new_id() for _ in range(6)][0]

            def own(self, h):
                return self.full.at[h, a, pl.ds(pl.multiple_of(c * HR, HR), HR)]

            def z(self, h):
                return Xfer(self.own(h), self.own(h), zp, self.ids + h)

            def c(self, h):
                return Xfer(self.own(h), self.own(h), sib, self.ids + 2 + h)

            def f(self, h):
                there = self.full.at[h, 1 - a, pl.ds(pl.multiple_of(c * HR, HR), HR)]
                return Xfer(there, there, sib, self.ids + 4 + h)

            def send(self, h):
                self.z(h).start()
                self.c(h).start()

            def near(self, h):
                self.c(h).recv()

            def pass_on(self, h):
                self.z(h).recv()
                self.f(h).start()

            def last(self, h):
                self.f(h).recv()

            def sent(self):
                for h in range(2):
                    for x in (self.z(h), self.c(h), self.f(h)):
                        x.sent()

        class Scatter:
            def __init__(self, pb, sb, rb):
                self.pb, self.sb, self.rb = pb, sb, rb
                self.parts, self.n = sb.shape[0], sb.shape[2]
                self.ids = [new_id() for _ in range(3 * self.parts)][0]

            def rows(self, h):
                return pl.ds(h * self.n if isinstance(h, int) else pl.multiple_of(h * self.n, self.n), self.n)

            def x(self, slot, h, dev):
                return Xfer(self.sb.at[h, slot], self.rb.at[h, slot], dev, self.ids + slot * self.parts + h)

            def c0(self, h):
                return self.x(0, h, sib)

            def z(self, h):
                return self.x(1, h, zp)

            def c2(self, h):
                return self.x(2, h, sib)

            def emit(self, k, kick=True):
                @pl.when(k == 0)
                def _():
                    for h in range(self.parts):
                        self.sb[h, 0] = self.pb[self.rows(h)].astype(BF)
                        self.c0(h).start()

                @pl.when(k == 1)
                def _():
                    for h in range(self.parts):
                        self.c0(h).recv()
                        self.sb[h, 1] = (self.pb[self.rows(h)] + self.rb[h, 0].astype(F32)).astype(BF)
                        if kick:
                            self.z(h).start()

                @pl.when(k == 2)
                def _():
                    for h in range(self.parts):
                        self.sb[h, 2] = self.pb[self.rows(h)].astype(BF)
                        self.c2(h).start()

            def loop(self, partial, kick=True):
                def step(k, carry):
                    partial(blk_rs(k))
                    self.emit(k, kick)
                    return carry

                lax.fori_loop(0, 4, step, 0)

            def emit_pair(self, h, partial, kick=True):
                mine = pl.ds(pl.multiple_of(c * HR, HR), HR)
                other = pl.ds(pl.multiple_of((1 - c) * HR, HR), HR)
                v.pf[...] = partial(h, 1 - a)
                self.sb[h, 0] = v.pf[other].astype(BF)
                self.c0(h).start()
                self.sb[h, 1] = v.pf[mine].astype(BF)
                v.pf[...] = partial(h, a)
                self.sb[h, 2] = v.pf[other].astype(BF)
                self.c2(h).start()
                self.pb[self.rows(h)] = v.pf[mine]
                self.c0(h).recv()
                self.sb[h, 1] = (self.sb[h, 1].astype(F32) + self.rb[h, 0].astype(F32)).astype(BF)
                if kick:
                    self.z(h).start()

            def kick(self):
                for h in range(self.parts):
                    self.z(h).start()

            def finish(self, h, fin):
                self.c2(h).recv()
                self.z(h).recv()
                rows = self.rows(h)
                fin(h, rows, self.pb[rows] + self.rb[h, 2].astype(F32) + self.rb[h, 1].astype(F32))

            def sent(self):
                for h in range(self.parts):
                    for x in (self.c0(h), self.z(h), self.c2(h)):
                        x.sent()

        def ag_loop(gather, body):
            def step(k, carry):
                gather.arrive(k)
                body(blk_ag(k))
                return carry

            lax.fori_loop(0, 4, step, 0)

        def halves(gather, body, scatter, partial, after=None):
            def half(h, carry):
                def step(k, inner):
                    pl.when(k == 0)(lambda: gather.near(h))

                    @pl.when(k == 1)
                    def _():
                        gather.pass_on(h)
                        gather.last(h)

                    body(h, a + k - 2 * a * k)
                    return inner

                lax.fori_loop(0, 2, step, 0)
                scatter.emit_pair(h, partial)
                if after is not None:
                    after(h)
                return carry

            lax.fori_loop(0, 2, half, 0)

        def W(name, lo=0, rows=None):
            first, total = d.w[name]
            return v.wv[pl.ds(first + lo, total if rows is None else rows)]

        def gain(i):
            return gains_ref[pl.ds(i, 1)].astype(F32)

        sx = [Swap(x_ref.at[pl.ds(h * HR, HR)], v.xb.at[pl.ds(h * HR, HR)]) for h in range(PARTS)]
        saux, scot = Swap(v.aux0, v.aux), Swap(cot_ref, v.cotb)
        senc = Swap(e_ref, v.encf.at[z])
        weights = {name: Weight(name) for name in wnames if name != "qkv"}
        qkv3 = [Weight("qkv", i, 3) for i in range(3)]
        ag1, agd1 = (Gather(f, R, PARTS) for f in (v.h1f, v.d1f))
        ag2, ag3, agd3, agd2 = (PairGather(f) for f in (v.h2f, v.h3f, v.d3f, v.d2f))
        agenc = Gather(v.encf, E, 1)
        rs1, rs2, rs3, rs4, rs5 = (Scatter(v.pb, v.sb, v.rb) for _ in range(5))
        rso = Scatter(v.opb, v.osb, v.orb)
        rse = Scatter(v.epb, v.esb, v.erb)
        out_lo, out_eg = Swap(v.lov, lo_ref), Swap(v.egv, eg_ref)
        out_ig = [Swap(v.igv.at[pl.ds(h * HR, HR)], ig_ref.at[pl.ds(h * HR, HR)]) for h in range(PARTS)]

        class Reduce:
            def __init__(self, name):
                self.base, self.rows, self.loc, self.land = d.groups[name]
                self.sl = sl = self.rows // d.nd
                self.tile = 96 if sl % 96 == 0 else sl
                at = lambda f: pl.ds(pl.multiple_of(self.base + f * sl, 16), sl)
                here = pl.ds(self.land, sl)
                self.own = at(dl)
                self.to = [
                    Xfer(v.gsend.at[at(f)], v.grecv.at[k, here], peer)
                    for k, (f, peer) in enumerate(zip(flips[1:], peers[1:]))
                ]
                self.zx = Xfer(v.gsend.at[self.own], v.gz.at[here], z2)
                self.keep = Local(v.gfo.at[here], gout_ref.at[self.own])
                self.spread = [Xfer(v.gfo.at[here], gout_ref.at[self.own], peer) for peer in peers[1:]]
                self.core = [Xfer(v.gfo.at[here], gout_ref.at[self.own], sib)] + [
                    Xfer(gout_ref.at[at(f)], gout_ref.at[at(f)], sib) for f in flips[1:]
                ]

            def tiles(self, rows, body):
                def step(i, carry):
                    body(pl.multiple_of(i * self.tile, 16))
                    return carry

                lax.fori_loop(0, rows // self.tile, step, 0)

            def send(self):
                def cast(r):
                    v.gsend[pl.ds(self.base + r, self.tile)] = v.gf[pl.ds(self.loc + r, self.tile)].astype(BF)

                self.tiles(self.rows, cast)
                for x in self.to:
                    x.start()

                def keep(r):
                    v.gk[pl.ds(self.land + r, self.tile)] = v.gf[
                        pl.ds(self.loc + pl.multiple_of(dl * self.sl, 16) + r, self.tile)
                    ]

                self.tiles(self.sl, keep)

            def combine(self):
                for x in self.to:
                    x.recv()

                def add(r):
                    total = v.gk[pl.ds(self.land + r, self.tile)]
                    for k in range(d.nd - 1):
                        total = total + v.grecv[k, pl.ds(self.land + r, self.tile)].astype(F32)
                    v.gk[pl.ds(self.land + r, self.tile)] = total
                    v.gsend[pl.ds(pl.multiple_of(self.base + dl * self.sl, 16) + r, self.tile)] = total.astype(BF)

                self.tiles(self.sl, add)
                pl.when(is_sw)(self.zx.start)

            def finish(self):
                @pl.when(not_sw)
                def _():
                    self.zx.recv()

                    def add(r):
                        rows = pl.ds(self.land + r, self.tile)
                        v.gfo[rows] = (v.gk[rows] + v.gz[rows].astype(F32)).astype(BF)

                    self.tiles(self.sl, add)
                    self.keep.start()
                    for x in self.spread:
                        x.start()
                    self.core[0].start()

            def relay(self):
                @pl.when(not_sw)
                def _():
                    for x, y in zip(self.spread, self.core[1:]):
                        x.recv()
                        y.start()

            def done(self):
                for x in self.to:
                    x.sent()

                @pl.when(is_sw)
                def _():
                    self.zx.sent()
                    for x in self.core:
                        x.recv()

                @pl.when(not_sw)
                def _():
                    self.keep.wait()
                    for x in self.spread + self.core:
                        x.sent()

        redS, redO, redC, redG, redH = (Reduce(name) for name in "SOCGH")

        bar = pltpu.get_barrier_semaphore()
        for dev in [sib, zp, z2] + peers[1:]:
            pl.semaphore_signal(bar, inc=1, device_id={"dp": dev[0], "mp": dev[1]}, device_id_type=MESH)

        @pl.when(is_sw)
        def _():
            pl.semaphore_signal(bar, inc=1, device_id={"dp": mate[0], "mp": mate[1]}, device_id_type=MESH)

        pl.semaphore_wait(bar, 2 + d.nd + sw)

        for x in sx:
            x.start()
        for x in qkv3:
            x.start()
        turns = D // 128
        loads = [Local(ff_ref.at[pl.ds(i * 1024, 1024)], v.ffb.at[i % 2]) for i in range(turns)]
        loads[0].start()

        def first_norm():
            for h in range(PARTS):
                sx[h].wait()
                rows = pl.ds(h * HR, HR)
                v.h1f[t, rows] = norm_fwd(v.xb[rows].astype(F32), gain(0))
                ag1.send(h)

        pl.when(not_sw)(first_norm)

        pos = lax.broadcasted_iota(jnp.int32, (1, 4 * R), 1)
        dist = jnp.where(pos < 2 * R, pos, jnp.where(pos < 3 * R, pos - R, pos - 3 * R))
        onehot = jnp.where(lax.broadcasted_iota(jnp.int32, (NB, 4 * R), 0) == bucket_index(dist), 1.0, 0.0).astype(BF)
        lines = dot_nn(tab_ref[...], onehot)
        v.aux0[...] = jnp.zeros(v.aux0.shape, F32)
        v.aux0[pl.ds(0, 1)] = jnp.where(pos < dlen_ref[0], 0.0, MASK_FILL)
        v.aux0[pl.ds(1, 1)] = jnp.where(pos < elen_ref[0], 0.0, MASK_FILL)
        v.aux0[pl.ds(2, nh)] = jnp.where((pos >= R) & (pos < 2 * R), MASK_FILL, lines)
        v.aux0[pl.ds(2 + nh, nh)] = jnp.broadcast_to(lines[:, 2 * R : 2 * R + 1], (nh, 4 * R))
        saux.start()

        def turn(i):
            loads[i].wait()
            if i + 1 < turns:
                loads[i + 1].start()
            v.ffs[...] = v.ffb[i % 2].astype(F32)
            for j in range(8):
                part = v.ffs[pl.ds(j, 128, stride=8)]
                v.gsend[pl.ds((j % 2) * F + (j // 2) * 128, 128), pl.ds(i * 128, 128)] = jnp.transpose(part).astype(BF)

        for i in range(turns):
            turn(i)

        pl.when(is_sw)(first_norm)
        weights["so"].start()
        senc.start()
        for name in ("ckv", "cq", "co"):
            weights[name].start()
        for x in qkv3:
            x.forward()
        saux.wait()

        row16 = lax.broadcasted_iota(jnp.int32, (PADH, R), 0)
        ones_row = jnp.where(row16 == 0, 1.0, 0.0).astype(BF)

        def mask_rows(row, b):
            line = v.aux[pl.ds(row, 1), pl.ds(b * R, R)]
            return jnp.where(row16 == 0, jnp.broadcast_to(line, (PADH, R)), 0.0).astype(BF)

        for b in range(4):
            for h in range(nh):
                v.qa[b, h, pl.ds(hd, PADH)] = ones_row
                v.q2a[b // 2, b % 2, h, pl.ds(hd, PADH)] = ones_row
                v.ka[b, h, pl.ds(hd, PADH)] = mask_rows(0, b)
        for b in range(d.ne):
            for h in range(nh):
                v.k2a[b, h, pl.ds(hd, PADH)] = mask_rows(1, b)
        for h in range(nh):
            for i in range(2):
                line = v.aux[pl.ds(2 + h, 1), pl.ds(i * 2 * R, 2 * R)]
                v.bias[h, i] = pltpu.roll(jnp.broadcast_to(line, (R, 2 * R)), 0, 1, stride=1, stride_axis=0)[:, :R]
            v.bias[h, 2] = jnp.broadcast_to(v.aux[pl.ds(2 + nh + h, 1), pl.ds(0, R)], (R, R))

        @pl.when(is_sw)
        def _():
            ag1.near()
            ag1.far()

        for x in qkv3:
            x.wait()

        def project_self(b):
            qkv = dot_nt(W("qkv"), v.h1f[b]).astype(BF)
            for h in range(nh):
                v.qa[b, h, pl.ds(0, hd)] = qkv[h * hd : (h + 1) * hd]
                v.ka[b, h, pl.ds(0, hd)] = qkv[hc + h * hd : hc + (h + 1) * hd]
            v.vT[b] = qkv[2 * hc :]

        def project_step(k, carry):
            pl.when((k == 1) & not_sw)(ag1.near)
            pl.when((k == 2) & not_sw)(ag1.far)
            pl.when(k == 3)(ag1.last)
            pl.when(k == 2)(weights["so"].forward)
            project_self(blk_ag(k))
            return carry

        lax.fori_loop(0, 4, project_step, 0)
        senc.wait()
        agenc.send(0)

        def feat(h):
            return pl.ds(h * hd, hd)

        def attend_self(b):
            qs = [v.qa[b, h] for h in range(nh)]

            def block(j, state):
                out = []
                for h in range(nh):
                    m, total, acc = state[h]
                    s = dot_tn(v.ka[j, h], qs[h]) + v.bias[h, jnp.minimum(b - j, 2)]
                    new = jnp.maximum(m, jnp.max(s, axis=0, keepdims=True))
                    p = jnp.exp(s - new)
                    scale = jnp.exp(m - new)
                    total = total * scale + jnp.sum(p, axis=0, keepdims=True)
                    out.append((new, total, acc * scale + dot_nn(v.vT[j, feat(h)], p.astype(BF))))
                return tuple(out)

            first = (jnp.full((1, R), -1e30, F32), jnp.zeros((1, R), F32), jnp.zeros((hd, R), F32))
            state = lax.fori_loop(0, b + 1, block, (first,) * nh)
            for h in range(nh):
                m, total, acc = state[h]
                v.o1[b, feat(h)] = (acc / total).astype(BF)
                v.lse1[b, pl.ds(h, 1)] = m + jnp.log(total)

        def attend_cross(i, j):
            for h in range(nh):
                q = v.q2a[i, j, h]
                s = [dot_tn(v.k2a[e, h], q) for e in range(d.ne)]
                m = jnp.max(s[0], axis=0, keepdims=True)
                for part in s[1:]:
                    m = jnp.maximum(m, jnp.max(part, axis=0, keepdims=True))
                p = [jnp.exp(part - m) for part in s]
                total = sum(jnp.sum(part, axis=0, keepdims=True) for part in p)
                acc = sum(dot_nn(v.v2T[e, feat(h)], part.astype(BF)) for e, part in enumerate(p))
                v.o2[i, j, feat(h)] = (acc / total).astype(BF)
                v.lse2[i, j, pl.ds(h, 1)] = m + jnp.log(total)

        def tile_back(h, q, k, vals, da, inner, logsum, bias):
            s = dot_tn(k, q)
            if bias is not None:
                s = s + bias
            p = jnp.exp(s - logsum)
            ds = p * (dot_tn(vals, da) - inner)
            return p.astype(BF), ds, ds.astype(BF)

        def head_back(h, q, out, lse):
            da = v.da[feat(h)]
            inner = jnp.sum(da.astype(F32) * out.astype(F32), axis=0, keepdims=True)
            return q, da, inner, lse

        def attend_self_back(b):
            heads = [head_back(h, v.qa[b, h], v.o1[b, feat(h)], v.lse1[b, pl.ds(h, 1)]) for h in range(nh)]

            def block(j, dqs):
                kind = jnp.minimum(b - j, 2)
                out = []
                for h in range(nh):
                    q, da, inner, logsum = heads[h]
                    k = v.ka[j, h]
                    p, ds, low = tile_back(h, q, k, v.vT[j, feat(h)], da, inner, logsum, v.bias[h, kind])
                    v.dka[j, h] += dot_nt(q, low)
                    v.dva[j, feat(h)] += dot_nt(da, p)
                    v.dsacc[h, kind] += ds
                    out.append(dqs[h] + dot_nn(k, low))
                return tuple(out)

            dqs = lax.fori_loop(0, b + 1, block, (jnp.zeros((ha, R), F32),) * nh)
            for h in range(nh):
                v.dqkvT[b, feat(h)] = dqs[h][:hd].astype(BF)

        def attend_cross_back(i, j):
            for h in range(nh):
                q, da, inner, logsum = head_back(h, v.q2a[i, j, h], v.o2[i, j, feat(h)], v.lse2[i, j, pl.ds(h, 1)])
                dq = jnp.zeros((ha, R), F32)
                for e in range(d.ne):
                    k = v.k2a[e, h]
                    p, ds, low = tile_back(h, q, k, v.v2T[e, feat(h)], da, inner, logsum, None)
                    v.dka[e, h] += dot_nt(q, low)
                    v.dva[e, feat(h)] += dot_nt(da, p)
                    dq = dq + dot_nn(k, low)
                v.dq2T[i, j, feat(h)] = dq[:hd].astype(BF)

        def self_forward(k, carry):
            b = blk_rs(k)
            attend_self(b)
            pl.when(k == 0)(weights["so"].wait)
            v.pb[...] = dot_tn(v.o1[b], W("so"))
            rs1.emit(k)
            pl.when(k == 1)(scot.start)
            pl.when(k == 1)(agenc.near)
            pl.when(k == 1)(agenc.far)
            for name in ("ckv", "cq", "co"):
                pl.when(k == 2)(weights[name].forward)
            return carry

        lax.fori_loop(0, 4, self_forward, 0)
        agenc.last()
        weights["ckv"].wait()
        per = R // E
        for b in range(4):
            lanes = pl.ds((b % per) * E, E)
            kv = dot_nt(W("ckv"), v.encf[b]).astype(BF)
            for h in range(nh):
                v.k2a[b // per, h, pl.ds(0, hd), lanes] = kv[h * hd : (h + 1) * hd]
            v.v2T[b // per, :, lanes] = kv[hc:]

        def fin1(h, rows, total):
            x1 = v.xb[rows].astype(F32) + total
            v.x1[rows] = x1
            v.h2f[h, a, pl.ds(pl.multiple_of(c * HR, HR), HR)] = norm_fwd(x1, gain(1))
            ag2.send(h)

        for h in range(2):
            rs1.finish(h, fin1)
        for name in ("gu", "fo"):
            weights[name].start()

        weights["cq"].wait()
        weights["co"].wait()

        def cross_block(i, j):
            q = dot_nt(W("cq"), v.h2f[i, j]).astype(BF)
            for h in range(nh):
                v.q2a[i, j, h, pl.ds(0, hd)] = q[h * hd : (h + 1) * hd]
            attend_cross(i, j)

        def send_cot(h):
            pl.when(h == 0)(scot.wait)
            rows = pl.ds(pl.multiple_of(h * HR, HR), HR)
            v.d3f[h, a, pl.ds(pl.multiple_of(c * HR, HR), HR)] = v.cotb[rows]
            agd3.send(h)

        rs1.sent()
        halves(ag2, cross_block, rs2, lambda i, j: dot_tn(v.o2[i, j], W("co")), send_cot)
        for name in ("gu", "fo"):
            weights[name].forward()

        def fin2(h, rows, total):
            x2 = v.x1[rows] + total
            v.x2[rows] = x2
            v.h3f[h, a, pl.ds(pl.multiple_of(c * HR, HR), HR)] = norm_fwd(x2, gain(2))
            ag3.send(h)

        for h in range(2):
            rs2.finish(h, fin2)
        for h in range(2):
            agd3.near(h)
            agd3.pass_on(h)
        for h in range(2):
            agd3.last(h)
        for name in ("gu", "fo"):
            weights[name].wait()

        fc = 64

        def hidden_block(i, j):
            rows = v.h3f[i, j]
            v.gus[pl.ds(0, F)] = dot_nt(W("gu", 0, F), rows)
            v.gus[pl.ds(F, F)] = dot_nt(W("gu", F, F), rows)
            v.gus[pl.ds(2 * F, F)] = dot_nt(W("fo"), v.d3f[i, j])

            def chunk(n, carry):
                r = pl.multiple_of(n * fc, fc)
                gate, up, dact = (v.gus[pl.ds(m * F + r, fc)] for m in range(3))
                sq = gate * gate
                th = jnp.tanh(gate * (GELU_C + (GELU_C * 0.044715) * sq))
                half = 0.5 + 0.5 * th
                gelu = gate * half
                slope = half + gate * (0.5 - 0.5 * th * th) * (GELU_C + (3.0 * GELU_C * 0.044715) * sq)
                v.actT[i, j, pl.ds(r, fc)] = (gelu * up).astype(BF)
                v.dguT[i, j, pl.ds(r, fc)] = (dact * up * slope).astype(BF)
                v.dguT[i, j, pl.ds(F + r, fc)] = (dact * gelu).astype(BF)
                return carry

            lax.fori_loop(0, F // fc, chunk, 0)

        rs2.sent()
        halves(ag3, hidden_block, rs3, lambda i, j: dot_tn(v.dguT[i, j], W("gu")))

        def grads(at, lhs, rows, rhs, tile):
            spots = [(b,) for b in range(4)] if len(lhs.shape) == 3 else [(b // 2, b % 2) for b in range(4)]

            def step(i, carry):
                r = pl.multiple_of(i * tile, 64)
                total = None
                for spot in spots:
                    part = dot_nn(lhs[spot + (pl.ds(r, tile),)], rhs[spot])
                    total = part if total is None else total + part
                v.gf[pl.ds(at + r, tile)] = total
                return carry

            lax.fori_loop(0, rows // tile, step, 0)

        def loc(name, group):
            base, _, at, _ = d.groups[group]
            return d.w[name][0] - base + at

        def add_gain(i, h, part):
            if h == 0:
                v.smc[pl.ds(i, 1)] = part
            else:
                v.smc[pl.ds(i, 1)] += part

        v.smc[...] = jnp.zeros(v.smc.shape, F32)

        def fin3(h, rows, total):
            grad, part = norm_bwd(v.x2[rows], gain(2), total)
            add_gain(2, h, part)
            g2 = v.cotb[rows].astype(F32) + grad
            v.gb[rows] = g2
            v.d2f[h, a, pl.ds(pl.multiple_of(c * HR, HR), HR)] = g2.astype(BF)
            agd2.send(h)

        rs3.finish(0, fin3)
        grads(loc("gu", "G"), v.dguT, 2 * F, v.h3f, 256)
        pl.when(is_sw)(weights["gu"].far.sent)
        redG.send()

        def hidden_out(h, carry):
            rso.emit_pair(h, lambda i, j: dot_tn(v.actT[i, j], W("fo")), kick=False)
            return carry

        lax.fori_loop(0, 2, hidden_out, 0)
        rs3.finish(1, fin3)
        grads(loc("fo", "H"), v.actT, F, v.d3f, 256)
        redH.send()
        rso.kick()

        v.dka[...] = jnp.zeros(v.dka.shape, F32)
        v.dva[...] = jnp.zeros(v.dva.shape, F32)

        def cross_back_block(i, j):
            v.da[...] = dot_nt(W("co"), v.d2f[i, j]).astype(BF)
            attend_cross_back(i, j)

        rs3.sent()
        halves(agd2, cross_back_block, rs4, lambda i, j: dot_tn(v.dq2T[i, j], W("cq")))

        def fin4(h, rows, total):
            grad, part = norm_bwd(v.x1[rows], gain(1), total)
            add_gain(1, h, part)
            g1 = v.gb[rows] + grad
            v.gb[rows] = g1
            v.d1f[t, rows] = g1.astype(BF)
            agd1.send(h)

        for b in range(4):
            lanes = pl.ds((b % per) * E, E)
            for h in range(nh):
                v.dkv2T[b, pl.ds(h * hd, hd)] = v.dka[b // per, h, pl.ds(0, hd), lanes].astype(BF)
            v.dkv2T[b, pl.ds(hc, hc)] = v.dva[b // per, :, lanes].astype(BF)

        def enc_part(b):
            v.epb[...] = dot_tn(v.dkv2T[b], W("ckv"))

        rse.loop(enc_part, kick=False)
        grads(loc("cq", "C"), v.dq2T, hc, v.h2f, hc)
        grads(loc("co", "C"), v.o2, hc, v.d2f, hc)
        grads(loc("ckv", "C"), v.dkv2T, 2 * hc, v.encf, hc)
        redC.send()
        rs4.finish(0, fin4)

        def fin_out(h, rows, total):
            v.lov[rows] = (v.x2[rows] + total).astype(BF)

        for h in range(2):
            rso.finish(h, fin_out)
        rs4.finish(1, fin4)
        redG.combine()

        v.dka[...] = jnp.zeros(v.dka.shape, F32)
        v.dva[...] = jnp.zeros(v.dva.shape, F32)
        v.dsacc[...] = jnp.zeros(v.dsacc.shape, F32)

        def self_back(k, carry):
            b = blk_ag(k)
            agd1.arrive(k)
            pl.when(k == 2)(out_lo.start)
            pl.when(k == 3)(rse.kick)
            pl.when(k == 2)(redH.combine)

            @pl.when(k == 3)
            def _():
                grads(loc("so", "O"), v.o1, hc, v.d1f, hc)
                redO.send()

            v.da[...] = dot_nt(W("so"), v.d1f[b]).astype(BF)
            attend_self_back(b)
            return carry

        lax.fori_loop(0, 4, self_back, 0)

        for b in range(4):
            for h in range(nh):
                v.dqkvT[b, pl.ds(hc + h * hd, hd)] = v.dka[b, h, pl.ds(0, hd)].astype(BF)
            v.dqkvT[b, pl.ds(2 * hc, hc)] = v.dva[b].astype(BF)
        grads(loc("qkv", "S"), v.dqkvT, 3 * hc, v.h1f, hc)
        redS.send()

        def self_qkv_part(b):
            v.pb[...] = dot_tn(v.dqkvT[b], W("qkv"))

        rs4.sent()
        rs5.loop(self_qkv_part)
        redC.combine()
        redO.combine()
        redG.finish()
        redH.finish()

        def fin_enc(h, rows, total):
            v.egv[rows] = total.astype(BF)


        iota0 = lax.broadcasted_iota(jnp.int32, (R, R), 0)
        iota1 = lax.broadcasted_iota(jnp.int32, (R, R), 1)
        flip = (iota0 + iota1 == R - 1).astype(F32)

        def diagonals(h, i):
            turned = lax.dot_general(
                flip, v.dsacc[h, i], (((1,), (0,)), ((), ())), precision=lax.Precision.HIGHEST, preferred_element_type=F32
            )
            wide = jnp.concatenate([turned, jnp.zeros((R, R), F32)], axis=1)
            return jnp.sum(pltpu.roll(wide, 0, 1, stride=1, stride_axis=0), axis=0, keepdims=True)

        lane = lax.broadcasted_iota(jnp.int32, (1, 2 * R), 1)
        for h in range(nh):
            near, off = diagonals(h, 0), diagonals(h, 1)
            far = jnp.sum(jnp.sum(v.dsacc[h, 2], axis=0, keepdims=True), axis=1, keepdims=True)
            off = off + jnp.where(lane == 2 * R - 1, far, 0.0)
            line = jnp.concatenate([pltpu.roll(near, R + 1, 1)[:, :R], off], axis=1)
            for q in range(4):
                v.smc[pl.ds(3 + q * nh + h, 1), pl.ds(0, 3 * R)] = jnp.where(t == q, line, 0.0)

        def fin5(h, rows, total):
            grad, part = norm_bwd(v.xb[rows].astype(F32), gain(0), total)
            add_gain(0, h, part)
            v.igv[rows] = (v.gb[rows] + grad).astype(BF)

        plane = peers[1:]
        lines = [zp, z2]
        first = [Xfer(v.sms.at[i], v.smr.at[i], dev) for i, dev in enumerate(lines)]
        second = [Xfer(v.sms.at[2], v.smr.at[3 + i], dev) for i, dev in enumerate(plane)]
        third = [Xfer(v.sms.at[3], v.smr.at[6], sib)]
        redS.combine()
        for h in range(2):
            rs5.finish(h, fin5)
        v.sms[0] = v.smc[...]
        first[0].start()
        first[0].recv()
        v.sms[1] = v.sms[0] + v.smr[0]
        first[1].start()
        for x in out_ig:
            x.start()
        redS.finish()
        redC.finish()
        redO.finish()
        first[1].recv()
        v.sms[2] = v.sms[1] + v.smr[1]
        for x in second:
            x.start()
        rse.finish(0, fin_enc)
        out_eg.start()
        redG.relay()
        redH.relay()
        redC.relay()
        for x in second:
            x.recv()
        if len(plane) == 3:
            v.sms[3] = (v.sms[2] + v.smr[3]) + (v.smr[4] + v.smr[5])
        elif len(plane) == 1:
            v.sms[3] = v.sms[2] + v.smr[3]
        else:
            v.sms[3] = v.sms[2]
        third[0].start()
        redO.relay()
        redS.relay()
        third[0].recv()
        sm_ref[...] = v.sms[3] + v.smr[6]

        for x in first + second + third:
            x.sent()
        for x in (ag1, ag2, ag3, agd1, agd2, agd3, agenc, rs5, rso, rse):
            x.sent()
        for x in [saux, scot, senc] + sx:
            x.sent()
        for name, x in weights.items():
            x.sent(name != "gu")
        for x in qkv3:
            x.sent()
        for x in [out_lo, out_eg] + out_ig:
            x.wait()
            x.sent()
        for r in (redG, redH, redC, redO, redS):
            r.done()

    return kernel


def unpack(d, gw, lo, ig, eg, sm):
    R, D, F, hc, nh, E = d.R, d.D, d.F, d.hc, d.nh, d.E
    steps = 3
    cols = D // steps

    def kernel(gu_ref, fo_ref, qkv_ref, so_ref, ckv_ref, cq_ref, co_ref, lo_ref, ig_ref, eg_ref, sm_ref, *outs):
        lo_out, ig_out, eg_out, gu_out, fo_out, qkv_out, so_out, ckv_out, cq_out, co_out, gains_out, table_out = outs
        for j in range(2 * F // 128):
            part = jnp.transpose(gu_ref[pl.ds((j % 2) * F + (j // 2) * 128, 128)].astype(F32))
            gu_out[pl.ds(j, cols, stride=2 * F // 128)] = part
        for src, dst in (
            (fo_ref, fo_out), (qkv_ref, qkv_out), (so_ref, so_out), (ckv_ref, ckv_out), (cq_ref, cq_out), (co_ref, co_out)
        ):
            dst[...] = src[...].astype(F32)

        @pl.when(pl.program_id(0) == 0)
        def _():
            lo_out[...] = lo_ref[...]
            ig_out[...] = ig_ref[...].astype(F32)
            eg_out[...] = eg_ref[...].astype(F32)
            gains_out[...] = sm_ref[pl.ds(0, 3)]
            col = lax.broadcasted_iota(jnp.int32, (1, D), 1)
            dist = jnp.where(col < R, col, jnp.where(col < 3 * R - 1, col - R + 1, 4 * R))
            pick = (lax.broadcasted_iota(jnp.int32, (NB, D), 0) == bucket_index(dist)).astype(F32)
            z = lax.axis_index("mp")
            mine = jnp.zeros((nh, D), F32)
            for q in range(4):
                mine = jnp.where(z == q, sm_ref[pl.ds(3 + q * nh, nh)], mine)
            table_out[...] = lax.dot_general(
                mine, pick, (((1,), (1,)), ((), ())), precision=lax.Precision.HIGHEST, preferred_element_type=F32
            )

    at = lambda name: d.w[name][0]
    rows = lambda name, n: pl.BlockSpec((n, D), lambda i: (at(name) // n + i, 0))
    out_rows = lambda n: pl.BlockSpec((n, D), lambda i: (i, 0))
    whole = lambda *shape: pl.BlockSpec(shape, lambda i: (0,) * len(shape))
    third = {name: d.w[name][1] // steps for name in ("qkv", "so", "ckv", "cq", "co")}
    half = F // 2
    assert all(at(name) % n == 0 for name, n in third.items()) and at("fo") % half == 0 and at("gu") == 0
    shape = lambda *dims: jax.ShapeDtypeStruct(dims, F32)
    return pl.pallas_call(
        kernel,
        grid=(steps,),
        in_specs=[
            pl.BlockSpec((2 * F, cols), lambda i: (0, i)),
            pl.BlockSpec((half, D), lambda i: (at("fo") // half + jnp.minimum(i, 1), 0)),
        ]
        + [rows(name, n) for name, n in third.items()]
        + [whole(R, D), whole(R, D), whole(E, D), whole(d.small, D)],
        out_specs=[
            whole(R, D), whole(R, D), whole(E, D),
            pl.BlockSpec((cols * 2 * F // 128, 128), lambda i: (i, 0)),
            pl.BlockSpec((half, D), lambda i: (jnp.minimum(i, 1), 0)),
        ]
        + [out_rows(n) for n in third.values()]
        + [whole(3, D), whole(nh, NB)],
        out_shape=[
            jax.ShapeDtypeStruct((R, D), BF), shape(R, D), shape(E, D), shape(D * 2 * F // 128, 128), shape(F, D),
            shape(3 * hc, D), shape(hc, D), shape(2 * hc, D), shape(hc, D), shape(hc, D), shape(3, D), shape(nh, NB),
        ],
        compiler_params=pltpu.CompilerParams(vmem_limit_bytes=63 << 20),
    )(*[gw] * 7, lo, ig, eg, sm)


def local_fn(mesh):
    def local(x_in, enc_in, cotangent, dec_len, enc_len, self_qkv, self_out, cross_q, cross_kv, cross_out, ff_in, ff_out, gains, table):
        d = make_dims(mesh, x_in, enc_in, self_qkv, ff_in, table)
        R, D, hc, nh, F = d.R, d.D, d.hc, d.nh, d.F
        hbm = pl.BlockSpec(memory_space=pl.ANY)
        vmem = pl.BlockSpec(memory_space=pltpu.VMEM)
        smem = pl.BlockSpec(memory_space=pltpu.SMEM)
        ws = {
            "qkv": jnp.transpose(self_qkv, (1, 2, 0)).reshape(3 * hc, D),
            "so": self_out,
            "cq": jnp.transpose(cross_q),
            "ckv": jnp.transpose(cross_kv, (1, 2, 0)).reshape(2 * hc, D),
            "co": cross_out,
            "gu": jnp.transpose(ff_in.reshape(D, 2, F // 128, 128), (0, 2, 1, 3)).reshape(D * 2 * F // 128, 128),
            "fo": ff_out,
        }
        outs = pl.pallas_call(
            build_kernel(d),
            out_shape=(
                jax.ShapeDtypeStruct((R, D), BF),
                jax.ShapeDtypeStruct((R, D), BF),
                jax.ShapeDtypeStruct((d.E, D), BF),
                jax.ShapeDtypeStruct((d.rows, D), BF),
                jax.ShapeDtypeStruct((d.small, D), F32),
            ),
            in_specs=[hbm, hbm, hbm, vmem, smem, smem, vmem] + [hbm] * len(d.w),
            out_specs=(hbm, hbm, hbm, hbm, vmem),
            scratch_shapes=[pltpu.VMEM(shape, dtype) for _, shape, dtype in scratch_list(d)]
            + [pltpu.SemaphoreType.DMA((SEMS,))] * 3,
            compiler_params=pltpu.CompilerParams(collective_id=0, has_side_effects=True, vmem_limit_bytes=63 << 20),
        )(x_in, enc_in, cotangent, jnp.transpose(table), dec_len, enc_len, gains, *[ws[name] for name in d.w])
        lo, ig, eg, gw, sm = outs
        others = d.ndp // (2 * d.nd)
        if others > 1:
            gw, sm = lax.psum((gw.astype(F32), sm), "dp")
            gw, sm = gw * (1.0 / (2 * d.nd)), sm * (1.0 / (2 * d.nd))
        res = unpack(d, gw, lo, ig, eg, sm)
        gu = jnp.transpose(res[3].reshape(D, F // 128, 2, 128), (0, 2, 1, 3)).reshape(D, 2, F)
        return (
            res[0],
            res[1],
            res[2],
            jnp.transpose(res[5].reshape(3, hc, D), (2, 0, 1)),
            res[6],
            jnp.transpose(res[8]),
            jnp.transpose(res[7].reshape(2, hc, D), (2, 0, 1)),
            res[9],
            gu,
            res[4],
            res[10],
            jnp.transpose(res[11]),
        )

    return local


def solution(mesh):
    rows = P(("dp", "mp"), None)
    in_specs = (
        rows, rows, rows, P("dp"), P("dp"), P(None, None, "mp"), P("mp", None), P(None, "mp"), P(None, None, "mp"),
        P("mp", None), P(None, None, "mp"), P("mp", None), P(), P(None, "mp"),
    )
    out_specs = (
        rows, rows, rows, P(None, None, "mp"), P("mp", None), P(None, "mp"), P(None, None, "mp"), P("mp", None),
        P(None, None, "mp"), P("mp", None), P(), P(None, "mp"),
    )
    return jax.shard_map(local_fn(mesh), mesh=mesh, in_specs=in_specs, out_specs=out_specs, check_vma=False)
```

```python
import math

import jax
import jax.numpy as jnp
from jax import lax
from jax.experimental import pallas as pl
from jax.experimental.pallas import tpu as pltpu
from jax.sharding import PartitionSpec as P

NB = 32
MAXD = 128
NORM_EPS = 1e-06
MASK_FILL = -1000000000.0
MESH = pl.DeviceIdType.MESH
BF = jnp.bfloat16
F32 = jnp.float32
PARTS = 2
PADH = 16
GELU_C = math.sqrt(2.0 / math.pi)
SEMS = 256


def bucket_index(distance):
    half_count = NB // 2
    clipped = jnp.maximum(distance, 0)
    bucket_ids = jnp.minimum(clipped, half_count)
    for level_pos in range(1, half_count):
        threshold = math.ceil(half_count * (MAXD / half_count) ** (level_pos / half_count))
        bucket_ids = bucket_ids + (clipped >= threshold).astype(jnp.int32)
    return bucket_ids


def dot_nn(a, b):
    return lax.dot_general(a, b, (((1,), (0,)), ((), ())), preferred_element_type=F32)


def dot_nt(a, b):
    return lax.dot_general(a, b, (((1,), (1,)), ((), ())), preferred_element_type=F32)


def dot_tn(a, b):
    return lax.dot_general(a, b, (((0,), (0,)), ((), ())), preferred_element_type=F32)


def norm_fwd(v, g):
    inv = lax.rsqrt(jnp.mean(v * v, axis=-1, keepdims=True) + NORM_EPS)
    return (v * inv * g).astype(BF)


def norm_bwd(v, g, u):
    inv = lax.rsqrt(jnp.mean(v * v, axis=-1, keepdims=True) + NORM_EPS)
    gu = u * g
    mean = jnp.mean(gu * v, axis=-1, keepdims=True)
    grad = inv * gu - v * (inv * inv * inv * mean)
    gain = jnp.sum(u * v * inv, axis=0, keepdims=True)
    return grad, gain


class Dims:
    pass


def make_dims(mesh, x_in, enc_in, self_qkv, ff_in, table):
    d = Dims()
    d.ndp, d.nmp = mesh.shape["dp"], mesh.shape["mp"]
    d.nd = min(4, d.ndp // 2)
    d.R, d.D = x_in.shape
    d.E = enc_in.shape[0]
    d.nh = table.shape[1]
    d.hc = self_qkv.shape[2]
    d.hd = d.hc // d.nh
    d.F = ff_in.shape[2]
    d.ha = d.hd + PADH
    d.ne = 4 * d.E // d.R
    d.axr = -(-(2 + 2 * d.nh) // 8) * 8
    hc, F = d.hc, d.F
    names = (("gu", 2 * F), ("fo", F), ("qkv", 3 * hc), ("so", hc), ("ckv", 2 * hc), ("cq", hc), ("co", hc))
    d.w, at = {}, 0
    for name, rows in names:
        d.w[name] = (at, rows)
        at += rows
    d.rows = at
    s, c = 3 * hc, 4 * hc
    d.groups = {}
    land = 0
    for name, base, rows in (("G", 0, 2 * F), ("H", 2 * F, F), ("S", 3 * F, s), ("O", 3 * F + s, hc), ("C", 3 * F + s + hc, c)):
        d.groups[name] = (base, rows, 0, land)
        land += rows // d.nd
    d.land = land
    d.locrows = max(s, c, 2 * F)
    d.small = -(-(3 + d.nh) // 8) * 8
    return d


def scratch_list(d):
    R, D, hc, nh, hd, ha, F, E = d.R, d.D, d.hc, d.nh, d.hd, d.ha, d.F, d.E
    full = ((4, R, D), BF)
    pair = ((2, 2, R, D), BF)
    HR = R // 2
    return [
        ("xb", (R, D), BF), ("cotb", (R, D), BF), ("aux", (d.axr, 4 * R), F32), ("aux0", (d.axr, 4 * R), F32), ("ffb", (2, 1024, 128), BF), ("ffs", (1024, 128), F32), ("wv", (d.rows, D), BF),
        ("h1f",) + full, ("h2f",) + pair, ("h3f",) + pair, ("d3f",) + pair, ("d2f",) + pair, ("d1f",) + full,
        ("encf", (4, E, D), BF),
        ("qa", (4, nh, ha, R), BF), ("ka", (4, nh, ha, R), BF), ("vT", (4, hc, R), BF), ("o1", (4, hc, R), BF),
        ("q2a", (2, 2, nh, ha, R), BF), ("k2a", (d.ne, nh, ha, R), BF), ("v2T", (d.ne, hc, R), BF), ("o2", (2, 2, hc, R), BF),
        ("lse1", (4, 8, R), F32), ("lse2", (2, 2, 8, R), F32),
        ("bias", (nh, 3, R, R), F32), ("dsacc", (nh, 3, R, R), F32),
        ("x1", (R, D), F32), ("x2", (R, D), F32), ("gb", (R, D), F32),
        ("pb", (R, D), F32), ("pf", (R, D), F32), ("sb", (2, 3, HR, D), BF), ("rb", (2, 3, HR, D), BF),
        ("opb", (R, D), F32), ("osb", (2, 3, HR, D), BF), ("orb", (2, 3, HR, D), BF), ("lov", (R, D), BF), ("igv", (R, D), BF),
        ("epb", (E, D), F32), ("esb", (1, 3, E, D), BF), ("erb", (1, 3, E, D), BF), ("egv", (E, D), BF),
        ("actT", (2, 2, F, R), BF), ("dguT", (2, 2, 2 * F, R), BF), ("gus", (3 * F, R), F32),
        ("da", (hc, R), BF), ("dqkvT", (4, 3 * hc, R), BF), ("dq2T", (2, 2, hc, R), BF), ("dkv2T", (4, 2 * hc, E), BF),
        ("dka", (4, nh, ha, R), F32), ("dva", (4, hc, R), F32),
        ("gf", (d.locrows, D), F32), ("gsend", (d.rows, D), BF), ("grecv", (max(d.nd - 1, 1), d.land, D), BF),
        ("gz", (d.land, D), BF), ("gk", (d.land, D), F32), ("gfo", (d.land, D), BF),
        ("smc", (d.small, D), F32), ("sms", (4, d.small, D), F32), ("smr", (7, d.small, D), F32),
    ]


def build_kernel(d):
    R, D, hc, nh, hd, ha, F, E = d.R, d.D, d.hc, d.nh, d.hd, d.ha, d.F, d.E
    names = [item[0] for item in scratch_list(d)]
    wnames = list(d.w)
    HR = R // PARTS

    def kernel(*refs):
        x_ref, e_ref, cot_ref, tab_ref, dlen_ref, elen_ref, gains_ref = refs[:7]
        w_refs = dict(zip(wnames, refs[7 : 7 + len(wnames)]))
        lo_ref, ig_ref, eg_ref, gout_ref, sm_ref = refs[7 + len(wnames) : 12 + len(wnames)]
        tail = refs[12 + len(wnames) :]
        v = Dims()
        for name, ref in zip(names, tail):
            setattr(v, name, ref)
        ss, rs, ls = tail[len(names) :]
        ff_ref = w_refs["gu"]
        w_refs["gu"] = v.gsend.at[pl.ds(0, 2 * F)]

        dp, z = lax.axis_index("dp"), lax.axis_index("mp")
        c, chip = dp % 2, dp // 2
        a, u = z % 2, z // 2
        t = a + 2 * c
        sw = c + u - 2 * c * u
        dl = chip % d.nd
        base_dp = (chip - dl) * 2
        sib = (dp + 1 - 2 * c, z)
        zp = (dp, z + 1 - 2 * a)
        z2 = (dp, z + 2 - 4 * u)
        mate = (2 * chip + u, a + 2 * c)
        d0, d1 = dl % 2, dl // 2
        flips = [dl, dl + 1 - 2 * d0, dl + 2 - 4 * d1, 3 - dl][: d.nd]
        peers = [(base_dp + 2 * f + c, z) for f in flips]
        is_sw, not_sw = sw == 1, sw == 0

        count = [0]

        def new_id():
            count[0] += 1
            assert count[0] <= SEMS
            return count[0] - 1

        class Xfer:
            def __init__(self, src, dst, dev, i=None):
                self.i, self.src, self.dst, self.dev = new_id() if i is None else i, src, dst, dev

            def desc(self):
                return pltpu.make_async_remote_copy(
                    src_ref=self.src, dst_ref=self.dst, send_sem=ss.at[self.i], recv_sem=rs.at[self.i],
                    device_id={"dp": self.dev[0], "mp": self.dev[1]}, device_id_type=MESH,
                )

            def start(self):
                self.desc().start()

            def recv(self):
                self.desc().wait_recv()

            def sent(self):
                self.desc().wait_send()

        class Local:
            def __init__(self, src, dst):
                self.i, self.src, self.dst = new_id(), src, dst

            def desc(self):
                return pltpu.make_async_copy(self.src, self.dst, ls.at[self.i])

            def start(self):
                self.desc().start()

            def wait(self):
                self.desc().wait()

        class Swap:
            def __init__(self, src, dst):
                self.far, self.near = Xfer(src, dst, mate), Local(src, dst)

            def start(self):
                pl.when(is_sw)(self.far.start)
                pl.when(not_sw)(self.near.start)

            def wait(self):
                pl.when(is_sw)(self.far.recv)
                pl.when(not_sw)(self.near.wait)

            def sent(self):
                pl.when(is_sw)(self.far.sent)

        class Weight:
            def __init__(self, name, piece=0, pieces=1):
                first, rows = d.w[name]
                rows = rows // pieces
                at = piece * rows
                first += at
                sl = rows // d.nd
                mine = pl.ds(pl.multiple_of(at + dl * sl, 16), sl)
                here = v.wv.at[pl.ds(pl.multiple_of(first + dl * sl, 16), sl)]
                self.near = Local(w_refs[name].at[pl.ds(at, rows)], v.wv.at[pl.ds(first, rows)])
                self.far = Xfer(w_refs[name].at[mine], here, mate)
                self.on = [Xfer(here, here, peer) for peer in peers[1:]]

            def start(self):
                pl.when(is_sw)(self.far.start)
                pl.when(not_sw)(self.near.start)

            def forward(self):
                @pl.when(is_sw)
                def _():
                    self.far.recv()
                    for x in self.on:
                        x.start()

            def wait(self):
                pl.when(not_sw)(self.near.wait)

                @pl.when(is_sw)
                def _():
                    for x in self.on:
                        x.recv()

            def sent(self, first=True):
                @pl.when(is_sw)
                def _():
                    if first:
                        self.far.sent()
                    for x in self.on:
                        x.sent()

        def blk_ag(k):
            k1, k2 = k % 2, k // 2
            return (a + k2 - 2 * a * k2) + 2 * (c + k1 - 2 * c * k1)

        def blk_rs(k):
            return blk_ag(3 - k)

        class Gather:
            def __init__(self, full, rows, parts):
                self.parts = parts
                n = rows // parts
                at = lambda b, h: full.at[b, pl.ds(h * n, n)]
                b_zp = (1 - a) + 2 * c
                self.z = [Xfer(at(t, h), at(t, h), zp) for h in range(parts)]
                self.c = [Xfer(at(t, h), at(t, h), sib) for h in range(parts)]
                self.f = [Xfer(at(b_zp, h), at(b_zp, h), sib) for h in range(parts)]

            def send(self, h):
                self.z[h].start()
                self.c[h].start()

            def near(self):
                for x in self.c:
                    x.recv()

            def far(self):
                for x, y in zip(self.z, self.f):
                    x.recv()
                    y.start()

            def last(self):
                for x in self.f:
                    x.recv()

            def arrive(self, k):
                pl.when(k == 1)(self.near)
                pl.when(k == 2)(self.far)
                pl.when(k == 3)(self.last)

            def sent(self):
                for x in self.z + self.c + self.f:
                    x.sent()

        class PairGather:
            def __init__(self, full):
                self.full, self.ids = full, [new_id() for _ in range(6)][0]

            def own(self, h):
                return self.full.at[h, a, pl.ds(pl.multiple_of(c * HR, HR), HR)]

            def z(self, h):
                return Xfer(self.own(h), self.own(h), zp, self.ids + h)

            def c(self, h):
                return Xfer(self.own(h), self.own(h), sib, self.ids + 2 + h)

            def f(self, h):
                there = self.full.at[h, 1 - a, pl.ds(pl.multiple_of(c * HR, HR), HR)]
                return Xfer(there, there, sib, self.ids + 4 + h)

            def send(self, h):
                self.z(h).start()
                self.c(h).start()

            def near(self, h):
                self.c(h).recv()

            def pass_on(self, h):
                self.z(h).recv()
                self.f(h).start()

            def last(self, h):
                self.f(h).recv()

            def sent(self):
                for h in range(2):
                    for x in (self.z(h), self.c(h), self.f(h)):
                        x.sent()

        class Scatter:
            def __init__(self, pb, sb, rb):
                self.pb, self.sb, self.rb = pb, sb, rb
                self.parts, self.n = sb.shape[0], sb.shape[2]
                self.ids = [new_id() for _ in range(3 * self.parts)][0]

            def rows(self, h):
                return pl.ds(h * self.n if isinstance(h, int) else pl.multiple_of(h * self.n, self.n), self.n)

            def x(self, slot, h, dev):
                return Xfer(self.sb.at[h, slot], self.rb.at[h, slot], dev, self.ids + slot * self.parts + h)

            def c0(self, h):
                return self.x(0, h, sib)

            def z(self, h):
                return self.x(1, h, zp)

            def c2(self, h):
                return self.x(2, h, sib)

            def emit(self, k, kick=True):
                @pl.when(k == 0)
                def _():
                    for h in range(self.parts):
                        self.sb[h, 0] = self.pb[self.rows(h)].astype(BF)
                        self.c0(h).start()

                @pl.when(k == 1)
                def _():
                    for h in range(self.parts):
                        self.c0(h).recv()
                        self.sb[h, 1] = (self.pb[self.rows(h)] + self.rb[h, 0].astype(F32)).astype(BF)
                        if kick:
                            self.z(h).start()

                @pl.when(k == 2)
                def _():
                    for h in range(self.parts):
                        self.sb[h, 2] = self.pb[self.rows(h)].astype(BF)
                        self.c2(h).start()

            def loop(self, partial, kick=True):
                def step(k, carry):
                    partial(blk_rs(k))
                    self.emit(k, kick)
                    return carry

                lax.fori_loop(0, 4, step, 0)

            def emit_pair(self, h, partial, kick=True):
                mine = pl.ds(pl.multiple_of(c * HR, HR), HR)
                other = pl.ds(pl.multiple_of((1 - c) * HR, HR), HR)
                v.pf[...] = partial(h, 1 - a)
                self.sb[h, 0] = v.pf[other].astype(BF)
                self.c0(h).start()
                self.sb[h, 1] = v.pf[mine].astype(BF)
                v.pf[...] = partial(h, a)
                self.sb[h, 2] = v.pf[other].astype(BF)
                self.c2(h).start()
                self.pb[self.rows(h)] = v.pf[mine]
                self.c0(h).recv()
                self.sb[h, 1] = (self.sb[h, 1].astype(F32) + self.rb[h, 0].astype(F32)).astype(BF)
                if kick:
                    self.z(h).start()

            def kick(self):
                for h in range(self.parts):
                    self.z(h).start()

            def finish(self, h, fin):
                self.c2(h).recv()
                self.z(h).recv()
                rows = self.rows(h)
                fin(h, rows, self.pb[rows] + self.rb[h, 2].astype(F32) + self.rb[h, 1].astype(F32))

            def sent(self):
                for h in range(self.parts):
                    for x in (self.c0(h), self.z(h), self.c2(h)):
                        x.sent()

        def ag_loop(gather, body):
            def step(k, carry):
                gather.arrive(k)
                body(blk_ag(k))
                return carry

            lax.fori_loop(0, 4, step, 0)

        def halves(gather, body, scatter, partial, after=None):
            def half(h, carry):
                def step(k, inner):
                    pl.when(k == 0)(lambda: gather.near(h))

                    @pl.when(k == 1)
                    def _():
                        gather.pass_on(h)
                        gather.last(h)

                    body(h, a + k - 2 * a * k)
                    return inner

                lax.fori_loop(0, 2, step, 0)
                scatter.emit_pair(h, partial)
                if after is not None:
                    after(h)
                return carry

            lax.fori_loop(0, 2, half, 0)

        def W(name, lo=0, rows=None):
            first, total = d.w[name]
            return v.wv[pl.ds(first + lo, total if rows is None else rows)]

        def gain(i):
            return gains_ref[pl.ds(i, 1)].astype(F32)

        sx = [Swap(x_ref.at[pl.ds(h * HR, HR)], v.xb.at[pl.ds(h * HR, HR)]) for h in range(PARTS)]
        saux, scot = Swap(v.aux0, v.aux), Swap(cot_ref, v.cotb)
        senc = Swap(e_ref, v.encf.at[z])
        weights = {name: Weight(name) for name in wnames if name != "qkv"}
        qkv3 = [Weight("qkv", i, 3) for i in range(3)]
        ag1, agd1 = (Gather(f, R, PARTS) for f in (v.h1f, v.d1f))
        ag2, ag3, agd3, agd2 = (PairGather(f) for f in (v.h2f, v.h3f, v.d3f, v.d2f))
        agenc = Gather(v.encf, E, 1)
        rs1, rs2, rs3, rs4, rs5 = (Scatter(v.pb, v.sb, v.rb) for _ in range(5))
        rso = Scatter(v.opb, v.osb, v.orb)
        rse = Scatter(v.epb, v.esb, v.erb)
        out_lo, out_eg = Swap(v.lov, lo_ref), Swap(v.egv, eg_ref)
        out_ig = [Swap(v.igv.at[pl.ds(h * HR, HR)], ig_ref.at[pl.ds(h * HR, HR)]) for h in range(PARTS)]

        class Reduce:
            def __init__(self, name):
                self.base, self.rows, self.loc, self.land = d.groups[name]
                self.sl = sl = self.rows // d.nd
                self.tile = 96 if sl % 96 == 0 else sl
                at = lambda f: pl.ds(pl.multiple_of(self.base + f * sl, 16), sl)
                here = pl.ds(self.land, sl)
                self.own = at(dl)
                self.to = [
                    Xfer(v.gsend.at[at(f)], v.grecv.at[k, here], peer)
                    for k, (f, peer) in enumerate(zip(flips[1:], peers[1:]))
                ]
                self.zx = Xfer(v.gsend.at[self.own], v.gz.at[here], z2)
                self.keep = Local(v.gfo.at[here], gout_ref.at[self.own])
                self.spread = [Xfer(v.gfo.at[here], gout_ref.at[self.own], peer) for peer in peers[1:]]
                self.core = [Xfer(v.gfo.at[here], gout_ref.at[self.own], sib)] + [
                    Xfer(gout_ref.at[at(f)], gout_ref.at[at(f)], sib) for f in flips[1:]
                ]

            def tiles(self, rows, body):
                def step(i, carry):
                    body(pl.multiple_of(i * self.tile, 16))
                    return carry

                lax.fori_loop(0, rows // self.tile, step, 0)

            def send(self):
                def cast(r):
                    v.gsend[pl.ds(self.base + r, self.tile)] = v.gf[pl.ds(self.loc + r, self.tile)].astype(BF)

                self.tiles(self.rows, cast)
                for x in self.to:
                    x.start()

                def keep(r):
                    v.gk[pl.ds(self.land + r, self.tile)] = v.gf[
                        pl.ds(self.loc + pl.multiple_of(dl * self.sl, 16) + r, self.tile)
                    ]

                self.tiles(self.sl, keep)

            def combine(self):
                for x in self.to:
                    x.recv()

                def add(r):
                    total = v.gk[pl.ds(self.land + r, self.tile)]
                    for k in range(d.nd - 1):
                        total = total + v.grecv[k, pl.ds(self.land + r, self.tile)].astype(F32)
                    v.gk[pl.ds(self.land + r, self.tile)] = total
                    v.gsend[pl.ds(pl.multiple_of(self.base + dl * self.sl, 16) + r, self.tile)] = total.astype(BF)

                self.tiles(self.sl, add)
                pl.when(is_sw)(self.zx.start)

            def finish(self):
                @pl.when(not_sw)
                def _():
                    self.zx.recv()

                    def add(r):
                        rows = pl.ds(self.land + r, self.tile)
                        v.gfo[rows] = (v.gk[rows] + v.gz[rows].astype(F32)).astype(BF)

                    self.tiles(self.sl, add)
                    self.keep.start()
                    for x in self.spread:
                        x.start()
                    self.core[0].start()

            def relay(self):
                @pl.when(not_sw)
                def _():
                    for x, y in zip(self.spread, self.core[1:]):
                        x.recv()
                        y.start()

            def done(self):
                for x in self.to:
                    x.sent()

                @pl.when(is_sw)
                def _():
                    self.zx.sent()
                    for x in self.core:
                        x.recv()

                @pl.when(not_sw)
                def _():
                    self.keep.wait()
                    for x in self.spread + self.core:
                        x.sent()

        redS, redO, redC, redG, redH = (Reduce(name) for name in "SOCGH")

        bar = pltpu.get_barrier_semaphore()
        for dev in [sib, zp, z2] + peers[1:]:
            pl.semaphore_signal(bar, inc=1, device_id={"dp": dev[0], "mp": dev[1]}, device_id_type=MESH)

        @pl.when(is_sw)
        def _():
            pl.semaphore_signal(bar, inc=1, device_id={"dp": mate[0], "mp": mate[1]}, device_id_type=MESH)

        pl.semaphore_wait(bar, 2 + d.nd + sw)

        for x in sx:
            x.start()
        for x in qkv3:
            x.start()
        turns = D // 128
        loads = [Local(ff_ref.at[pl.ds(i * 1024, 1024)], v.ffb.at[i % 2]) for i in range(turns)]
        loads[0].start()

        def first_norm():
            for h in range(PARTS):
                sx[h].wait()
                rows = pl.ds(h * HR, HR)
                v.h1f[t, rows] = norm_fwd(v.xb[rows].astype(F32), gain(0))
                ag1.send(h)

        pl.when(not_sw)(first_norm)

        pos = lax.broadcasted_iota(jnp.int32, (1, 4 * R), 1)
        dist = jnp.where(pos < 2 * R, pos, jnp.where(pos < 3 * R, pos - R, pos - 3 * R))
        onehot = jnp.where(lax.broadcasted_iota(jnp.int32, (NB, 4 * R), 0) == bucket_index(dist), 1.0, 0.0).astype(BF)
        lines = dot_nn(tab_ref[...], onehot)
        v.aux0[...] = jnp.zeros(v.aux0.shape, F32)
        v.aux0[pl.ds(0, 1)] = jnp.where(pos < dlen_ref[...], 0.0, MASK_FILL)
        v.aux0[pl.ds(1, 1)] = jnp.where(pos < elen_ref[...], 0.0, MASK_FILL)
        v.aux0[pl.ds(2, nh)] = jnp.where((pos >= R) & (pos < 2 * R), MASK_FILL, lines)
        v.aux0[pl.ds(2 + nh, nh)] = jnp.broadcast_to(lines[:, 2 * R : 2 * R + 1], (nh, 4 * R))
        saux.start()

        def turn(i):
            loads[i].wait()
            if i + 1 < turns:
                loads[i + 1].start()
            v.ffs[...] = v.ffb[i % 2].astype(F32)
            for j in range(8):
                part = v.ffs[pl.ds(j, 128, stride=8)]
                v.gsend[pl.ds((j % 2) * F + (j // 2) * 128, 128), pl.ds(i * 128, 128)] = jnp.transpose(part).astype(BF)

        for i in range(turns):
            turn(i)

        pl.when(is_sw)(first_norm)
        weights["so"].start()
        senc.start()
        for name in ("ckv", "cq", "co"):
            weights[name].start()
        for x in qkv3:
            x.forward()
        saux.wait()

        row16 = lax.broadcasted_iota(jnp.int32, (PADH, R), 0)
        ones_row = jnp.where(row16 == 0, 1.0, 0.0).astype(BF)

        def mask_rows(row, b):
            line = v.aux[pl.ds(row, 1), pl.ds(b * R, R)]
            return jnp.where(row16 == 0, jnp.broadcast_to(line, (PADH, R)), 0.0).astype(BF)

        for b in range(4):
            for h in range(nh):
                v.qa[b, h, pl.ds(hd, PADH)] = ones_row
                v.q2a[b // 2, b % 2, h, pl.ds(hd, PADH)] = ones_row
                v.ka[b, h, pl.ds(hd, PADH)] = mask_rows(0, b)
        for b in range(d.ne):
            for h in range(nh):
                v.k2a[b, h, pl.ds(hd, PADH)] = mask_rows(1, b)
        for h in range(nh):
            for i in range(2):
                line = v.aux[pl.ds(2 + h, 1), pl.ds(i * 2 * R, 2 * R)]
                v.bias[h, i] = pltpu.roll(jnp.broadcast_to(line, (R, 2 * R)), 0, 1, stride=1, stride_axis=0)[:, :R]
            v.bias[h, 2] = jnp.broadcast_to(v.aux[pl.ds(2 + nh + h, 1), pl.ds(0, R)], (R, R))

        @pl.when(is_sw)
        def _():
            ag1.near()
            ag1.far()

        for x in qkv3:
            x.wait()

        def project_self(b):
            qkv = dot_nt(W("qkv"), v.h1f[b]).astype(BF)
            for h in range(nh):
                v.qa[b, h, pl.ds(0, hd)] = qkv[h * hd : (h + 1) * hd]
                v.ka[b, h, pl.ds(0, hd)] = qkv[hc + h * hd : hc + (h + 1) * hd]
            v.vT[b] = qkv[2 * hc :]

        def project_step(k, carry):
            pl.when((k == 1) & not_sw)(ag1.near)
            pl.when((k == 2) & not_sw)(ag1.far)
            pl.when(k == 3)(ag1.last)
            pl.when(k == 2)(weights["so"].forward)
            project_self(blk_ag(k))
            return carry

        lax.fori_loop(0, 4, project_step, 0)
        senc.wait()
        agenc.send(0)

        def feat(h):
            return pl.ds(h * hd, hd)

        def attend_self(b):
            qs = [v.qa[b, h] for h in range(nh)]

            def block(j, state):
                out = []
                for h in range(nh):
                    m, total, acc = state[h]
                    s = dot_tn(v.ka[j, h], qs[h]) + v.bias[h, jnp.minimum(b - j, 2)]
                    new = jnp.maximum(m, jnp.max(s, axis=0, keepdims=True))
                    p = jnp.exp(s - new)
                    scale = jnp.exp(m - new)
                    total = total * scale + jnp.sum(p, axis=0, keepdims=True)
                    out.append((new, total, acc * scale + dot_nn(v.vT[j, feat(h)], p.astype(BF))))
                return tuple(out)

            first = (jnp.full((1, R), -1e30, F32), jnp.zeros((1, R), F32), jnp.zeros((hd, R), F32))
            state = lax.fori_loop(0, b + 1, block, (first,) * nh)
            for h in range(nh):
                m, total, acc = state[h]
                v.o1[b, feat(h)] = (acc / total).astype(BF)
                v.lse1[b, pl.ds(h, 1)] = m + jnp.log(total)

        def attend_cross(i, j):
            for h in range(nh):
                q = v.q2a[i, j, h]
                s = [dot_tn(v.k2a[e, h], q) for e in range(d.ne)]
                m = jnp.max(s[0], axis=0, keepdims=True)
                for part in s[1:]:
                    m = jnp.maximum(m, jnp.max(part, axis=0, keepdims=True))
                p = [jnp.exp(part - m) for part in s]
                total = sum(jnp.sum(part, axis=0, keepdims=True) for part in p)
                acc = sum(dot_nn(v.v2T[e, feat(h)], part.astype(BF)) for e, part in enumerate(p))
                v.o2[i, j, feat(h)] = (acc / total).astype(BF)
                v.lse2[i, j, pl.ds(h, 1)] = m + jnp.log(total)

        def tile_back(h, q, k, vals, da, inner, logsum, bias):
            s = dot_tn(k, q)
            if bias is not None:
                s = s + bias
            p = jnp.exp(s - logsum)
            ds = p * (dot_tn(vals, da) - inner)
            return p.astype(BF), ds, ds.astype(BF)

        def head_back(h, q, out, lse):
            da = v.da[feat(h)]
            inner = jnp.sum(da.astype(F32) * out.astype(F32), axis=0, keepdims=True)
            return q, da, inner, lse

        def attend_self_back(b):
            heads = [head_back(h, v.qa[b, h], v.o1[b, feat(h)], v.lse1[b, pl.ds(h, 1)]) for h in range(nh)]

            def block(j, dqs):
                kind = jnp.minimum(b - j, 2)
                out = []
                for h in range(nh):
                    q, da, inner, logsum = heads[h]
                    k = v.ka[j, h]
                    p, ds, low = tile_back(h, q, k, v.vT[j, feat(h)], da, inner, logsum, v.bias[h, kind])
                    v.dka[j, h] += dot_nt(q, low)
                    v.dva[j, feat(h)] += dot_nt(da, p)
                    v.dsacc[h, kind] += ds
                    out.append(dqs[h] + dot_nn(k, low))
                return tuple(out)

            dqs = lax.fori_loop(0, b + 1, block, (jnp.zeros((ha, R), F32),) * nh)
            for h in range(nh):
                v.dqkvT[b, feat(h)] = dqs[h][:hd].astype(BF)

        def attend_cross_back(i, j):
            for h in range(nh):
                q, da, inner, logsum = head_back(h, v.q2a[i, j, h], v.o2[i, j, feat(h)], v.lse2[i, j, pl.ds(h, 1)])
                dq = jnp.zeros((ha, R), F32)
                for e in range(d.ne):
                    k = v.k2a[e, h]
                    p, ds, low = tile_back(h, q, k, v.v2T[e, feat(h)], da, inner, logsum, None)
                    v.dka[e, h] += dot_nt(q, low)
                    v.dva[e, feat(h)] += dot_nt(da, p)
                    dq = dq + dot_nn(k, low)
                v.dq2T[i, j, feat(h)] = dq[:hd].astype(BF)

        def self_forward(k, carry):
            b = blk_rs(k)
            attend_self(b)
            pl.when(k == 0)(weights["so"].wait)
            v.pb[...] = dot_tn(v.o1[b], W("so"))
            rs1.emit(k)
            pl.when(k == 1)(scot.start)
            pl.when(k == 1)(agenc.near)
            pl.when(k == 1)(agenc.far)
            for name in ("ckv", "cq", "co"):
                pl.when(k == 2)(weights[name].forward)
            return carry

        lax.fori_loop(0, 4, self_forward, 0)
        agenc.last()
        weights["ckv"].wait()
        per = R // E
        for b in range(4):
            lanes = pl.ds((b % per) * E, E)
            kv = dot_nt(W("ckv"), v.encf[b]).astype(BF)
            for h in range(nh):
                v.k2a[b // per, h, pl.ds(0, hd), lanes] = kv[h * hd : (h + 1) * hd]
            v.v2T[b // per, :, lanes] = kv[hc:]

        def fin1(h, rows, total):
            x1 = v.xb[rows].astype(F32) + total
            v.x1[rows] = x1
            v.h2f[h, a, pl.ds(pl.multiple_of(c * HR, HR), HR)] = norm_fwd(x1, gain(1))
            ag2.send(h)

        for h in range(2):
            rs1.finish(h, fin1)
        for name in ("gu", "fo"):
            weights[name].start()

        weights["cq"].wait()
        weights["co"].wait()

        def cross_block(i, j):
            q = dot_nt(W("cq"), v.h2f[i, j]).astype(BF)
            for h in range(nh):
                v.q2a[i, j, h, pl.ds(0, hd)] = q[h * hd : (h + 1) * hd]
            attend_cross(i, j)

        def send_cot(h):
            pl.when(h == 0)(scot.wait)
            rows = pl.ds(pl.multiple_of(h * HR, HR), HR)
            v.d3f[h, a, pl.ds(pl.multiple_of(c * HR, HR), HR)] = v.cotb[rows]
            agd3.send(h)

        rs1.sent()
        halves(ag2, cross_block, rs2, lambda i, j: dot_tn(v.o2[i, j], W("co")), send_cot)
        for name in ("gu", "fo"):
            weights[name].forward()

        def fin2(h, rows, total):
            x2 = v.x1[rows] + total
            v.x2[rows] = x2
            v.h3f[h, a, pl.ds(pl.multiple_of(c * HR, HR), HR)] = norm_fwd(x2, gain(2))
            ag3.send(h)

        for h in range(2):
            rs2.finish(h, fin2)
        for h in range(2):
            agd3.near(h)
            agd3.pass_on(h)
        for h in range(2):
            agd3.last(h)
        for name in ("gu", "fo"):
            weights[name].wait()

        fc = 64

        def hidden_block(i, j):
            rows = v.h3f[i, j]
            v.gus[pl.ds(0, F)] = dot_nt(W("gu", 0, F), rows)
            v.gus[pl.ds(F, F)] = dot_nt(W("gu", F, F), rows)
            v.gus[pl.ds(2 * F, F)] = dot_nt(W("fo"), v.d3f[i, j])

            def chunk(n, carry):
                r = pl.multiple_of(n * fc, fc)
                gate, up, dact = (v.gus[pl.ds(m * F + r, fc)] for m in range(3))
                sq = gate * gate
                th = jnp.tanh(gate * (GELU_C + (GELU_C * 0.044715) * sq))
                half = 0.5 + 0.5 * th
                gelu = gate * half
                slope = half + gate * (0.5 - 0.5 * th * th) * (GELU_C + (3.0 * GELU_C * 0.044715) * sq)
                v.actT[i, j, pl.ds(r, fc)] = (gelu * up).astype(BF)
                v.dguT[i, j, pl.ds(r, fc)] = (dact * up * slope).astype(BF)
                v.dguT[i, j, pl.ds(F + r, fc)] = (dact * gelu).astype(BF)
                return carry

            lax.fori_loop(0, F // fc, chunk, 0)

        rs2.sent()
        halves(ag3, hidden_block, rs3, lambda i, j: dot_tn(v.dguT[i, j], W("gu")))

        def grads(at, lhs, rows, rhs, tile):
            spots = [(b,) for b in range(4)] if len(lhs.shape) == 3 else [(b // 2, b % 2) for b in range(4)]

            def step(i, carry):
                r = pl.multiple_of(i * tile, 64)
                total = None
                for spot in spots:
                    part = dot_nn(lhs[spot + (pl.ds(r, tile),)], rhs[spot])
                    total = part if total is None else total + part
                v.gf[pl.ds(at + r, tile)] = total
                return carry

            lax.fori_loop(0, rows // tile, step, 0)

        def loc(name, group):
            base, _, at, _ = d.groups[group]
            return d.w[name][0] - base + at

        def add_gain(i, h, part):
            if h == 0:
                v.smc[pl.ds(i, 1)] = part
            else:
                v.smc[pl.ds(i, 1)] += part

        v.smc[...] = jnp.zeros(v.smc.shape, F32)

        def fin3(h, rows, total):
            grad, part = norm_bwd(v.x2[rows], gain(2), total)
            add_gain(2, h, part)
            g2 = v.cotb[rows].astype(F32) + grad
            v.gb[rows] = g2
            v.d2f[h, a, pl.ds(pl.multiple_of(c * HR, HR), HR)] = g2.astype(BF)
            agd2.send(h)

        rs3.finish(0, fin3)
        grads(loc("gu", "G"), v.dguT, 2 * F, v.h3f, 256)
        pl.when(is_sw)(weights["gu"].far.sent)
        redG.send()

        def hidden_out(h, carry):
            rso.emit_pair(h, lambda i, j: dot_tn(v.actT[i, j], W("fo")), kick=False)
            return carry

        lax.fori_loop(0, 2, hidden_out, 0)
        rs3.finish(1, fin3)
        grads(loc("fo", "H"), v.actT, F, v.d3f, 256)
        redH.send()
        rso.kick()

        v.dka[...] = jnp.zeros(v.dka.shape, F32)
        v.dva[...] = jnp.zeros(v.dva.shape, F32)

        def cross_back_block(i, j):
            v.da[...] = dot_nt(W("co"), v.d2f[i, j]).astype(BF)
            attend_cross_back(i, j)

        rs3.sent()
        halves(agd2, cross_back_block, rs4, lambda i, j: dot_tn(v.dq2T[i, j], W("cq")))

        def fin4(h, rows, total):
            grad, part = norm_bwd(v.x1[rows], gain(1), total)
            add_gain(1, h, part)
            g1 = v.gb[rows] + grad
            v.gb[rows] = g1
            v.d1f[t, rows] = g1.astype(BF)
            agd1.send(h)

        for b in range(4):
            lanes = pl.ds((b % per) * E, E)
            for h in range(nh):
                v.dkv2T[b, pl.ds(h * hd, hd)] = v.dka[b // per, h, pl.ds(0, hd), lanes].astype(BF)
            v.dkv2T[b, pl.ds(hc, hc)] = v.dva[b // per, :, lanes].astype(BF)

        def enc_part(b):
            v.epb[...] = dot_tn(v.dkv2T[b], W("ckv"))

        rse.loop(enc_part, kick=False)
        grads(loc("cq", "C"), v.dq2T, hc, v.h2f, hc)
        grads(loc("co", "C"), v.o2, hc, v.d2f, hc)
        grads(loc("ckv", "C"), v.dkv2T, 2 * hc, v.encf, hc)
        redC.send()
        rs4.finish(0, fin4)

        def fin_out(h, rows, total):
            v.lov[rows] = (v.x2[rows] + total).astype(BF)

        for h in range(2):
            rso.finish(h, fin_out)
        rs4.finish(1, fin4)


        v.dka[...] = jnp.zeros(v.dka.shape, F32)
        v.dva[...] = jnp.zeros(v.dva.shape, F32)
        v.dsacc[...] = jnp.zeros(v.dsacc.shape, F32)

        def self_back(k, carry):
            b = blk_ag(k)
            agd1.arrive(k)
            pl.when(k == 1)(redG.combine)
            pl.when(k == 3)(rse.kick)
            pl.when(k == 2)(out_lo.start)
            pl.when(k == 3)(redH.combine)

            @pl.when(k == 3)
            def _():
                grads(loc("so", "O"), v.o1, hc, v.d1f, hc)
                redO.send()

            v.da[...] = dot_nt(W("so"), v.d1f[b]).astype(BF)
            attend_self_back(b)
            return carry

        lax.fori_loop(0, 4, self_back, 0)

        for b in range(4):
            for h in range(nh):
                v.dqkvT[b, pl.ds(hc + h * hd, hd)] = v.dka[b, h, pl.ds(0, hd)].astype(BF)
            v.dqkvT[b, pl.ds(2 * hc, hc)] = v.dva[b].astype(BF)
        grads(loc("qkv", "S"), v.dqkvT, 3 * hc, v.h1f, hc)
        redS.send()

        def self_qkv_part(b):
            v.pb[...] = dot_tn(v.dqkvT[b], W("qkv"))

        rs4.sent()
        rs5.loop(self_qkv_part)
        redC.combine()
        redO.combine()
        redG.finish()
        redH.finish()

        def fin_enc(h, rows, total):
            v.egv[rows] = total.astype(BF)


        iota0 = lax.broadcasted_iota(jnp.int32, (R, R), 0)
        iota1 = lax.broadcasted_iota(jnp.int32, (R, R), 1)
        flip = (iota0 + iota1 == R - 1).astype(F32)

        def diagonals(h, i):
            turned = lax.dot_general(
                flip, v.dsacc[h, i], (((1,), (0,)), ((), ())), precision=lax.Precision.HIGHEST, preferred_element_type=F32
            )
            wide = jnp.concatenate([turned, jnp.zeros((R, R), F32)], axis=1)
            return jnp.sum(pltpu.roll(wide, 0, 1, stride=1, stride_axis=0), axis=0, keepdims=True)

        lane = lax.broadcasted_iota(jnp.int32, (1, 2 * R), 1)
        for h in range(nh):
            near, off = diagonals(h, 0), diagonals(h, 1)
            far = jnp.sum(jnp.sum(v.dsacc[h, 2], axis=0, keepdims=True), axis=1, keepdims=True)
            off = off + jnp.where(lane == 2 * R - 1, far, 0.0)
            line = jnp.concatenate([pltpu.roll(near, R + 1, 1)[:, :R], off], axis=1)
            v.smc[pl.ds(3 + h, 1), pl.ds(0, 3 * R)] = line

        def fin5(h, rows, total):
            grad, part = norm_bwd(v.xb[rows].astype(F32), gain(0), total)
            add_gain(0, h, part)
            v.igv[rows] = (v.gb[rows] + grad).astype(BF)

        plane = peers[1:]
        first = [Xfer(v.sms.at[0], v.smr.at[i], dev) for i, dev in enumerate(plane)]
        rest = [Xfer(v.sms.at[1 + i], v.smr.at[3 + i], dev) for i, dev in enumerate([z2, zp, sib])]
        redS.combine()
        for h in range(2):
            rs5.finish(h, fin5)
        v.sms[0] = v.smc[...]
        for x in first:
            x.start()
        for x in out_ig:
            x.start()
        redS.finish()
        for x in first:
            x.recv()
        if len(plane) == 3:
            v.sms[1] = (v.sms[0] + v.smr[0]) + (v.smr[1] + v.smr[2])
        elif len(plane) == 1:
            v.sms[1] = v.sms[0] + v.smr[0]
        else:
            v.sms[1] = v.sms[0]
        rest[0].start()
        redC.finish()
        redO.finish()
        rest[0].recv()
        v.sms[2] = v.sms[1] + v.smr[3]
        v.smc[...] = v.sms[2]
        rest[1].start()
        rse.finish(0, fin_enc)
        out_eg.start()
        redG.relay()
        redH.relay()
        rest[1].recv()
        only = lax.broadcasted_iota(jnp.int32, v.smc.shape, 0) < 3
        v.sms[3] = jnp.where(only, v.sms[2] + v.smr[4], v.sms[2])
        rest[2].start()
        redC.relay()
        redO.relay()
        redS.relay()
        rest[2].recv()
        total = v.sms[3] + v.smr[5]
        table_rows = jnp.where(is_sw, v.smr[5], v.smc[...])
        sm_ref[...] = jnp.where(only, total, table_rows)

        for x in first + rest:
            x.sent()
        for x in (ag1, ag2, ag3, agd1, agd2, agd3, agenc, rs5, rso, rse):
            x.sent()
        for x in [saux, scot, senc] + sx:
            x.sent()
        for name, x in weights.items():
            x.sent(name != "gu")
        for x in qkv3:
            x.sent()
        for x in [out_lo, out_eg] + out_ig:
            x.wait()
            x.sent()
        for r in (redG, redH, redC, redO, redS):
            r.done()

    return kernel


def unpack(d, gw, lo, ig, eg, sm):
    R, D, F, hc, nh, E = d.R, d.D, d.F, d.hc, d.nh, d.E
    steps = 3
    cols = D // steps

    def kernel(gu_ref, fo_ref, qkv_ref, so_ref, ckv_ref, cq_ref, co_ref, lo_ref, ig_ref, eg_ref, sm_ref, *outs):
        lo_out, ig_out, eg_out, gu_out, fo_out, qkv_out, so_out, ckv_out, cq_out, co_out, gains_out, table_out = outs
        for j in range(2 * F // 128):
            part = jnp.transpose(gu_ref[pl.ds((j % 2) * F + (j // 2) * 128, 128)].astype(F32))
            gu_out[pl.ds(j, cols, stride=2 * F // 128)] = part
        for src, dst in (
            (fo_ref, fo_out), (qkv_ref, qkv_out), (so_ref, so_out), (ckv_ref, ckv_out), (cq_ref, cq_out), (co_ref, co_out)
        ):
            dst[...] = src[...].astype(F32)

        @pl.when(pl.program_id(0) == 0)
        def _():
            lo_out[...] = lo_ref[...]
            ig_out[...] = ig_ref[...].astype(F32)
            eg_out[...] = eg_ref[...].astype(F32)
            gains_out[...] = sm_ref[pl.ds(0, 3)]
            col = lax.broadcasted_iota(jnp.int32, (1, D), 1)
            dist = jnp.where(col < R, col, jnp.where(col < 3 * R - 1, col - R + 1, 4 * R))
            pick = (lax.broadcasted_iota(jnp.int32, (NB, D), 0) == bucket_index(dist)).astype(F32)
            mine = sm_ref[pl.ds(3, nh)]
            table_out[...] = lax.dot_general(
                mine, pick, (((1,), (1,)), ((), ())), precision=lax.Precision.HIGHEST, preferred_element_type=F32
            )

    at = lambda name: d.w[name][0]
    rows = lambda name, n: pl.BlockSpec((n, D), lambda i: (at(name) // n + i, 0))
    out_rows = lambda n: pl.BlockSpec((n, D), lambda i: (i, 0))
    whole = lambda *shape: pl.BlockSpec(shape, lambda i: (0,) * len(shape))
    third = {name: d.w[name][1] // steps for name in ("qkv", "so", "ckv", "cq", "co")}
    half = F // 2
    assert all(at(name) % n == 0 for name, n in third.items()) and at("fo") % half == 0 and at("gu") == 0
    shape = lambda *dims: jax.ShapeDtypeStruct(dims, F32)
    return pl.pallas_call(
        kernel,
        grid=(steps,),
        in_specs=[
            pl.BlockSpec((2 * F, cols), lambda i: (0, i)),
            pl.BlockSpec((half, D), lambda i: (at("fo") // half + jnp.minimum(i, 1), 0)),
        ]
        + [rows(name, n) for name, n in third.items()]
        + [whole(R, D), whole(R, D), whole(E, D), whole(d.small, D)],
        out_specs=[
            whole(R, D), whole(R, D), whole(E, D),
            pl.BlockSpec((cols * 2 * F // 128, 128), lambda i: (i, 0)),
            pl.BlockSpec((half, D), lambda i: (jnp.minimum(i, 1), 0)),
        ]
        + [out_rows(n) for n in third.values()]
        + [whole(3, D), whole(nh, NB)],
        out_shape=[
            jax.ShapeDtypeStruct((R, D), BF), shape(R, D), shape(E, D), shape(D * 2 * F // 128, 128), shape(F, D),
            shape(3 * hc, D), shape(hc, D), shape(2 * hc, D), shape(hc, D), shape(hc, D), shape(3, D), shape(nh, NB),
        ],
        compiler_params=pltpu.CompilerParams(vmem_limit_bytes=63 << 20),
    )(*[gw] * 7, lo, ig, eg, sm)


def local_fn(mesh):
    def local(x_in, enc_in, cotangent, dec_len, enc_len, self_qkv, self_out, cross_q, cross_kv, cross_out, ff_in, ff_out, gains, table):
        d = make_dims(mesh, x_in, enc_in, self_qkv, ff_in, table)
        R, D, hc, nh, F = d.R, d.D, d.hc, d.nh, d.F
        hbm = pl.BlockSpec(memory_space=pl.ANY)
        vmem = pl.BlockSpec(memory_space=pltpu.VMEM)
        ws = {
            "qkv": jnp.transpose(self_qkv, (1, 2, 0)).reshape(3 * hc, D),
            "so": self_out,
            "cq": jnp.transpose(cross_q),
            "ckv": jnp.transpose(cross_kv, (1, 2, 0)).reshape(2 * hc, D),
            "co": cross_out,
            "gu": jnp.transpose(ff_in.reshape(D, 2, F // 128, 128), (0, 2, 1, 3)).reshape(D * 2 * F // 128, 128),
            "fo": ff_out,
        }
        outs = pl.pallas_call(
            build_kernel(d),
            out_shape=(
                jax.ShapeDtypeStruct((R, D), BF),
                jax.ShapeDtypeStruct((R, D), BF),
                jax.ShapeDtypeStruct((d.E, D), BF),
                jax.ShapeDtypeStruct((d.rows, D), BF),
                jax.ShapeDtypeStruct((d.small, D), F32),
            ),
            in_specs=[hbm, hbm, hbm, vmem, vmem, vmem, vmem] + [hbm] * len(d.w),
            out_specs=(hbm, hbm, hbm, hbm, vmem),
            scratch_shapes=[pltpu.VMEM(shape, dtype) for _, shape, dtype in scratch_list(d)]
            + [pltpu.SemaphoreType.DMA((SEMS,))] * 3,
            compiler_params=pltpu.CompilerParams(collective_id=0, has_side_effects=True, vmem_limit_bytes=63 << 20),
        )(x_in, enc_in, cotangent, jnp.transpose(table), dec_len.reshape(1, 1), enc_len.reshape(1, 1), gains, *[ws[name] for name in d.w])
        lo, ig, eg, gw, sm = outs
        others = d.ndp // (2 * d.nd)
        if others > 1:
            gw, sm = lax.psum((gw.astype(F32), sm), "dp")
            gw, sm = gw * (1.0 / (2 * d.nd)), sm * (1.0 / (2 * d.nd))
        res = unpack(d, gw, lo, ig, eg, sm)
        gu = jnp.transpose(res[3].reshape(D, F // 128, 2, 128), (0, 2, 1, 3)).reshape(D, 2, F)
        return (
            res[0],
            res[1],
            res[2],
            jnp.transpose(res[5].reshape(3, hc, D), (2, 0, 1)),
            res[6],
            jnp.transpose(res[8]),
            jnp.transpose(res[7].reshape(2, hc, D), (2, 0, 1)),
            res[9],
            gu,
            res[4],
            res[10],
            jnp.transpose(res[11]),
        )

    return local


def solution(mesh):
    rows = P(("dp", "mp"), None)
    in_specs = (
        rows, rows, rows, P("dp"), P("dp"), P(None, None, "mp"), P("mp", None), P(None, "mp"), P(None, None, "mp"),
        P("mp", None), P(None, None, "mp"), P("mp", None), P(), P(None, "mp"),
    )
    out_specs = (
        rows, rows, rows, P(None, None, "mp"), P("mp", None), P(None, "mp"), P(None, None, "mp"), P("mp", None),
        P(None, None, "mp"), P("mp", None), P(), P(None, "mp"),
    )
    return jax.shard_map(local_fn(mesh), mesh=mesh, in_specs=in_specs, out_specs=out_specs, check_vma=False)
```

```python
import math

import jax
import jax.numpy as jnp
from jax import lax
from jax.experimental import pallas as pl
from jax.experimental.pallas import tpu as pltpu
from jax.sharding import PartitionSpec as P

NB = 32
MAXD = 128
NORM_EPS = 1e-06
MASK_FILL = -1000000000.0
MESH = pl.DeviceIdType.MESH
BF = jnp.bfloat16
F32 = jnp.float32
PARTS = 2
PADH = 16
GELU_C = math.sqrt(2.0 / math.pi)
SEMS = 256


def bucket_index(distance):
    half_count = NB // 2
    clipped = jnp.maximum(distance, 0)
    bucket_ids = jnp.minimum(clipped, half_count)
    for level_pos in range(1, half_count):
        threshold = math.ceil(half_count * (MAXD / half_count) ** (level_pos / half_count))
        bucket_ids = bucket_ids + (clipped >= threshold).astype(jnp.int32)
    return bucket_ids


def dot_nn(a, b):
    return lax.dot_general(a, b, (((1,), (0,)), ((), ())), preferred_element_type=F32)


def dot_nt(a, b):
    return lax.dot_general(a, b, (((1,), (1,)), ((), ())), preferred_element_type=F32)


def dot_tn(a, b):
    return lax.dot_general(a, b, (((0,), (0,)), ((), ())), preferred_element_type=F32)


def norm_fwd(v, g):
    inv = lax.rsqrt(jnp.mean(v * v, axis=-1, keepdims=True) + NORM_EPS)
    return (v * inv * g).astype(BF)


def norm_bwd(v, g, u):
    inv = lax.rsqrt(jnp.mean(v * v, axis=-1, keepdims=True) + NORM_EPS)
    gu = u * g
    mean = jnp.mean(gu * v, axis=-1, keepdims=True)
    grad = inv * gu - v * (inv * inv * inv * mean)
    gain = jnp.sum(u * v * inv, axis=0, keepdims=True)
    return grad, gain


class Dims:
    pass


def make_dims(mesh, x_in, enc_in, self_qkv, ff_in, table):
    d = Dims()
    d.ndp, d.nmp = mesh.shape["dp"], mesh.shape["mp"]
    d.nd = min(4, d.ndp // 2)
    d.R, d.D = x_in.shape
    d.E = enc_in.shape[0]
    d.nh = table.shape[1]
    d.hc = self_qkv.shape[2]
    d.hd = d.hc // d.nh
    d.F = ff_in.shape[2]
    d.ha = d.hd + PADH
    d.ne = 4 * d.E // d.R
    d.axr = -(-(2 + 2 * d.nh) // 8) * 8
    hc, F = d.hc, d.F
    names = (("gu", 2 * F), ("fo", F), ("qkv", 3 * hc), ("so", hc), ("ckv", 2 * hc), ("cq", hc), ("co", hc))
    d.w, at = {}, 0
    for name, rows in names:
        d.w[name] = (at, rows)
        at += rows
    d.rows = at
    s, c = 3 * hc, 4 * hc
    d.groups = {}
    land = 0
    for name, base, rows in (("G", 0, 2 * F), ("H", 2 * F, F), ("S", 3 * F, s), ("O", 3 * F + s, hc), ("C", 3 * F + s + hc, c)):
        d.groups[name] = (base, rows, 0, land)
        land += rows // d.nd
    d.land = land
    d.locrows = max(s, c, 2 * F)
    d.small = -(-(3 + d.nh) // 8) * 8
    return d


def scratch_list(d):
    R, D, hc, nh, hd, ha, F, E = d.R, d.D, d.hc, d.nh, d.hd, d.ha, d.F, d.E
    full = ((4, R, D), BF)
    pair = ((2, 2, R, D), BF)
    HR = R // 2
    return [
        ("xb", (R, D), BF), ("cotb", (R, D), BF), ("aux", (d.axr, 4 * R), F32), ("aux0", (d.axr, 4 * R), F32), ("ffb", (2, 1024, 128), BF), ("ffs", (1024, 128), F32), ("wv", (d.rows, D), BF),
        ("h1f",) + full, ("h2f",) + pair, ("h3f",) + pair, ("d3f",) + pair, ("d2f",) + pair, ("d1f",) + full,
        ("encf", (4, E, D), BF),
        ("qa", (4, nh, ha, R), BF), ("ka", (4, nh, ha, R), BF), ("vT", (4, hc, R), BF), ("o1", (4, hc, R), BF),
        ("q2a", (2, 2, nh, ha, R), BF), ("k2a", (d.ne, nh, ha, R), BF), ("v2T", (d.ne, hc, R), BF), ("o2", (2, 2, hc, R), BF),
        ("lse1", (4, 8, R), F32), ("lse2", (2, 2, 8, R), F32),
        ("bias", (nh, 3, R, R), F32), ("dsacc", (nh, 3, R, R), F32),
        ("x1", (R, D), F32), ("x2", (R, D), F32), ("gb", (R, D), F32),
        ("pb", (R, D), F32), ("pf", (R, D), F32), ("sb", (2, 3, HR, D), BF), ("rb", (2, 3, HR, D), BF),
        ("opb", (R, D), F32), ("osb", (2, 3, HR, D), BF), ("orb", (2, 3, HR, D), BF), ("lov", (R, D), BF), ("igv", (R, D), BF),
        ("epb", (E, D), F32), ("esb", (1, 3, E, D), BF), ("erb", (1, 3, E, D), BF), ("egv", (E, D), BF),
        ("actT", (2, 2, F, R), BF), ("dguT", (2, 2, 2 * F, R), BF), ("gus", (3 * F, R), F32),
        ("da", (hc, R), BF), ("dqkvT", (4, 3 * hc, R), BF), ("dq2T", (2, 2, hc, R), BF), ("dkv2T", (4, 2 * hc, E), BF),
        ("dka", (4, nh, ha, R), F32), ("dva", (4, hc, R), F32),
        ("gf", (d.locrows, D), F32), ("gsend", (d.rows, D), BF), ("grecv", (max(d.nd - 1, 1), d.land, D), BF),
        ("gz", (d.land, D), BF), ("gk", (d.land, D), F32), ("gfo", (d.land, D), BF),
        ("smc", (d.small, D), F32), ("sms", (4, d.small, D), F32), ("smr", (7, d.small, D), F32),
    ]


def build_kernel(d):
    R, D, hc, nh, hd, ha, F, E = d.R, d.D, d.hc, d.nh, d.hd, d.ha, d.F, d.E
    names = [item[0] for item in scratch_list(d)]
    wnames = list(d.w)
    HR = R // PARTS

    def kernel(*refs):
        x_ref, e_ref, cot_ref, tab_ref, dlen_ref, elen_ref, gains_ref = refs[:7]
        w_refs = dict(zip(wnames, refs[7 : 7 + len(wnames)]))
        lo_ref, ig_ref, eg_ref, gout_ref, sm_ref = refs[7 + len(wnames) : 12 + len(wnames)]
        tail = refs[12 + len(wnames) :]
        v = Dims()
        for name, ref in zip(names, tail):
            setattr(v, name, ref)
        ss, rs, ls = tail[len(names) :]
        ff_ref = w_refs["gu"]
        w_refs["gu"] = v.gsend.at[pl.ds(0, 2 * F)]

        dp, z = lax.axis_index("dp"), lax.axis_index("mp")
        c, chip = dp % 2, dp // 2
        a, u = z % 2, z // 2
        t = a + 2 * c
        sw = c + u - 2 * c * u
        dl = chip % d.nd
        base_dp = (chip - dl) * 2
        sib = (dp + 1 - 2 * c, z)
        zp = (dp, z + 1 - 2 * a)
        z2 = (dp, z + 2 - 4 * u)
        mate = (2 * chip + u, a + 2 * c)
        d0, d1 = dl % 2, dl // 2
        flips = [dl, dl + 1 - 2 * d0, dl + 2 - 4 * d1, 3 - dl][: d.nd]
        peers = [(base_dp + 2 * f + c, z) for f in flips]
        is_sw, not_sw = sw == 1, sw == 0

        count = [0]

        def new_id():
            count[0] += 1
            assert count[0] <= SEMS
            return count[0] - 1

        class Xfer:
            def __init__(self, src, dst, dev, i=None):
                self.i, self.src, self.dst, self.dev = new_id() if i is None else i, src, dst, dev

            def desc(self):
                return pltpu.make_async_remote_copy(
                    src_ref=self.src, dst_ref=self.dst, send_sem=ss.at[self.i], recv_sem=rs.at[self.i],
                    device_id={"dp": self.dev[0], "mp": self.dev[1]}, device_id_type=MESH,
                )

            def start(self):
                self.desc().start()

            def recv(self):
                self.desc().wait_recv()

            def sent(self):
                self.desc().wait_send()

        class Local:
            def __init__(self, src, dst):
                self.i, self.src, self.dst = new_id(), src, dst

            def desc(self):
                return pltpu.make_async_copy(self.src, self.dst, ls.at[self.i])

            def start(self):
                self.desc().start()

            def wait(self):
                self.desc().wait()

        class Swap:
            def __init__(self, src, dst):
                self.far, self.near = Xfer(src, dst, mate), Local(src, dst)

            def start(self):
                pl.when(is_sw)(self.far.start)
                pl.when(not_sw)(self.near.start)

            def wait(self):
                pl.when(is_sw)(self.far.recv)
                pl.when(not_sw)(self.near.wait)

            def sent(self):
                pl.when(is_sw)(self.far.sent)

        class Weight:
            def __init__(self, name, piece=0, pieces=1):
                first, rows = d.w[name]
                rows = rows // pieces
                at = piece * rows
                first += at
                sl = rows // d.nd
                mine = pl.ds(pl.multiple_of(at + dl * sl, 16), sl)
                here = v.wv.at[pl.ds(pl.multiple_of(first + dl * sl, 16), sl)]
                self.near = Local(w_refs[name].at[pl.ds(at, rows)], v.wv.at[pl.ds(first, rows)])
                self.far = Xfer(w_refs[name].at[mine], here, mate)
                self.on = [Xfer(here, here, peer) for peer in peers[1:]]

            def start(self):
                pl.when(is_sw)(self.far.start)
                pl.when(not_sw)(self.near.start)

            def forward(self):
                @pl.when(is_sw)
                def _():
                    self.far.recv()
                    for x in self.on:
                        x.start()

            def wait(self):
                pl.when(not_sw)(self.near.wait)

                @pl.when(is_sw)
                def _():
                    for x in self.on:
                        x.recv()

            def sent(self, first=True):
                @pl.when(is_sw)
                def _():
                    if first:
                        self.far.sent()
                    for x in self.on:
                        x.sent()

        def blk_ag(k):
            k1, k2 = k % 2, k // 2
            return (a + k2 - 2 * a * k2) + 2 * (c + k1 - 2 * c * k1)

        def blk_rs(k):
            return blk_ag(3 - k)

        class Gather:
            def __init__(self, full, rows, parts):
                self.parts = parts
                n = rows // parts
                at = lambda b, h: full.at[b, pl.ds(h * n, n)]
                b_zp = (1 - a) + 2 * c
                self.z = [Xfer(at(t, h), at(t, h), zp) for h in range(parts)]
                self.c = [Xfer(at(t, h), at(t, h), sib) for h in range(parts)]
                self.f = [Xfer(at(b_zp, h), at(b_zp, h), sib) for h in range(parts)]

            def send(self, h):
                self.z[h].start()
                self.c[h].start()

            def near(self):
                for x in self.c:
                    x.recv()

            def far(self):
                for x, y in zip(self.z, self.f):
                    x.recv()
                    y.start()

            def last(self):
                for x in self.f:
                    x.recv()

            def arrive(self, k):
                pl.when(k == 1)(self.near)
                pl.when(k == 2)(self.far)
                pl.when(k == 3)(self.last)

            def sent(self):
                for x in self.z + self.c + self.f:
                    x.sent()

        class PairGather:
            def __init__(self, full):
                self.full, self.ids = full, [new_id() for _ in range(6)][0]

            def own(self, h):
                return self.full.at[h, a, pl.ds(pl.multiple_of(c * HR, HR), HR)]

            def z(self, h):
                return Xfer(self.own(h), self.own(h), zp, self.ids + h)

            def c(self, h):
                return Xfer(self.own(h), self.own(h), sib, self.ids + 2 + h)

            def f(self, h):
                there = self.full.at[h, 1 - a, pl.ds(pl.multiple_of(c * HR, HR), HR)]
                return Xfer(there, there, sib, self.ids + 4 + h)

            def send(self, h):
                self.z(h).start()
                self.c(h).start()

            def near(self, h):
                self.c(h).recv()

            def pass_on(self, h):
                self.z(h).recv()
                self.f(h).start()

            def last(self, h):
                self.f(h).recv()

            def sent(self):
                for h in range(2):
                    for x in (self.z(h), self.c(h), self.f(h)):
                        x.sent()

        class Scatter:
            def __init__(self, pb, sb, rb):
                self.pb, self.sb, self.rb = pb, sb, rb
                self.parts, self.n = sb.shape[0], sb.shape[2]
                self.ids = [new_id() for _ in range(3 * self.parts)][0]

            def rows(self, h):
                return pl.ds(h * self.n if isinstance(h, int) else pl.multiple_of(h * self.n, self.n), self.n)

            def x(self, slot, h, dev):
                return Xfer(self.sb.at[h, slot], self.rb.at[h, slot], dev, self.ids + slot * self.parts + h)

            def c0(self, h):
                return self.x(0, h, sib)

            def z(self, h):
                return self.x(1, h, zp)

            def c2(self, h):
                return self.x(2, h, sib)

            def emit(self, k, kick=True):
                @pl.when(k == 0)
                def _():
                    for h in range(self.parts):
                        self.sb[h, 0] = self.pb[self.rows(h)].astype(BF)
                        self.c0(h).start()

                @pl.when(k == 1)
                def _():
                    for h in range(self.parts):
                        self.c0(h).recv()
                        self.sb[h, 1] = (self.pb[self.rows(h)] + self.rb[h, 0].astype(F32)).astype(BF)
                        if kick:
                            self.z(h).start()

                @pl.when(k == 2)
                def _():
                    for h in range(self.parts):
                        self.sb[h, 2] = self.pb[self.rows(h)].astype(BF)
                        self.c2(h).start()

            def loop(self, partial, kick=True):
                def step(k, carry):
                    partial(blk_rs(k))
                    self.emit(k, kick)
                    return carry

                lax.fori_loop(0, 4, step, 0)

            def emit_pair(self, h, partial, kick=True):
                mine = pl.ds(pl.multiple_of(c * HR, HR), HR)
                other = pl.ds(pl.multiple_of((1 - c) * HR, HR), HR)
                v.pf[...] = partial(h, 1 - a)
                self.sb[h, 0] = v.pf[other].astype(BF)
                self.c0(h).start()
                self.sb[h, 1] = v.pf[mine].astype(BF)
                v.pf[...] = partial(h, a)
                self.sb[h, 2] = v.pf[other].astype(BF)
                self.c2(h).start()
                self.pb[self.rows(h)] = v.pf[mine]
                self.c0(h).recv()
                self.sb[h, 1] = (self.sb[h, 1].astype(F32) + self.rb[h, 0].astype(F32)).astype(BF)
                if kick:
                    self.z(h).start()

            def kick(self):
                for h in range(self.parts):
                    self.z(h).start()

            def finish(self, h, fin):
                self.c2(h).recv()
                self.z(h).recv()
                rows = self.rows(h)
                fin(h, rows, self.pb[rows] + self.rb[h, 2].astype(F32) + self.rb[h, 1].astype(F32))

            def sent(self):
                for h in range(self.parts):
                    for x in (self.c0(h), self.z(h), self.c2(h)):
                        x.sent()

        def ag_loop(gather, body):
            def step(k, carry):
                gather.arrive(k)
                body(blk_ag(k))
                return carry

            lax.fori_loop(0, 4, step, 0)

        def halves(gather, body, scatter, partial, after=None):
            def half(h, carry):
                def step(k, inner):
                    pl.when(k == 0)(lambda: gather.near(h))

                    @pl.when(k == 1)
                    def _():
                        gather.pass_on(h)
                        gather.last(h)

                    body(h, a + k - 2 * a * k)
                    return inner

                lax.fori_loop(0, 2, step, 0)
                scatter.emit_pair(h, partial)
                if after is not None:
                    after(h)
                return carry

            lax.fori_loop(0, 2, half, 0)

        def W(name, lo=0, rows=None):
            first, total = d.w[name]
            return v.wv[pl.ds(first + lo, total if rows is None else rows)]

        def gain(i):
            return gains_ref[pl.ds(i, 1)].astype(F32)

        sx = [Swap(x_ref.at[pl.ds(h * HR, HR)], v.xb.at[pl.ds(h * HR, HR)]) for h in range(PARTS)]
        saux, scot = Swap(v.aux0, v.aux), Swap(cot_ref, v.cotb)
        senc = Swap(e_ref, v.encf.at[z])
        weights = {name: Weight(name) for name in wnames if name != "qkv"}
        qkv3 = [Weight("qkv", i, 3) for i in range(3)]
        ag1, agd1 = (Gather(f, R, PARTS) for f in (v.h1f, v.d1f))
        ag2, ag3, agd3, agd2 = (PairGather(f) for f in (v.h2f, v.h3f, v.d3f, v.d2f))
        agenc = Gather(v.encf, E, 1)
        rs1, rs2, rs3, rs4, rs5 = (Scatter(v.pb, v.sb, v.rb) for _ in range(5))
        rso = Scatter(v.opb, v.osb, v.orb)
        rse = Scatter(v.epb, v.esb, v.erb)
        out_lo, out_eg = Swap(v.lov, lo_ref), Swap(v.egv, eg_ref)
        out_ig = [Swap(v.igv.at[pl.ds(h * HR, HR)], ig_ref.at[pl.ds(h * HR, HR)]) for h in range(PARTS)]

        class Reduce:
            def __init__(self, name):
                self.base, self.rows, self.loc, self.land = d.groups[name]
                self.sl = sl = self.rows // d.nd
                self.tile = 96 if sl % 96 == 0 else sl
                at = lambda f: pl.ds(pl.multiple_of(self.base + f * sl, 16), sl)
                here = pl.ds(self.land, sl)
                self.own = at(dl)
                self.to = [
                    Xfer(v.gsend.at[at(f)], v.grecv.at[k, here], peer)
                    for k, (f, peer) in enumerate(zip(flips[1:], peers[1:]))
                ]
                self.zx = Xfer(v.gsend.at[self.own], v.gz.at[here], z2)
                self.keep = Local(v.gfo.at[here], gout_ref.at[self.own])
                self.spread = [Xfer(v.gfo.at[here], gout_ref.at[self.own], peer) for peer in peers[1:]]
                self.core = [Xfer(v.gfo.at[here], gout_ref.at[self.own], sib)] + [
                    Xfer(gout_ref.at[at(f)], gout_ref.at[at(f)], sib) for f in flips[1:]
                ]

            def tiles(self, rows, body):
                def step(i, carry):
                    body(pl.multiple_of(i * self.tile, 16))
                    return carry

                lax.fori_loop(0, rows // self.tile, step, 0)

            def send(self):
                def cast(r):
                    v.gsend[pl.ds(self.base + r, self.tile)] = v.gf[pl.ds(self.loc + r, self.tile)].astype(BF)

                self.tiles(self.rows, cast)
                for x in self.to:
                    x.start()

                def keep(r):
                    v.gk[pl.ds(self.land + r, self.tile)] = v.gf[
                        pl.ds(self.loc + pl.multiple_of(dl * self.sl, 16) + r, self.tile)
                    ]

                self.tiles(self.sl, keep)

            def combine(self):
                for x in self.to:
                    x.recv()

                def add(r):
                    total = v.gk[pl.ds(self.land + r, self.tile)]
                    for k in range(d.nd - 1):
                        total = total + v.grecv[k, pl.ds(self.land + r, self.tile)].astype(F32)
                    v.gk[pl.ds(self.land + r, self.tile)] = total
                    v.gsend[pl.ds(pl.multiple_of(self.base + dl * self.sl, 16) + r, self.tile)] = total.astype(BF)

                self.tiles(self.sl, add)
                pl.when(is_sw)(self.zx.start)

            def finish(self):
                @pl.when(not_sw)
                def _():
                    self.zx.recv()

                    def add(r):
                        rows = pl.ds(self.land + r, self.tile)
                        v.gfo[rows] = (v.gk[rows] + v.gz[rows].astype(F32)).astype(BF)

                    self.tiles(self.sl, add)
                    self.keep.start()
                    for x in self.spread:
                        x.start()
                    self.core[0].start()

            def relay(self):
                @pl.when(not_sw)
                def _():
                    for x, y in zip(self.spread, self.core[1:]):
                        x.recv()
                        y.start()

            def done(self):
                for x in self.to:
                    x.sent()

                @pl.when(is_sw)
                def _():
                    self.zx.sent()
                    for x in self.core:
                        x.recv()

                @pl.when(not_sw)
                def _():
                    self.keep.wait()
                    for x in self.spread + self.core:
                        x.sent()

        redS, redO, redC, redG, redH = (Reduce(name) for name in "SOCGH")

        bar = pltpu.get_barrier_semaphore()
        for dev in [sib, zp, z2] + peers[1:]:
            pl.semaphore_signal(bar, inc=1, device_id={"dp": dev[0], "mp": dev[1]}, device_id_type=MESH)

        @pl.when(is_sw)
        def _():
            pl.semaphore_signal(bar, inc=1, device_id={"dp": mate[0], "mp": mate[1]}, device_id_type=MESH)

        pl.semaphore_wait(bar, 2 + d.nd + sw)

        for x in sx:
            x.start()
        for x in qkv3:
            x.start()
        turns = D // 128
        loads = [Local(ff_ref.at[pl.ds(i * 1024, 1024)], v.ffb.at[i % 2]) for i in range(turns)]
        loads[0].start()

        def first_norm():
            for h in range(PARTS):
                sx[h].wait()
                rows = pl.ds(h * HR, HR)
                v.h1f[t, rows] = norm_fwd(v.xb[rows].astype(F32), gain(0))
                ag1.send(h)

        pl.when(not_sw)(first_norm)

        pos = lax.broadcasted_iota(jnp.int32, (1, 4 * R), 1)
        dist = jnp.where(pos < 2 * R, pos, jnp.where(pos < 3 * R, pos - R, pos - 3 * R))
        onehot = jnp.where(lax.broadcasted_iota(jnp.int32, (NB, 4 * R), 0) == bucket_index(dist), 1.0, 0.0).astype(BF)
        lines = dot_nn(tab_ref[...], onehot)
        v.aux0[...] = jnp.zeros(v.aux0.shape, F32)
        v.aux0[pl.ds(0, 1)] = jnp.where(pos < dlen_ref[...], 0.0, MASK_FILL)
        v.aux0[pl.ds(1, 1)] = jnp.where(pos < elen_ref[...], 0.0, MASK_FILL)
        v.aux0[pl.ds(2, nh)] = jnp.where((pos >= R) & (pos < 2 * R), MASK_FILL, lines)
        v.aux0[pl.ds(2 + nh, nh)] = jnp.broadcast_to(lines[:, 2 * R : 2 * R + 1], (nh, 4 * R))
        saux.start()

        def turn(i):
            loads[i].wait()
            if i + 1 < turns:
                loads[i + 1].start()
            v.ffs[...] = v.ffb[i % 2].astype(F32)
            for j in range(8):
                part = v.ffs[pl.ds(j, 128, stride=8)]
                v.gsend[pl.ds((j % 2) * F + (j // 2) * 128, 128), pl.ds(i * 128, 128)] = jnp.transpose(part).astype(BF)

        for i in range(turns):
            turn(i)

        pl.when(is_sw)(first_norm)
        weights["so"].start()
        senc.start()
        for name in ("ckv", "cq", "co"):
            weights[name].start()
        for x in qkv3:
            x.forward()
        saux.wait()

        row16 = lax.broadcasted_iota(jnp.int32, (PADH, R), 0)
        ones_row = jnp.where(row16 == 0, 1.0, 0.0).astype(BF)

        def mask_rows(row, b):
            line = v.aux[pl.ds(row, 1), pl.ds(b * R, R)]
            return jnp.where(row16 == 0, jnp.broadcast_to(line, (PADH, R)), 0.0).astype(BF)

        for b in range(4):
            for h in range(nh):
                v.qa[b, h, pl.ds(hd, PADH)] = ones_row
                v.q2a[b // 2, b % 2, h, pl.ds(hd, PADH)] = ones_row
                v.ka[b, h, pl.ds(hd, PADH)] = mask_rows(0, b)
        for b in range(d.ne):
            for h in range(nh):
                v.k2a[b, h, pl.ds(hd, PADH)] = mask_rows(1, b)
        for h in range(nh):
            for i in range(2):
                line = v.aux[pl.ds(2 + h, 1), pl.ds(i * 2 * R, 2 * R)]
                v.bias[h, i] = pltpu.roll(jnp.broadcast_to(line, (R, 2 * R)), 0, 1, stride=1, stride_axis=0)[:, :R]
            v.bias[h, 2] = jnp.broadcast_to(v.aux[pl.ds(2 + nh + h, 1), pl.ds(0, R)], (R, R))

        @pl.when(is_sw)
        def _():
            ag1.near()
            ag1.far()

        for x in qkv3:
            x.wait()

        def project_self(b):
            qkv = dot_nt(W("qkv"), v.h1f[b]).astype(BF)
            for h in range(nh):
                v.qa[b, h, pl.ds(0, hd)] = qkv[h * hd : (h + 1) * hd]
                v.ka[b, h, pl.ds(0, hd)] = qkv[hc + h * hd : hc + (h + 1) * hd]
            v.vT[b] = qkv[2 * hc :]

        def project_step(k, carry):
            pl.when((k == 1) & not_sw)(ag1.near)
            pl.when((k == 2) & not_sw)(ag1.far)
            pl.when(k == 3)(ag1.last)
            pl.when(k == 2)(weights["so"].forward)
            project_self(blk_ag(k))
            return carry

        lax.fori_loop(0, 4, project_step, 0)
        senc.wait()
        agenc.send(0)

        def feat(h):
            return pl.ds(h * hd, hd)

        def attend_self(b):
            qs = [v.qa[b, h] for h in range(nh)]

            def block(j, state):
                out = []
                for h in range(nh):
                    m, total, acc = state[h]
                    s = dot_tn(v.ka[j, h], qs[h]) + v.bias[h, jnp.minimum(b - j, 2)]
                    new = jnp.maximum(m, jnp.max(s, axis=0, keepdims=True))
                    p = jnp.exp(s - new)
                    scale = jnp.exp(m - new)
                    total = total * scale + jnp.sum(p, axis=0, keepdims=True)
                    out.append((new, total, acc * scale + dot_nn(v.vT[j, feat(h)], p.astype(BF))))
                return tuple(out)

            first = (jnp.full((1, R), -1e30, F32), jnp.zeros((1, R), F32), jnp.zeros((hd, R), F32))
            state = lax.fori_loop(0, b + 1, block, (first,) * nh)
            for h in range(nh):
                m, total, acc = state[h]
                v.o1[b, feat(h)] = (acc / total).astype(BF)
                v.lse1[b, pl.ds(h, 1)] = m + jnp.log(total)

        def attend_cross(i, j):
            for h in range(nh):
                q = v.q2a[i, j, h]
                s = [dot_tn(v.k2a[e, h], q) for e in range(d.ne)]
                m = jnp.max(s[0], axis=0, keepdims=True)
                for part in s[1:]:
                    m = jnp.maximum(m, jnp.max(part, axis=0, keepdims=True))
                p = [jnp.exp(part - m) for part in s]
                total = sum(jnp.sum(part, axis=0, keepdims=True) for part in p)
                acc = sum(dot_nn(v.v2T[e, feat(h)], part.astype(BF)) for e, part in enumerate(p))
                v.o2[i, j, feat(h)] = (acc / total).astype(BF)
                v.lse2[i, j, pl.ds(h, 1)] = m + jnp.log(total)

        def tile_back(h, q, k, vals, da, inner, logsum, bias):
            s = dot_tn(k, q)
            if bias is not None:
                s = s + bias
            p = jnp.exp(s - logsum)
            ds = p * (dot_tn(vals, da) - inner)
            return p.astype(BF), ds, ds.astype(BF)

        def head_back(h, q, out, lse):
            da = v.da[feat(h)]
            inner = jnp.sum(da.astype(F32) * out.astype(F32), axis=0, keepdims=True)
            return q, da, inner, lse

        def attend_self_back(b):
            heads = [head_back(h, v.qa[b, h], v.o1[b, feat(h)], v.lse1[b, pl.ds(h, 1)]) for h in range(nh)]

            def block(j, dqs):
                kind = jnp.minimum(b - j, 2)
                out = []
                for h in range(nh):
                    q, da, inner, logsum = heads[h]
                    k = v.ka[j, h]
                    p, ds, low = tile_back(h, q, k, v.vT[j, feat(h)], da, inner, logsum, v.bias[h, kind])
                    v.dka[j, h] += dot_nt(q, low)
                    v.dva[j, feat(h)] += dot_nt(da, p)
                    v.dsacc[h, kind] += ds
                    out.append(dqs[h] + dot_nn(k, low))
                return tuple(out)

            dqs = lax.fori_loop(0, b + 1, block, (jnp.zeros((ha, R), F32),) * nh)
            for h in range(nh):
                v.dqkvT[b, feat(h)] = dqs[h][:hd].astype(BF)

        def attend_cross_back(i, j):
            for h in range(nh):
                q, da, inner, logsum = head_back(h, v.q2a[i, j, h], v.o2[i, j, feat(h)], v.lse2[i, j, pl.ds(h, 1)])
                dq = jnp.zeros((ha, R), F32)
                for e in range(d.ne):
                    k = v.k2a[e, h]
                    p, ds, low = tile_back(h, q, k, v.v2T[e, feat(h)], da, inner, logsum, None)
                    v.dka[e, h] += dot_nt(q, low)
                    v.dva[e, feat(h)] += dot_nt(da, p)
                    dq = dq + dot_nn(k, low)
                v.dq2T[i, j, feat(h)] = dq[:hd].astype(BF)

        def self_forward(k, carry):
            b = blk_rs(k)
            attend_self(b)
            pl.when(k == 0)(weights["so"].wait)
            v.pb[...] = dot_tn(v.o1[b], W("so"))
            rs1.emit(k)
            pl.when(k == 1)(scot.start)
            pl.when(k == 1)(agenc.near)
            pl.when(k == 1)(agenc.far)
            for name in ("ckv", "cq", "co"):
                pl.when(k == 2)(weights[name].forward)
            return carry

        lax.fori_loop(0, 4, self_forward, 0)
        agenc.last()
        weights["ckv"].wait()
        per = R // E
        for b in range(4):
            lanes = pl.ds((b % per) * E, E)
            kv = dot_nt(W("ckv"), v.encf[b]).astype(BF)
            for h in range(nh):
                v.k2a[b // per, h, pl.ds(0, hd), lanes] = kv[h * hd : (h + 1) * hd]
            v.v2T[b // per, :, lanes] = kv[hc:]

        def fin1(h, rows, total):
            x1 = v.xb[rows].astype(F32) + total
            v.x1[rows] = x1
            v.h2f[h, a, pl.ds(pl.multiple_of(c * HR, HR), HR)] = norm_fwd(x1, gain(1))
            ag2.send(h)

        for h in range(2):
            rs1.finish(h, fin1)
        weights["gu"].start()

        weights["cq"].wait()
        weights["co"].wait()

        def cross_block(i, j):
            q = dot_nt(W("cq"), v.h2f[i, j]).astype(BF)
            for h in range(nh):
                v.q2a[i, j, h, pl.ds(0, hd)] = q[h * hd : (h + 1) * hd]
            attend_cross(i, j)

        def send_cot(h):
            pl.when(h == 0)(scot.wait)
            pl.when(h == 0)(weights["fo"].start)
            rows = pl.ds(pl.multiple_of(h * HR, HR), HR)
            v.d3f[h, a, pl.ds(pl.multiple_of(c * HR, HR), HR)] = v.cotb[rows]
            agd3.send(h)

        rs1.sent()
        halves(ag2, cross_block, rs2, lambda i, j: dot_tn(v.o2[i, j], W("co")), send_cot)
        for name in ("gu", "fo"):
            weights[name].forward()

        def fin2(h, rows, total):
            x2 = v.x1[rows] + total
            v.x2[rows] = x2
            v.h3f[h, a, pl.ds(pl.multiple_of(c * HR, HR), HR)] = norm_fwd(x2, gain(2))
            ag3.send(h)

        for h in range(2):
            rs2.finish(h, fin2)
        for h in range(2):
            agd3.near(h)
            agd3.pass_on(h)
        for h in range(2):
            agd3.last(h)
        for name in ("gu", "fo"):
            weights[name].wait()

        fc = 64

        def hidden_block(i, j):
            rows = v.h3f[i, j]
            v.gus[pl.ds(0, F)] = dot_nt(W("gu", 0, F), rows)
            v.gus[pl.ds(F, F)] = dot_nt(W("gu", F, F), rows)
            v.gus[pl.ds(2 * F, F)] = dot_nt(W("fo"), v.d3f[i, j])

            def chunk(n, carry):
                r = pl.multiple_of(n * fc, fc)
                gate, up, dact = (v.gus[pl.ds(m * F + r, fc)] for m in range(3))
                sq = gate * gate
                th = jnp.tanh(gate * (GELU_C + (GELU_C * 0.044715) * sq))
                half = 0.5 + 0.5 * th
                gelu = gate * half
                slope = half + gate * (0.5 - 0.5 * th * th) * (GELU_C + (3.0 * GELU_C * 0.044715) * sq)
                v.actT[i, j, pl.ds(r, fc)] = (gelu * up).astype(BF)
                v.dguT[i, j, pl.ds(r, fc)] = (dact * up * slope).astype(BF)
                v.dguT[i, j, pl.ds(F + r, fc)] = (dact * gelu).astype(BF)
                return carry

            lax.fori_loop(0, F // fc, chunk, 0)

        rs2.sent()
        halves(ag3, hidden_block, rs3, lambda i, j: dot_tn(v.dguT[i, j], W("gu")))

        def grads(at, lhs, rows, rhs, tile):
            spots = [(b,) for b in range(4)] if len(lhs.shape) == 3 else [(b // 2, b % 2) for b in range(4)]

            def step(i, carry):
                r = pl.multiple_of(i * tile, 64)
                total = None
                for spot in spots:
                    part = dot_nn(lhs[spot + (pl.ds(r, tile),)], rhs[spot])
                    total = part if total is None else total + part
                v.gf[pl.ds(at + r, tile)] = total
                return carry

            lax.fori_loop(0, rows // tile, step, 0)

        def loc(name, group):
            base, _, at, _ = d.groups[group]
            return d.w[name][0] - base + at

        def add_gain(i, h, part):
            if h == 0:
                v.smc[pl.ds(i, 1)] = part
            else:
                v.smc[pl.ds(i, 1)] += part

        v.smc[...] = jnp.zeros(v.smc.shape, F32)

        def fin3(h, rows, total):
            grad, part = norm_bwd(v.x2[rows], gain(2), total)
            add_gain(2, h, part)
            g2 = v.cotb[rows].astype(F32) + grad
            v.gb[rows] = g2
            v.d2f[h, a, pl.ds(pl.multiple_of(c * HR, HR), HR)] = g2.astype(BF)
            agd2.send(h)

        rs3.finish(0, fin3)
        grads(loc("gu", "G"), v.dguT, 2 * F, v.h3f, 256)
        pl.when(is_sw)(weights["gu"].far.sent)
        redG.send()

        def hidden_out(h, carry):
            rso.emit_pair(h, lambda i, j: dot_tn(v.actT[i, j], W("fo")), kick=False)
            return carry

        lax.fori_loop(0, 2, hidden_out, 0)
        rs3.finish(1, fin3)
        grads(loc("fo", "H"), v.actT, F, v.d3f, 256)
        redH.send()
        rso.kick()

        v.dka[...] = jnp.zeros(v.dka.shape, F32)
        v.dva[...] = jnp.zeros(v.dva.shape, F32)

        def cross_back_block(i, j):
            v.da[...] = dot_nt(W("co"), v.d2f[i, j]).astype(BF)
            attend_cross_back(i, j)

        rs3.sent()
        halves(agd2, cross_back_block, rs4, lambda i, j: dot_tn(v.dq2T[i, j], W("cq")))

        def fin4(h, rows, total):
            grad, part = norm_bwd(v.x1[rows], gain(1), total)
            add_gain(1, h, part)
            g1 = v.gb[rows] + grad
            v.gb[rows] = g1
            v.d1f[t, rows] = g1.astype(BF)
            agd1.send(h)

        for b in range(4):
            lanes = pl.ds((b % per) * E, E)
            for h in range(nh):
                v.dkv2T[b, pl.ds(h * hd, hd)] = v.dka[b // per, h, pl.ds(0, hd), lanes].astype(BF)
            v.dkv2T[b, pl.ds(hc, hc)] = v.dva[b // per, :, lanes].astype(BF)

        def enc_part(b):
            v.epb[...] = dot_tn(v.dkv2T[b], W("ckv"))

        rse.loop(enc_part, kick=False)
        grads(loc("cq", "C"), v.dq2T, hc, v.h2f, hc)
        grads(loc("co", "C"), v.o2, hc, v.d2f, hc)
        grads(loc("ckv", "C"), v.dkv2T, 2 * hc, v.encf, hc)
        redC.send()
        rs4.finish(0, fin4)

        def fin_out(h, rows, total):
            v.lov[rows] = (v.x2[rows] + total).astype(BF)

        for h in range(2):
            rso.finish(h, fin_out)
        rs4.finish(1, fin4)


        v.dka[...] = jnp.zeros(v.dka.shape, F32)
        v.dva[...] = jnp.zeros(v.dva.shape, F32)
        v.dsacc[...] = jnp.zeros(v.dsacc.shape, F32)

        def self_back(k, carry):
            b = blk_ag(k)
            agd1.arrive(k)
            pl.when(k == 1)(redG.combine)
            pl.when(k == 3)(rse.kick)
            pl.when(k == 2)(out_lo.start)
            pl.when(k == 3)(redH.combine)

            @pl.when(k == 3)
            def _():
                grads(loc("so", "O"), v.o1, hc, v.d1f, hc)
                redO.send()

            v.da[...] = dot_nt(W("so"), v.d1f[b]).astype(BF)
            attend_self_back(b)
            return carry

        lax.fori_loop(0, 4, self_back, 0)

        for b in range(4):
            for h in range(nh):
                v.dqkvT[b, pl.ds(hc + h * hd, hd)] = v.dka[b, h, pl.ds(0, hd)].astype(BF)
            v.dqkvT[b, pl.ds(2 * hc, hc)] = v.dva[b].astype(BF)
        grads(loc("qkv", "S"), v.dqkvT, 3 * hc, v.h1f, hc)
        redS.send()

        def self_qkv_part(b):
            v.pb[...] = dot_tn(v.dqkvT[b], W("qkv"))

        rs4.sent()
        rs5.loop(self_qkv_part)
        redC.combine()
        redO.combine()
        redG.finish()
        redH.finish()

        def fin_enc(h, rows, total):
            v.egv[rows] = total.astype(BF)


        iota0 = lax.broadcasted_iota(jnp.int32, (R, R), 0)
        iota1 = lax.broadcasted_iota(jnp.int32, (R, R), 1)
        flip = (iota0 + iota1 == R - 1).astype(F32)

        def diagonals(h, i):
            turned = lax.dot_general(
                flip, v.dsacc[h, i], (((1,), (0,)), ((), ())), precision=lax.Precision.HIGHEST, preferred_element_type=F32
            )
            wide = jnp.concatenate([turned, jnp.zeros((R, R), F32)], axis=1)
            return jnp.sum(pltpu.roll(wide, 0, 1, stride=1, stride_axis=0), axis=0, keepdims=True)

        lane = lax.broadcasted_iota(jnp.int32, (1, 2 * R), 1)
        for h in range(nh):
            near, off = diagonals(h, 0), diagonals(h, 1)
            far = jnp.sum(jnp.sum(v.dsacc[h, 2], axis=0, keepdims=True), axis=1, keepdims=True)
            off = off + jnp.where(lane == 2 * R - 1, far, 0.0)
            line = jnp.concatenate([pltpu.roll(near, R + 1, 1)[:, :R], off], axis=1)
            v.smc[pl.ds(3 + h, 1), pl.ds(0, 3 * R)] = line

        def fin5(h, rows, total):
            grad, part = norm_bwd(v.xb[rows].astype(F32), gain(0), total)
            add_gain(0, h, part)
            v.igv[rows] = (v.gb[rows] + grad).astype(BF)

        plane = peers[1:]
        first = [Xfer(v.sms.at[0], v.smr.at[i], dev) for i, dev in enumerate(plane)]
        rest = [Xfer(v.sms.at[1 + i], v.smr.at[3 + i], dev) for i, dev in enumerate([z2, zp, sib])]
        redS.combine()
        for h in range(2):
            rs5.finish(h, fin5)
        v.sms[0] = v.smc[...]
        for x in first:
            x.start()
        for x in out_ig:
            x.start()
        redS.finish()
        for x in first:
            x.recv()
        if len(plane) == 3:
            v.sms[1] = (v.sms[0] + v.smr[0]) + (v.smr[1] + v.smr[2])
        elif len(plane) == 1:
            v.sms[1] = v.sms[0] + v.smr[0]
        else:
            v.sms[1] = v.sms[0]
        rest[0].start()
        redC.finish()
        redO.finish()
        rest[0].recv()
        v.sms[2] = v.sms[1] + v.smr[3]
        v.smc[...] = v.sms[2]
        rest[1].start()
        rse.finish(0, fin_enc)
        out_eg.start()
        redG.relay()
        redH.relay()
        rest[1].recv()
        only = lax.broadcasted_iota(jnp.int32, v.smc.shape, 0) < 3
        v.sms[3] = jnp.where(only, v.sms[2] + v.smr[4], v.sms[2])
        rest[2].start()
        redC.relay()
        redO.relay()
        redS.relay()
        rest[2].recv()
        total = v.sms[3] + v.smr[5]
        table_rows = jnp.where(is_sw, v.smr[5], v.smc[...])
        sm_ref[...] = jnp.where(only, total, table_rows)

        for x in first + rest:
            x.sent()
        for x in (ag1, ag2, ag3, agd1, agd2, agd3, agenc, rs5, rso, rse):
            x.sent()
        for x in [saux, scot, senc] + sx:
            x.sent()
        for name, x in weights.items():
            x.sent(name != "gu")
        for x in qkv3:
            x.sent()
        for x in [out_lo, out_eg] + out_ig:
            x.wait()
            x.sent()
        for r in (redG, redH, redC, redO, redS):
            r.done()

    return kernel


def unpack(d, gw, lo, ig, eg, sm):
    R, D, F, hc, nh, E = d.R, d.D, d.F, d.hc, d.nh, d.E
    steps = 3
    cols = D // steps

    def kernel(gu_ref, fo_ref, qkv_ref, so_ref, ckv_ref, cq_ref, co_ref, lo_ref, ig_ref, eg_ref, sm_ref, *outs):
        lo_out, ig_out, eg_out, gu_out, fo_out, qkv_out, so_out, ckv_out, cq_out, co_out, gains_out, table_out = outs
        for j in range(2 * F // 128):
            part = jnp.transpose(gu_ref[pl.ds((j % 2) * F + (j // 2) * 128, 128)].astype(F32))
            gu_out[pl.ds(j, cols, stride=2 * F // 128)] = part
        for src, dst in (
            (fo_ref, fo_out), (qkv_ref, qkv_out), (so_ref, so_out), (ckv_ref, ckv_out), (cq_ref, cq_out), (co_ref, co_out)
        ):
            dst[...] = src[...].astype(F32)

        @pl.when(pl.program_id(0) == 0)
        def _():
            lo_out[...] = lo_ref[...]
            ig_out[...] = ig_ref[...].astype(F32)
            eg_out[...] = eg_ref[...].astype(F32)
            gains_out[...] = sm_ref[pl.ds(0, 3)]
            col = lax.broadcasted_iota(jnp.int32, (1, D), 1)
            dist = jnp.where(col < R, col, jnp.where(col < 3 * R - 1, col - R + 1, 4 * R))
            pick = (lax.broadcasted_iota(jnp.int32, (NB, D), 0) == bucket_index(dist)).astype(F32)
            mine = sm_ref[pl.ds(3, nh)]
            table_out[...] = lax.dot_general(
                mine, pick, (((1,), (1,)), ((), ())), precision=lax.Precision.HIGHEST, preferred_element_type=F32
            )

    at = lambda name: d.w[name][0]
    rows = lambda name, n: pl.BlockSpec((n, D), lambda i: (at(name) // n + i, 0))
    out_rows = lambda n: pl.BlockSpec((n, D), lambda i: (i, 0))
    whole = lambda *shape: pl.BlockSpec(shape, lambda i: (0,) * len(shape))
    third = {name: d.w[name][1] // steps for name in ("qkv", "so", "ckv", "cq", "co")}
    half = F // 2
    assert all(at(name) % n == 0 for name, n in third.items()) and at("fo") % half == 0 and at("gu") == 0
    shape = lambda *dims: jax.ShapeDtypeStruct(dims, F32)
    return pl.pallas_call(
        kernel,
        grid=(steps,),
        in_specs=[
            pl.BlockSpec((2 * F, cols), lambda i: (0, i)),
            pl.BlockSpec((half, D), lambda i: (at("fo") // half + jnp.minimum(i, 1), 0)),
        ]
        + [rows(name, n) for name, n in third.items()]
        + [whole(R, D), whole(R, D), whole(E, D), whole(d.small, D)],
        out_specs=[
            whole(R, D), whole(R, D), whole(E, D),
            pl.BlockSpec((cols * 2 * F // 128, 128), lambda i: (i, 0)),
            pl.BlockSpec((half, D), lambda i: (jnp.minimum(i, 1), 0)),
        ]
        + [out_rows(n) for n in third.values()]
        + [whole(3, D), whole(nh, NB)],
        out_shape=[
            jax.ShapeDtypeStruct((R, D), BF), shape(R, D), shape(E, D), shape(D * 2 * F // 128, 128), shape(F, D),
            shape(3 * hc, D), shape(hc, D), shape(2 * hc, D), shape(hc, D), shape(hc, D), shape(3, D), shape(nh, NB),
        ],
        compiler_params=pltpu.CompilerParams(vmem_limit_bytes=63 << 20),
    )(*[gw] * 7, lo, ig, eg, sm)


def local_fn(mesh):
    def local(x_in, enc_in, cotangent, dec_len, enc_len, self_qkv, self_out, cross_q, cross_kv, cross_out, ff_in, ff_out, gains, table):
        d = make_dims(mesh, x_in, enc_in, self_qkv, ff_in, table)
        R, D, hc, nh, F = d.R, d.D, d.hc, d.nh, d.F
        hbm = pl.BlockSpec(memory_space=pl.ANY)
        vmem = pl.BlockSpec(memory_space=pltpu.VMEM)
        ws = {
            "qkv": jnp.transpose(self_qkv, (1, 2, 0)).reshape(3 * hc, D),
            "so": self_out,
            "cq": jnp.transpose(cross_q),
            "ckv": jnp.transpose(cross_kv, (1, 2, 0)).reshape(2 * hc, D),
            "co": cross_out,
            "gu": jnp.transpose(ff_in.reshape(D, 2, F // 128, 128), (0, 2, 1, 3)).reshape(D * 2 * F // 128, 128),
            "fo": ff_out,
        }
        outs = pl.pallas_call(
            build_kernel(d),
            out_shape=(
                jax.ShapeDtypeStruct((R, D), BF),
                jax.ShapeDtypeStruct((R, D), BF),
                jax.ShapeDtypeStruct((d.E, D), BF),
                jax.ShapeDtypeStruct((d.rows, D), BF),
                jax.ShapeDtypeStruct((d.small, D), F32),
            ),
            in_specs=[hbm, hbm, hbm, vmem, vmem, vmem, vmem] + [hbm] * len(d.w),
            out_specs=(hbm, hbm, hbm, hbm, vmem),
            scratch_shapes=[pltpu.VMEM(shape, dtype) for _, shape, dtype in scratch_list(d)]
            + [pltpu.SemaphoreType.DMA((SEMS,))] * 3,
            compiler_params=pltpu.CompilerParams(collective_id=0, has_side_effects=True, vmem_limit_bytes=63 << 20),
        )(x_in, enc_in, cotangent, jnp.transpose(table), dec_len.reshape(1, 1), enc_len.reshape(1, 1), gains, *[ws[name] for name in d.w])
        lo, ig, eg, gw, sm = outs
        others = d.ndp // (2 * d.nd)
        if others > 1:
            gw, sm = lax.psum((gw.astype(F32), sm), "dp")
            gw, sm = gw * (1.0 / (2 * d.nd)), sm * (1.0 / (2 * d.nd))
        res = unpack(d, gw, lo, ig, eg, sm)
        gu = jnp.transpose(res[3].reshape(D, F // 128, 2, 128), (0, 2, 1, 3)).reshape(D, 2, F)
        return (
            res[0],
            res[1],
            res[2],
            jnp.transpose(res[5].reshape(3, hc, D), (2, 0, 1)),
            res[6],
            jnp.transpose(res[8]),
            jnp.transpose(res[7].reshape(2, hc, D), (2, 0, 1)),
            res[9],
            gu,
            res[4],
            res[10],
            jnp.transpose(res[11]),
        )

    return local


def solution(mesh):
    rows = P(("dp", "mp"), None)
    in_specs = (
        rows, rows, rows, P("dp"), P("dp"), P(None, None, "mp"), P("mp", None), P(None, "mp"), P(None, None, "mp"),
        P("mp", None), P(None, None, "mp"), P("mp", None), P(), P(None, "mp"),
    )
    out_specs = (
        rows, rows, rows, P(None, None, "mp"), P("mp", None), P(None, "mp"), P(None, None, "mp"), P("mp", None),
        P(None, None, "mp"), P("mp", None), P(), P(None, "mp"),
    )
    return jax.shard_map(local_fn(mesh), mesh=mesh, in_specs=in_specs, out_specs=out_specs, check_vma=False)
```
